32 devices in a mesh: seq: 8 (over z, y), head: 4 (over x, core).
Axes of the slice: x: 2, y: 2, z: 4, core: 2. Of those that a mesh axis runs over, the one named last changes fastest.
Arguments:
- mixer_input: bfloat16 [12288, 16, 512], P('seq', 'head'), may hold values from -6 to 6
- filter_coefficients: float32 [4, 16, 512], P(None, 'head'), may hold values from -3 to 3
- step_size: float32 [12288, 16, 8], P('seq', 'head'), may hold values from 0 to 1
- decay_log: float32 [16, 8], P('head'), may hold values from -4 to 6
- state_input_weight: bfloat16 [12288, 1024], P('seq'), may hold values from -6 to 6
- state_read: bfloat16 [12288, 1024], P('seq'), may hold values from -6 to 6
- skip_gain: float32 [16, 8], P('head'), may hold values from 0.5 to 1.5
- output_gradient: bfloat16 [12288, 16, 512], P('seq', 'head'), may hold values from -6 to 6
Outputs:
- mixed: bfloat16 [12288, 16, 512], P('seq', 'head')
- input_grad: bfloat16 [12288, 16, 512], P('seq', 'head')
- conv_grad: float32 [4, 16, 512], P(None, 'head')
- decay_grad: float32 [16, 8], P('head')
- write_grad: bfloat16 [12288, 1024], P('seq')
- read_grad: bfloat16 [12288, 1024], P('seq')
The draws below stay inside these ranges and needn't reach their ends.
All inputs are finite; a program needn't handle non-finite values.
Results may differ from the reference program's by a relative error of at most 0.015.
Values may be sent and summed in bfloat16 or wider, within the bound.
No kernel may reach another device: no remote copies, remote signals or barrier semaphores. Data moves between devices by JAX's collectives and lax.ppermute only.
A program may use at most 448 MiB of HBM per device.

```python
import math
import jax
import jax.numpy as jnp
from jax import lax

HDIM = 64
NSTATE = 128
GROUPS = 8
KCONV = 4
SPAN = 128
TOK_DEV = 1536
HPG = 16
SEQ_LEN = 12288
N_HEAD = 4


def head_rates(key):
    first, second, third, fourth = jax.random.split(jax.random.fold_in(key, 7), 4)
    share = 0.25
    quick_mask = jax.random.uniform(second, (HPG, GROUPS), jnp.float32, 0.0, 1.0) < share
    quick_rate = jnp.exp(jax.random.uniform(third, (HPG, GROUPS), jnp.float32, math.log(0.02), math.log(0.05)))
    slow_rate = jnp.exp(jax.random.uniform(first, (HPG, GROUPS), jnp.float32, math.log(0.2), math.log(1.2))) / SEQ_LEN
    per_token = jnp.where(quick_mask, quick_rate, slow_rate)
    level = jnp.exp(jax.random.uniform(fourth, (HPG, GROUPS), jnp.float32, math.log(0.00015), math.log(0.00035)))
    return (per_token, level, quick_mask)


def draw_decay_log(key, part):
    per_token, level, quick_mask = head_rates(key)
    return jnp.log(per_token) - jnp.log(level)


def draw_step_size(key, part):
    per_token, level, quick_mask = head_rates(key)
    first, second, third, fourth = jax.random.split(jax.random.fold_in(key, 11), 4)
    half_rows = max(TOK_DEV // 2, 1)
    block_count = SEQ_LEN // half_rows
    factor = jnp.exp(jax.random.uniform(first, (block_count,), jnp.float32, -0.7, 0.7))
    rough = jnp.exp(jax.random.uniform(second, (SEQ_LEN, HPG, GROUPS), jnp.float32, -0.5, 0.5))
    places = jnp.arange(SEQ_LEN, dtype=jnp.int32)
    drawn_step = level[None] * rough * factor[places // half_rows][:, None, None]
    storm_block = jax.random.randint(third, (HPG, GROUPS), 0, SEQ_LEN // SPAN)
    storm_strength = jax.random.uniform(fourth, (SEQ_LEN, HPG, GROUPS), jnp.float32, 1.6, 3.0)
    in_storm = jnp.logical_and((places // SPAN)[:, None, None] == storm_block[None], quick_mask[None])
    return jnp.where(in_storm, storm_strength * (level / per_token)[None], drawn_step)


def levels(key, shape, cuts, least, high):
    factor_of, own = 1.0, jax.random.fold_in(key, 6)
    for axis_at, shards_of in cuts:
        draws = jnp.exp(jax.random.uniform(jax.random.fold_in(own, axis_at), (shards_of,), jnp.float32, least / len(cuts), high / len(cuts)))
        factor_of = factor_of * jnp.repeat(draws, shape[axis_at] // shards_of).reshape([-1 if axis == axis_at else 1 for axis in range(len(shape))])
    return factor_of


def centred(stream_key, shape, scale, reach, cuts=(), kind=jnp.bfloat16):
    values = jax.random.normal(stream_key, shape, jnp.float32) * scale
    if len(cuts) > 0:
        values = levels(stream_key, shape, cuts, -0.22, 0.18) * values
    return jnp.clip(values, min=-reach, max=reach).astype(kind)


def setup_inputs(seed: int = 0) -> dict:
    streams_of = jax.random.split(jax.random.key(seed), 9)
    mixer_input = centred(streams_of[0], (SEQ_LEN, HPG, GROUPS * HDIM), 1.0, 6.0, ((0, 8), (1, 4)))
    filter_coefficients = centred(streams_of[1], (KCONV, HPG, GROUPS * HDIM), KCONV ** -0.5, 3.0, ((1, 4),), jnp.float32)
    step_size = draw_step_size(jax.random.fold_in(streams_of[8], 71), 0)
    decay_log = draw_decay_log(jax.random.fold_in(streams_of[8], 71), 0)
    state_input_weight = centred(streams_of[4], (SEQ_LEN, GROUPS * NSTATE), 1.0, 6.0, ((0, 8),))
    state_read = centred(streams_of[5], (SEQ_LEN, GROUPS * NSTATE), 1.0, 6.0, ((0, 8),))
    skip_gain = jnp.clip(0.5 + 1.0 * jax.random.uniform(streams_of[6], (HPG, GROUPS), jnp.float32) ** levels(streams_of[6], (HPG, GROUPS), ((0, 4),), -0.2, 0.2), 0.5, 1.5)
    output_gradient = centred(streams_of[7], (SEQ_LEN, HPG, GROUPS * HDIM), 1.0, 6.0, ((0, 8), (1, 4)))
    return dict(mixer_input=mixer_input, filter_coefficients=filter_coefficients, step_size=step_size, decay_log=decay_log, state_input_weight=state_input_weight, state_read=state_read, skip_gain=skip_gain, output_gradient=output_gradient)


PRECISE = lax.Precision.HIGH

def conv_silu(padded, weight):
    tap_count = weight.shape[0]
    count_rows = padded.shape[0] - tap_count + 1
    summed = weight[0] * padded[0:count_rows]
    for offset in range(1, tap_count):
        summed = summed + weight[offset] * padded[offset:offset + count_rows]
    return jax.nn.silu(summed)

def span_step(carry_state, inputs):
    u_block, logd_block, dt_block, write_block, read_block = inputs
    cumul = jnp.cumsum(logd_block, axis=0)
    length = cumul.shape[0]
    scores = jnp.einsum('tgn,sgn->tsg', read_block, write_block, precision=PRECISE)
    lower = (lax.broadcasted_iota(jnp.int32, (length, length), 0) >= lax.broadcasted_iota(jnp.int32, (length, length), 1))[:, :, None, None]
    spread = cumul[:, None] - cumul[None, :]
    decay = jnp.where(lower, jnp.exp(jnp.where(lower, spread, 0.0)), 0.0)
    mixing = scores[:, :, None, :] * decay * dt_block[None]
    inner = jnp.einsum('tsjg,sjgp->tjgp', mixing, u_block, precision=PRECISE)
    carried = jnp.einsum('tgn,jgpn->tjgp', read_block, carry_state, precision=PRECISE) * jnp.exp(cumul)[..., None]
    tail_weight = jnp.exp(cumul[-1][None] - cumul) * dt_block
    new_state = jnp.exp(cumul[-1])[..., None, None] * carry_state + jnp.einsum('sgn,sjgp->jgpn', write_block, u_block * tail_weight[..., None], precision=PRECISE)
    return (new_state, inner + carried)

def local_scan(hidden_u, logd, dt_all, write_all, read_all, span_rows):
    count_rows, heads_j, groups, hdim_local = hidden_u.shape
    nstate_local = write_all.shape[-1]
    number = count_rows // span_rows

    def split_rows(array):
        return array.reshape((number, span_rows) + array.shape[1:])
    initial = jnp.zeros((heads_j, groups, hdim_local, nstate_local), jnp.float32)
    ending, outputs = lax.scan(jax.checkpoint(span_step), initial, (split_rows(hidden_u), split_rows(logd), split_rows(dt_all), split_rows(write_all), split_rows(read_all)))
    return (outputs.reshape(hidden_u.shape), ending)

def reference(mixer_input, filter_coefficients, step_size, decay_log, state_input_weight, state_read, skip_gain, output_gradient):
    seq_rows = mixer_input.shape[0]
    heads_j = HPG // N_HEAD
    write_all = state_input_weight.astype(jnp.float32).reshape(seq_rows, GROUPS, NSTATE)
    read_all = state_read.astype(jnp.float32).reshape(seq_rows, GROUPS, NSTATE)

    def block_fn(totals, index):
        begin = index * heads_j

        def take(array, dim):
            return lax.dynamic_slice_in_dim(array, begin, heads_j, dim)
        x_block = take(mixer_input, 1).astype(jnp.float32)
        w_block = take(filter_coefficients, 1)
        dt_block = take(step_size, 1)
        log_block = take(decay_log, 0)
        gain_block = take(skip_gain, 0)
        adjoint_tile = take(output_gradient, 1).astype(jnp.float32).reshape(seq_rows, heads_j, GROUPS, HDIM)

        def forward(x_part, w_part, log_part, write_part, read_part):
            padded = jnp.concatenate([jnp.zeros((KCONV - 1,) + x_part.shape[1:], jnp.float32), x_part], axis=0)
            hidden_u = conv_silu(padded, w_part).reshape(seq_rows, heads_j, GROUPS, HDIM)
            logd = dt_block * -jnp.exp(log_part)
            outputs, ending = local_scan(hidden_u, logd, dt_block, write_part, read_part, SPAN)
            return outputs + gain_block[None, :, :, None] * hidden_u
        result, back_fn = jax.vjp(forward, x_block, w_block, log_block, write_all, read_all)
        grad_x, grad_w, grad_log, grad_write, grad_read = back_fn(adjoint_tile)
        part_write = lax.optimization_barrier(grad_write.astype(jnp.bfloat16)).astype(jnp.float32)
        part_read = lax.optimization_barrier(grad_read.astype(jnp.bfloat16)).astype(jnp.float32)
        outputs = (result.reshape(seq_rows, heads_j, GROUPS * HDIM).astype(jnp.bfloat16), grad_x.astype(jnp.bfloat16), grad_w, grad_log)
        return ((totals[0] + part_write, totals[1] + part_read), outputs)
    zero_sum = jnp.zeros((seq_rows, GROUPS, NSTATE), jnp.float32)
    totals, stacked = lax.scan(block_fn, (zero_sum, zero_sum), jnp.arange(N_HEAD, dtype=jnp.int32))
    mixed = jnp.moveaxis(stacked[0], 0, 1).reshape(seq_rows, HPG, GROUPS * HDIM)
    input_grad = jnp.moveaxis(stacked[1], 0, 1).reshape(seq_rows, HPG, GROUPS * HDIM)
    conv_grad = jnp.moveaxis(stacked[2], 0, 1).reshape(KCONV, HPG, GROUPS * HDIM)
    decay_grad = stacked[3].reshape(HPG, GROUPS)
    write_grad = totals[0].reshape(seq_rows, GROUPS * NSTATE).astype(jnp.bfloat16)
    read_grad = totals[1].reshape(seq_rows, GROUPS * NSTATE).astype(jnp.bfloat16)
    return (mixed, input_grad, conv_grad, decay_grad, write_grad, read_grad)
```

```python
import functools

import jax
import jax.numpy as jnp
from jax import lax
from jax.experimental import pallas as pl
from jax.experimental.pallas import tpu as pltpu
from jax.sharding import PartitionSpec as P

SPAN = 128
LANES = 128
HALF = 64
EDGE = 8
F32 = jnp.float32
BF16 = jnp.bfloat16
NT = (((1,), (1,)), ((), ()))
TN = (((0,), (0,)), ((), ()))


def dot(a, b, dims=None):
    if dims is None:
        return jnp.dot(a, b, preferred_element_type=F32)
    return lax.dot_general(a, b, dims, preferred_element_type=F32)


def halves(cols, base, j, low):
    first = cols[:, base + 2 * j : base + 2 * j + 1]
    second = cols[:, base + 2 * j + 1 : base + 2 * j + 2]
    return jnp.where(low, first, second)


def low_half(rows):
    return lax.broadcasted_iota(jnp.int32, (rows, LANES), 1) < HALF


def states_kernel(
    lane0, x_ref, halo_ref, w_ref, b_ref, colf_ref, y_ref, c_ref, colr_ref,
    v_ref, s_ref, r_ref, total_ref, x_buf, s_acc, r_acc, d_acc,
):
    step = pl.program_id(0)
    span, heads_j, _ = x_ref.shape
    heads = 2 * heads_j
    low = low_half(span)
    low1 = low_half(1)

    @pl.when(step == 0)
    def _():
        s_acc[...] = jnp.zeros_like(s_acc)
        r_acc[...] = jnp.zeros_like(r_acc)
        d_acc[...] = jnp.ones_like(d_acc)
        halo = halo_ref[...].astype(F32)
        for j in range(heads_j):
            for row in range(3):
                x_buf[j, EDGE - 3 + row : EDGE - 2 + row, :] = halo[row, j : j + 1, :]

    @pl.when(step > 0)
    def _():
        x_buf[:, 0:EDGE, :] = x_buf[:, span : span + EDGE, :]

    x_buf[:, EDGE : EDGE + span, :] = jnp.swapaxes(x_ref[...], 0, 1).astype(F32)
    colf = colf_ref[...][:, lane0 : lane0 + 4 * heads]
    colr = colr_ref[...][:, lane0 : lane0 + 4 * heads]
    weights = w_ref[...]
    b_all = b_ref[...]
    c_all = c_ref[...]
    grads = jnp.swapaxes(y_ref[...], 0, 1)
    s_ref[0] = s_acc[...].astype(BF16)
    r_ref[0] = r_acc[...].astype(BF16)
    for j in range(heads_j):
        v = weights[0, j : j + 1, :] * x_buf[j, EDGE - 3 : EDGE - 3 + span, :]
        for tap in range(1, 4):
            v = v + weights[tap, j : j + 1, :] * x_buf[j, EDGE - 3 + tap : EDGE - 3 + tap + span, :]
        v_ref[j] = v.astype(BF16)
        u = v / (1.0 + jnp.exp(-v))
        tail = halves(colf, heads, j, low) * halves(colf, 3 * heads, j, low)
        own = dot(b_all, (u * tail).astype(BF16), TN)
        keep = halves(colf[span - 1 : span], 2 * heads, j, low1)
        s_acc[j] = keep * s_acc[j] + jnp.where(low, own[:LANES], own[LANES:])
        d_acc[j : j + 1, :] = d_acc[j : j + 1, :] * keep
        lead = halves(colr, 2 * heads, j, low)
        own = dot(c_all, (grads[j].astype(F32) * lead).astype(BF16), TN)
        keep = halves(colr[span - 1 : span], 2 * heads, j, low1)
        r_acc[j] = keep * r_acc[j] + jnp.where(low, own[:LANES], own[LANES:])

    @pl.when(step == pl.num_programs(0) - 1)
    def _():
        total_ref[0, :, :LANES, :] = s_acc[...].astype(BF16)
        total_ref[1, :, :LANES, :] = r_acc[...].astype(BF16)
        for j in range(heads_j):
            decay = d_acc[j : j + 1, :]
            high = decay.astype(BF16).astype(F32)
            pair = jnp.concatenate([high, decay - high, jnp.zeros((6, LANES), F32)], axis=0)
            total_ref[0, j, LANES:, :] = pair.astype(BF16)
            total_ref[1, j, LANES:, :] = pair.astype(BF16)


def main_kernel(
    lane0, x_ref, v_ref, y_ref, b_ref, c_ref, col_ref, row_ref, s_ref, r_ref,
    enter_ref, leave_ref, from_ref, to_ref, w_ref, skip_ref, *rest,
):
    mixed_ref, dx_ref, db_ref, dc_ref, cg_ref, ag_ref, lg_ref, edge_ref, dv_buf = rest[-9:]
    step = pl.program_id(0)
    span, heads_j, _ = x_ref.shape
    heads = 2 * heads_j
    low = low_half(span)
    low1 = low_half(1)
    causal = lax.broadcasted_iota(jnp.int32, (span, span), 0) >= lax.broadcasted_iota(
        jnp.int32, (span, span), 1
    )

    @pl.when(step == 0)
    def _():
        cg_ref[...] = jnp.zeros_like(cg_ref)
        ag_ref[...] = jnp.zeros_like(ag_ref)
        lg_ref[...] = jnp.zeros_like(lg_ref)
        dv_buf[:, span : span + EDGE, :] = jnp.zeros((heads_j, EDGE, LANES), F32)

    @pl.when(step > 0)
    def _():
        dv_buf[:, span : span + EDGE, :] = dv_buf[:, 0:EDGE, :]

    xs = jnp.swapaxes(x_ref[...], 0, 1)
    grads = jnp.swapaxes(y_ref[...], 0, 1)
    cols = col_ref[...][:, lane0 : lane0 + 4 * heads]
    rows = row_ref[0]
    b_all = b_ref[...]
    c_all = c_ref[...]
    weights = w_ref[...]
    skips = skip_ref[...]
    scores = [dot(c_all[:, g * LANES : (g + 1) * LANES], b_all[:, g * LANES : (g + 1) * LANES], NT) for g in range(2)]
    score_grads = [jnp.zeros((span, span), F32) for _ in range(2)]
    zero = jnp.zeros((LANES, LANES), BF16)
    lowb = low_half(LANES)
    dc_inter = jnp.zeros((span, 2 * LANES), F32)
    db_inter = jnp.zeros((span, 2 * LANES), F32)
    out_rows = []
    for j in range(heads_j):
        a_b = halves(cols, 0, j, low)
        dt_b = halves(cols, heads, j, low)
        e_b = halves(cols, 2 * heads, j, low)
        f_b = halves(cols, 3 * heads, j, low)
        a_last = a_b[span - 1 : span]
        e_last = e_b[span - 1 : span]
        v = v_ref[j].astype(F32)
        gate = 1.0 / (1.0 + jnp.exp(-v))
        u = v * gate
        slope = gate + u * (1.0 - gate)
        dy16 = grads[j]
        dy = dy16.astype(F32)
        val = u * dt_b
        val16 = val.astype(BF16)
        tail16 = (val * f_b).astype(BF16)
        lead16 = (dy * e_b).astype(BF16)
        zero_rows = jnp.zeros((span, LANES), BF16)
        dy_two = jnp.concatenate([jnp.where(low, dy16, zero_rows), jnp.where(low, zero_rows, dy16)], axis=0)
        val_two = jnp.concatenate([jnp.where(low, val16, zero_rows), jnp.where(low, zero_rows, val16)], axis=0)
        products = dot(dy_two, val16, NT)
        mixes = []
        for g in range(2):
            h = 2 * j + g
            spread = cols[:, h : h + 1] - rows[h : h + 1, :]
            decay = jnp.exp(jnp.where(causal, spread, -jnp.inf))
            mixes.append((scores[g] * decay).astype(BF16))
            weighted = decay * products[g * span : (g + 1) * span]
            score_grads[g] = score_grads[g] + weighted
            term = scores[g] * weighted * jnp.where(causal, spread, 0.0)
            lg_ref[h : h + 1, :] = lg_ref[h : h + 1, :] + jnp.sum(term, axis=0, keepdims=True)
        inner = dot(jnp.concatenate(mixes, axis=1), val_two)
        dval = dot(jnp.concatenate(mixes, axis=0), dy_two, TN)
        state = s_ref[0, j].astype(F32) + from_ref[0, j : j + 1, :] * enter_ref[j]
        rstate = r_ref[0, j].astype(F32) + to_ref[0, j : j + 1, :] * leave_ref[j]
        state16 = state.astype(BF16)
        rstate16 = rstate.astype(BF16)
        state_two = jnp.concatenate([jnp.where(lowb, state16, zero), jnp.where(lowb, zero, state16)], axis=0)
        rstate_two = jnp.concatenate([jnp.where(lowb, rstate16, zero), jnp.where(lowb, zero, rstate16)], axis=0)
        carried = dot(c_all, state_two) * e_b
        back = dot(b_all, rstate_two) * f_b
        dc_inter = dc_inter + dot(lead16, state_two, NT)
        db_inter = db_inter + dot(tail16, rstate_two, NT)
        log_part = a_b * dy * carried + (a_last - a_b) * val * back
        through = jnp.sum(state * rstate, axis=0, keepdims=True) * (a_last * e_last)
        ag_ref[j : j + 1, :] = ag_ref[j : j + 1, :] + jnp.sum(log_part, axis=0, keepdims=True) + through
        skip = skips[j : j + 1, :]
        out_rows.append((inner + carried + skip * u).astype(BF16))
        du = dt_b * (dval + back) + skip * dy
        dv_buf[j, 0:span, :] = du * slope
    mixed_ref[...] = jnp.swapaxes(jnp.stack(out_rows, axis=0), 0, 1)
    dx_rows = []
    for j in range(heads_j):
        x = xs[j].astype(F32)
        total = None
        for tap in range(4):
            shifted = dv_buf[j, 3 - tap : 3 - tap + span, :]
            piece = weights[tap, j : j + 1, :] * shifted
            total = piece if total is None else total + piece
            cg_ref[tap, j : j + 1, :] = cg_ref[tap, j : j + 1, :] + jnp.sum(shifted * x, axis=0, keepdims=True)
        dx_rows.append(total.astype(BF16))
    dx_ref[...] = jnp.swapaxes(jnp.stack(dx_rows, axis=0), 0, 1)
    for g in range(2):
        inside = slice(g * LANES, (g + 1) * LANES)
        flow = score_grads[g].astype(BF16)
        dc_ref[:, inside] = (dot(flow, b_all[:, inside]) + dc_inter[:, inside]).astype(BF16)
        db_ref[:, inside] = (dot(flow, c_all[:, inside], TN) + db_inter[:, inside]).astype(BF16)

    @pl.when(step == pl.num_programs(0) - 1)
    def _():
        edge_ref[...] = dv_buf[:, 0:EDGE, :]


def unpack(sent):
    decay = sent[0, :, LANES, :].astype(F32) + sent[0, :, LANES + 1, :].astype(F32)
    return sent[0, :, :LANES, :].astype(F32), sent[1, :, :LANES, :].astype(F32), decay[:, None, :]


def pack(forward, backward, decay):
    high = lax.reduce_precision(decay, 8, 7)
    rows = jnp.concatenate([high, decay - high, jnp.zeros(decay.shape[:1] + (6, LANES), F32)], axis=1)
    return jnp.stack([jnp.concatenate([forward, rows], axis=1), jnp.concatenate([backward, rows], axis=1)]).astype(BF16)


def seq_exchange(total):
    count = lax.axis_size("seq")
    index = lax.axis_index("seq")
    forward, backward, decay = unpack(total)
    entering = jnp.zeros_like(forward)
    leaving = jnp.zeros_like(backward)
    ahead = jnp.ones_like(decay)
    behind = jnp.ones_like(decay)
    distance = 1
    while distance < count:
        route = [(i, i ^ distance) for i in range(count)]
        upper = (index // distance) % 2 == 1
        last = 2 * distance >= count
        if last:
            got = lax.ppermute(jnp.where(upper, backward, forward).astype(BF16), "seq", route).astype(F32)
            entering = entering + jnp.where(upper, ahead * got, 0.0)
            leaving = leaving + jnp.where(upper, 0.0, behind * got)
        else:
            got_f, got_b, got_d = unpack(lax.ppermute(total, "seq", route))
            entering = entering + jnp.where(upper, ahead * got_f, 0.0)
            leaving = leaving + jnp.where(upper, 0.0, behind * got_b)
            ahead = jnp.where(upper, ahead * got_d, ahead)
            behind = jnp.where(upper, behind, behind * got_d)
            forward = jnp.where(upper, forward + decay * got_f, got_f + got_d * forward)
            backward = jnp.where(upper, got_b + got_d * backward, backward + decay * got_b)
            decay = decay * got_d
            total = pack(forward, backward, decay)
        distance *= 2
    return entering, leaving


def passed_along(block, axis, distance):
    devices = range(lax.axis_size(axis))
    route = [(i - distance, i) for i in devices if i - distance in devices]
    return lax.ppermute(block, axis, route)


def on_device(x, taps, step_size, decay_log, write_in, read_in, skip_gain, out_grad):
    count, heads_j, width = x.shape
    groups = decay_log.shape[1]
    pairs = groups // 2
    spans = count // SPAN
    heads = 2 * heads_j
    rim = taps.shape[0] - 1
    halo = passed_along(x[count - rim :], "seq", 1)

    def by_pair(array):
        return array.reshape(array.shape[:-2] + (heads_j, pairs, 2))

    rates = -jnp.exp(decay_log)
    steps = step_size.reshape(spans, SPAN, heads_j * groups)
    logd = steps * rates.reshape(1, 1, heads_j * groups)
    lower = jnp.tril(jnp.ones((SPAN, SPAN), F32))
    cumul = jnp.einsum("ts,bsh->bth", lower, logd, precision=lax.Precision.HIGHEST)
    ends = cumul[:, -1:]
    quantities = jnp.stack([cumul, steps, jnp.exp(cumul), jnp.exp(ends - cumul)], axis=2)
    quantities = quantities.reshape(count, 4, heads_j, pairs, 2)
    cols = jnp.transpose(quantities, (0, 3, 1, 2, 4)).reshape(count, pairs * 4 * heads)
    rows = jnp.transpose(by_pair(cumul.reshape(count, heads_j, groups)), (2, 1, 3, 0)).reshape(pairs, heads, count)
    end_logs = ends.reshape(spans, heads_j * groups)
    until = jnp.cumsum(end_logs, axis=0)
    from_start = jnp.exp(until - end_logs)
    to_end = jnp.exp(until[-1:] - until)

    def lanes_of(array):
        lead = array.shape[:-1]
        array = array.reshape(lead + (heads_j, groups, 1))
        return jnp.broadcast_to(array, lead + (heads_j, groups, HALF)).reshape(lead + (heads_j, width))

    from_start = lanes_of(from_start)
    to_end = lanes_of(to_end)
    skips = lanes_of(skip_gain.reshape(heads_j * groups))
    n_cols = cols.shape[1]
    last = spans - 1
    totals, values, s_all, r_all = [], [], [], []
    for p in range(pairs):
        kernel = functools.partial(states_kernel, p * 4 * heads)
        v, s_loc, r_loc, total = pl.pallas_call(
            kernel,
            grid=(spans,),
            in_specs=[
                pl.BlockSpec((SPAN, heads_j, LANES), lambda i, p=p: (i, 0, p)),
                pl.BlockSpec((rim, heads_j, LANES), lambda i, p=p: (0, 0, p)),
                pl.BlockSpec((4, heads_j, LANES), lambda i, p=p: (0, 0, p)),
                pl.BlockSpec((SPAN, 2 * LANES), lambda i, p=p: (i, p)),
                pl.BlockSpec((SPAN, n_cols), lambda i: (i, 0)),
                pl.BlockSpec((SPAN, heads_j, LANES), lambda i, p=p: (last - i, 0, p)),
                pl.BlockSpec((SPAN, 2 * LANES), lambda i, p=p: (last - i, p)),
                pl.BlockSpec((SPAN, n_cols), lambda i: (last - i, 0)),
            ],
            out_specs=[
                pl.BlockSpec((heads_j, SPAN, LANES), lambda i: (0, i, 0)),
                pl.BlockSpec((1, heads_j, LANES, LANES), lambda i: (i, 0, 0, 0)),
                pl.BlockSpec((1, heads_j, LANES, LANES), lambda i: (last - i, 0, 0, 0)),
                pl.BlockSpec((2, heads_j, LANES + EDGE, LANES), lambda i: (0, 0, 0, 0)),
            ],
            out_shape=[
                jax.ShapeDtypeStruct((heads_j, count, LANES), BF16),
                jax.ShapeDtypeStruct((spans, heads_j, LANES, LANES), BF16),
                jax.ShapeDtypeStruct((spans, heads_j, LANES, LANES), BF16),
                jax.ShapeDtypeStruct((2, heads_j, LANES + EDGE, LANES), BF16),
            ],
            scratch_shapes=[
                pltpu.VMEM((heads_j, SPAN + EDGE, LANES), F32),
                pltpu.VMEM((heads_j, LANES, LANES), F32),
                pltpu.VMEM((heads_j, LANES, LANES), F32),
                pltpu.VMEM((heads_j, LANES), F32),
            ],
            name=f"states{p}",
        )(x, halo, taps, write_in, cols, out_grad, read_in, cols)
        totals.append(total)
        values.append(v)
        s_all.append(s_loc)
        r_all.append(r_loc)

    both = [seq_exchange(total) for total in totals]
    mixed = dx = None
    cgs, ags, lgs, edges, dbs, dcs = [], [], [], [], [], []
    for p in range(pairs):
        entering, leaving = both[p]
        operands = [x, values[p], out_grad, write_in, read_in, cols, rows, s_all[p], r_all[p],
                    entering, leaving, from_start, to_end, taps, skips]
        time3 = pl.BlockSpec((SPAN, heads_j, LANES), lambda i, p=p: (last - i, 0, p))
        time2 = pl.BlockSpec((SPAN, 2 * LANES), lambda i, p=p: (last - i, p))
        state = pl.BlockSpec((1, heads_j, LANES, LANES), lambda i: (last - i, 0, 0, 0))
        whole = pl.BlockSpec((heads_j, LANES, LANES), lambda i: (0, 0, 0))
        lane_row = pl.BlockSpec((1, heads_j, LANES), lambda i, p=p: (last - i, 0, p))
        in_specs = [
            time3,
            pl.BlockSpec((heads_j, SPAN, LANES), lambda i: (0, last - i, 0)),
            time3, time2, time2,
            pl.BlockSpec((SPAN, n_cols), lambda i: (last - i, 0)),
            pl.BlockSpec((1, heads, SPAN), lambda i, p=p: (p, 0, last - i)),
            state, state, whole, whole, lane_row, lane_row,
            pl.BlockSpec((4, heads_j, LANES), lambda i, p=p: (0, 0, p)),
            pl.BlockSpec((heads_j, LANES), lambda i, p=p: (0, p)),
        ]
        aliases = {}
        if p > 0:
            aliases = {len(operands): 0, len(operands) + 1: 1}
            operands += [mixed, dx]
            in_specs += [pl.BlockSpec(memory_space=pl.ANY)] * 2
        mixed, dx, db, dc, cg, ag, lg, edge = pl.pallas_call(
            functools.partial(main_kernel, p * 4 * heads),
            grid=(spans,),
            in_specs=in_specs,
            out_specs=[
                time3, time3,
                pl.BlockSpec((SPAN, 2 * LANES), lambda i: (last - i, 0)),
                pl.BlockSpec((SPAN, 2 * LANES), lambda i: (last - i, 0)),
                pl.BlockSpec((4, heads_j, LANES), lambda i: (0, 0, 0)),
                pl.BlockSpec((heads_j, LANES), lambda i: (0, 0)),
                pl.BlockSpec((heads, SPAN), lambda i: (0, 0)),
                pl.BlockSpec((heads_j, EDGE, LANES), lambda i: (0, 0, 0)),
            ],
            out_shape=[
                jax.ShapeDtypeStruct(x.shape, BF16),
                jax.ShapeDtypeStruct(x.shape, BF16),
                jax.ShapeDtypeStruct((count, 2 * LANES), BF16),
                jax.ShapeDtypeStruct((count, 2 * LANES), BF16),
                jax.ShapeDtypeStruct((4, heads_j, LANES), F32),
                jax.ShapeDtypeStruct((heads_j, LANES), F32),
                jax.ShapeDtypeStruct((heads, SPAN), F32),
                jax.ShapeDtypeStruct((heads_j, EDGE, LANES), F32),
            ],
            scratch_shapes=[pltpu.VMEM((heads_j, SPAN + EDGE, LANES), F32)],
            input_output_aliases=aliases,
            name=f"main{p}",
        )(*operands)
        cgs.append(cg)
        ags.append(ag)
        lgs.append(lg)
        edges.append(edge)
        dbs.append(db)
        dcs.append(dc)

    edge = jnp.transpose(jnp.concatenate(edges, axis=-1)[:, :rim, :], (1, 0, 2))
    after = passed_along(edge, "seq", -1)
    fixes = []
    for row in range(rim):
        fix = 0.0
        for tap in range(row + 1):
            fix = fix + taps[tap] * after[row - tap]
        fixes.append(fix)
    tail = dx[count - rim :].astype(F32) + jnp.stack(fixes)
    dx = lax.dynamic_update_slice(dx, tail.astype(BF16), (count - rim, 0, 0))
    before = halo.astype(F32)
    conv_grad = jnp.concatenate(cgs, axis=-1)
    extra = []
    for tap in range(4):
        piece = jnp.zeros_like(conv_grad[0])
        for row in range(rim - tap):
            piece = piece + edge[row] * before[row + tap]
        extra.append(piece)
    conv_grad = conv_grad + jnp.stack(extra)
    ag = jnp.stack(ags).reshape(pairs, heads_j, 2, HALF).sum(-1)
    lg = jnp.stack(lgs).reshape(pairs, heads_j, 2, SPAN).sum(-1)
    decay_grad = jnp.transpose(ag + lg, (1, 0, 2)).reshape(heads_j, groups)
    conv_grad, decay_grad = lax.psum((conv_grad, decay_grad), "seq")
    write_grad, read_grad = lax.psum((jnp.concatenate(dbs, axis=1), jnp.concatenate(dcs, axis=1)), "head")
    return (mixed, dx, conv_grad, decay_grad, write_grad, read_grad)


def solution(mesh):
    return jax.shard_map(
        on_device,
        mesh=mesh,
        in_specs=(
            P("seq", "head", None),
            P(None, "head", None),
            P("seq", "head", None),
            P("head", None),
            P("seq", None),
            P("seq", None),
            P("head", None),
            P("seq", "head", None),
        ),
        out_specs=(
            P("seq", "head", None),
            P("seq", "head", None),
            P(None, "head", None),
            P("head", None),
            P("seq", None),
            P("seq", None),
        ),
        check_vma=False,
    )
```

```python
import functools

import jax
import jax.numpy as jnp
import numpy as np
from jax import lax
from jax.experimental import pallas as pl
from jax.experimental.pallas import tpu as pltpu
from jax.sharding import PartitionSpec as P

SPAN = 128
LANES = 128
HALF = 64
EDGE = 8
F32 = jnp.float32
BF16 = jnp.bfloat16
NT = (((1,), (1,)), ((), ()))
TN = (((0,), (0,)), ((), ()))
LOG2E = 1.4426950408889634
LN2 = 0.6931471805599453
PARTS = (3, 2, 2, 2, 2)


def dot(a, b, dims=None):
    if dims is None:
        return jnp.dot(a, b, preferred_element_type=F32)
    return lax.dot_general(a, b, dims, preferred_element_type=F32)


def low_half(rows):
    return lax.broadcasted_iota(jnp.int32, (rows, LANES), 1) < HALF


def split_parts(value, count):
    parts = []
    for _ in range(count - 1):
        part = value.astype(BF16)
        parts.append(part)
        value = value - part.astype(F32)
    parts.append(value.astype(BF16))
    return parts


def part_lane(quantity, part, head, heads):
    return (sum(PARTS[:quantity]) + part) * heads + head


def gather_matrix(heads_j, groups):
    heads, pairs, count = 2 * heads_j, groups // 2, sum(PARTS)
    matrix = np.zeros((count * heads_j * groups, pairs * LANES), np.float32)
    for part in range(count):
        for j in range(heads_j):
            for g in range(groups):
                matrix[part * heads_j * groups + j * groups + g, (g // 2) * LANES + part * heads + 2 * j + g % 2] = 1.0
    return matrix


def spread_matrix(quantity, heads_j):
    heads = 2 * heads_j
    matrix = np.zeros((LANES, heads_j * LANES), np.float32)
    for part in range(PARTS[quantity]):
        for h in range(heads):
            matrix[part_lane(quantity, part, h, heads), h * HALF : (h + 1) * HALF] = 1.0
    return matrix


def head_matrix(heads_j):
    heads = 2 * heads_j
    matrix = np.zeros((LANES, heads * LANES), np.float32)
    for part in range(PARTS[0]):
        for h in range(heads):
            matrix[part_lane(0, part, h, heads), h * LANES : (h + 1) * LANES] = 1.0
    return matrix


def scales_kernel(dt_ref, log_ref, gather_ref, parts_ref, rows_ref):
    count, heads_j, groups = dt_ref.shape
    every = heads_j * groups
    steps = jnp.swapaxes(dt_ref[...], 0, 1)
    steps = jnp.concatenate([steps[j] for j in range(heads_j)], axis=1)
    rates = -LOG2E * jnp.exp(log_ref[...])
    rates = jnp.concatenate([rates[j : j + 1] for j in range(heads_j)], axis=1)
    lower = (
        lax.broadcasted_iota(jnp.int32, (SPAN, SPAN), 0) >= lax.broadcasted_iota(jnp.int32, (SPAN, SPAN), 1)
    ).astype(BF16)
    for at in range(0, count, SPAN):
        dt = steps[at : at + SPAN]
        logs = jnp.concatenate(split_parts(dt * rates, 3), axis=1)
        summed = dot(lower, logs)
        cumul = summed[:, :every] + summed[:, every : 2 * every] + summed[:, 2 * every :]
        lead = jnp.exp2(cumul)
        tail = jnp.exp2(cumul[SPAN - 1 : SPAN] - cumul)
        parts = []
        for value, number in zip((cumul, dt, lead, tail, dt * tail), PARTS, strict=True):
            parts += split_parts(value, number)
        placed = dot(jnp.concatenate(parts, axis=1), gather_ref[...]).astype(BF16)
        for p in range(parts_ref.shape[0]):
            parts_ref[p, at : at + SPAN, :] = placed[:, p * LANES : (p + 1) * LANES]
        rows_ref[:, at : at + SPAN] = cumul.T


def states_kernel(
    x_ref, halo_ref, w_ref, b_ref, partf_ref, y_ref, c_ref, partr_ref, lead_ref, tail_ref, chain_ref,
    u_ref, slope_ref, s_ref, r_ref, from_ref, to_ref, total_ref, x_buf, s_acc, r_acc, f_acc, t_acc,
):
    step = pl.program_id(0)
    rows, heads_j, _ = x_ref.shape
    low = low_half(SPAN)

    @pl.when(step == 0)
    def _():
        s_acc[...] = jnp.zeros_like(s_acc)
        r_acc[...] = jnp.zeros_like(r_acc)
        f_acc[...] = jnp.ones_like(f_acc)
        t_acc[...] = jnp.ones_like(t_acc)
        halo = halo_ref[...].astype(F32)
        for j in range(heads_j):
            for row in range(3):
                x_buf[j, EDGE - 3 + row : EDGE - 2 + row, :] = halo[row, j : j + 1, :]

    @pl.when(step > 0)
    def _():
        x_buf[:, 0:EDGE, :] = x_buf[:, rows : rows + EDGE, :]

    x_buf[:, EDGE : EDGE + rows, :] = jnp.swapaxes(x_ref[...], 0, 1).astype(F32)
    weights = w_ref[...]
    grads_all = jnp.swapaxes(y_ref[...], 0, 1)
    number = rows // SPAN
    for k in range(number):
        here = slice(k * SPAN, (k + 1) * SPAN)
        m = number - 1 - k
        there = slice(m * SPAN, (m + 1) * SPAN)
        partf = partf_ref[0, here, :]
        tails = dot(partf, tail_ref[...])
        leads = dot(jnp.concatenate([partr_ref[0, there, :], partf[SPAN - EDGE :]], axis=0), lead_ref[...])
        s_ref[k] = s_acc[...].astype(BF16)
        r_ref[m] = r_acc[...].astype(BF16)
        from_ref[k] = f_acc[...]
        to_ref[m] = t_acc[...]
        wrote, read = [], []
        for j in range(heads_j):
            lanes = slice(j * LANES, (j + 1) * LANES)
            base = EDGE - 3 + k * SPAN
            v = weights[0, j : j + 1, :] * x_buf[j, base : base + SPAN, :]
            for tap in range(1, 4):
                v = v + weights[tap, j : j + 1, :] * x_buf[j, base + tap : base + tap + SPAN, :]
            gate = 0.5 + 0.5 * jnp.tanh(0.5 * v)
            u = v * gate
            u_ref[j, here, :] = u.astype(BF16)
            slope_ref[j, here, :] = (gate + u * (1.0 - gate)).astype(BF16)
            wrote.append((u * tails[:, lanes]).astype(BF16))
            read.append((grads_all[j, there].astype(F32) * leads[:SPAN, lanes]).astype(BF16))
        own_s = dot(b_ref[here, :], jnp.concatenate(wrote, axis=1), TN)
        own_r = dot(c_ref[there, :], jnp.concatenate(read, axis=1), TN)
        for j in range(heads_j):
            lanes = slice(j * LANES, (j + 1) * LANES)
            keep = leads[SPAN + EDGE - 1 : SPAN + EDGE, lanes]
            s_acc[j] = keep * s_acc[j] + jnp.where(low, own_s[:LANES, lanes], own_s[LANES:, lanes])
            f_acc[j : j + 1, :] = f_acc[j : j + 1, :] * keep
            keep = leads[SPAN - 1 : SPAN, lanes]
            r_acc[j] = keep * r_acc[j] + jnp.where(low, own_r[:LANES, lanes], own_r[LANES:, lanes])
            t_acc[j : j + 1, :] = t_acc[j : j + 1, :] * keep

    @pl.when(step == pl.num_programs(0) - 1)
    def _():
        total_ref[0, :, :LANES, :] = s_acc[...].astype(BF16)
        total_ref[1, :, :LANES, :] = r_acc[...].astype(BF16)
        for j in range(heads_j):
            decay = f_acc[j : j + 1, :]
            high = decay.astype(BF16).astype(F32)
            pair = jnp.concatenate([high, decay - high, jnp.zeros((6, LANES), F32)], axis=0)
            total_ref[0, j, LANES:, :] = pair.astype(BF16)
            total_ref[1, j, LANES:, :] = pair.astype(BF16)


def fold(value):
    return jnp.sum(value.reshape(value.shape[0] // 8, 8, value.shape[1]), axis=0)


def main_kernel(
    head0, core_ref, x_ref, u_ref, slope_ref, y_ref, b_ref, c_ref, part_ref, row_ref, s_ref, r_ref,
    enter_ref, leave_ref, from_ref, to_ref, w_ref, skip_ref, heads_ref, a_ref, dt_ref, e_ref, f_ref, df_ref, *rest,
):
    mixed_ref, dx_ref, keep_ref, send_ref, sums_ref, edge_ref, dv_buf, acc = rest[-8:]
    step = pl.program_id(0)
    span, heads_j, _ = x_ref.shape
    groups = row_ref.shape[0] // heads_j
    low = low_half(span)
    causal = lax.broadcasted_iota(jnp.int32, (span, span), 0) >= lax.broadcasted_iota(
        jnp.int32, (span, span), 1
    )

    @pl.when(step == 0)
    def _():
        acc[...] = jnp.zeros_like(acc)
        dv_buf[:, span : span + EDGE, :] = jnp.zeros((heads_j, EDGE, LANES), F32)

    @pl.when(step > 0)
    def _():
        dv_buf[:, span : span + EDGE, :] = dv_buf[:, 0:EDGE, :]

    xs = jnp.swapaxes(x_ref[...], 0, 1)
    grads = jnp.swapaxes(y_ref[...], 0, 1)
    b_all = b_ref[...]
    c_all = c_ref[...]
    weights = w_ref[...]
    skips = skip_ref[...]
    part = part_ref[0]
    zero = jnp.zeros((span, LANES), BF16)
    scores = [dot(c_all[:, g * LANES : (g + 1) * LANES], b_all[:, g * LANES : (g + 1) * LANES], NT) for g in range(2)]
    score_grads = [None, None]
    states, rstates, state_cat, rstate_cat = [], [], [], []
    for j in range(heads_j):
        state = s_ref[0, j].astype(F32) + from_ref[0, j : j + 1, :] * enter_ref[j]
        rstate = r_ref[0, j].astype(F32) + to_ref[0, j : j + 1, :] * leave_ref[j]
        states.append(fold(state * rstate))
        state = state.astype(BF16)
        rstate = rstate.astype(BF16)
        state_cat.append(jnp.concatenate([jnp.where(low, state, zero), jnp.where(low, zero, state)], axis=0))
        rstate_cat.append(jnp.concatenate([jnp.where(low, rstate, zero), jnp.where(low, zero, rstate)], axis=0))
    state_cat = jnp.concatenate(state_cat, axis=1)
    rstate_cat = jnp.concatenate(rstate_cat, axis=1)
    carried_all = dot(c_all, state_cat)
    back_all = dot(b_all, rstate_cat)
    out_rows, leads, tails = [], [], []
    for j in range(heads_j):
        lanes = slice(j * LANES, (j + 1) * LANES)
        a_b = dot(part, a_ref[:, lanes])
        dt_b = dot(part, dt_ref[:, lanes])
        e_b = dot(part, e_ref[:, lanes])
        f_b = dot(part, f_ref[:, lanes])
        df_b = dot(part, df_ref[:, lanes])
        a_last = a_b[span - 1 : span]
        e_last = e_b[span - 1 : span]
        u = u_ref[j].astype(F32)
        dy16 = grads[j]
        dy = dy16.astype(F32)
        val16 = (u * dt_b).astype(BF16)
        val = val16.astype(F32)
        tails.append((u * df_b).astype(BF16))
        leads.append((dy * e_b).astype(BF16))
        dy_two = jnp.concatenate([jnp.where(low, dy16, zero), jnp.where(low, zero, dy16)], axis=0)
        val_two = jnp.concatenate([jnp.where(low, val16, zero), jnp.where(low, zero, val16)], axis=0)
        products = dot(dy_two, val16, NT)
        mixes = []
        for g in range(2):
            h = 2 * j + g
            at = j * groups + head0 + g
            spread = dot(part, heads_ref[:, h * LANES : (h + 1) * LANES]) - row_ref[at : at + 1, :]
            decay = jnp.exp2(jnp.where(causal, spread, -jnp.inf))
            mixes.append((scores[g] * decay).astype(BF16))
            weighted = decay * products[g * span : (g + 1) * span]
            score_grads[g] = weighted if score_grads[g] is None else score_grads[g] + weighted
        inner = dot(jnp.concatenate(mixes, axis=1), val_two)
        dval = dot(jnp.concatenate(mixes, axis=0), dy_two, TN)
        carried = carried_all[:, lanes] * e_b
        back = back_all[:, lanes] * f_b
        out = inner + carried
        dval_full = dval + back
        log_part = a_b * (dy * out - val * dval_full) + a_last * (val * back)
        acc[4, j] = acc[4, j] + fold(log_part) + states[j] * (a_last * e_last)
        skip = skips[j : j + 1, :]
        out_rows.append((out + skip * u).astype(BF16))
        dv_buf[j, 0:span, :] = (dt_b * dval_full + skip * dy) * slope_ref[j].astype(F32)
    mixed_ref[...] = jnp.swapaxes(jnp.stack(out_rows, axis=0), 0, 1)
    dc_inter = dot(jnp.concatenate(leads, axis=1), state_cat, NT)
    db_inter = dot(jnp.concatenate(tails, axis=1), rstate_cat, NT)
    dx_rows = []
    for j in range(heads_j):
        x = xs[j].astype(F32)
        total = None
        for tap in range(4):
            shifted = dv_buf[j, 3 - tap : 3 - tap + span, :]
            piece = weights[tap, j : j + 1, :] * shifted
            total = piece if total is None else total + piece
            acc[tap, j] = acc[tap, j] + fold(shifted * x)
        dx_rows.append(total.astype(BF16))
    dx_ref[...] = jnp.swapaxes(jnp.stack(dx_rows, axis=0), 0, 1)
    dbs, dcs = [], []
    for g in range(2):
        inside = slice(g * LANES, (g + 1) * LANES)
        flow = score_grads[g].astype(BF16)
        dcs.append((dot(flow, b_all[:, inside]) + dc_inter[:, inside]).astype(BF16))
        dbs.append((dot(flow, c_all[:, inside], TN) + db_inter[:, inside]).astype(BF16))
    db = jnp.concatenate(dbs, axis=1)
    dc = jnp.concatenate(dcs, axis=1)

    @pl.when(core_ref[0] == 0)
    def _():
        keep_ref[...] = db
        send_ref[...] = dc

    @pl.when(core_ref[0] != 0)
    def _():
        keep_ref[...] = dc
        send_ref[...] = db

    @pl.when(step == pl.num_programs(0) - 1)
    def _():
        edge_ref[...] = dv_buf[:, 0:EDGE, :]
        for tap in range(5):
            for j in range(heads_j):
                sums_ref[tap, j : j + 1, :] = jnp.sum(acc[tap, j], axis=0, keepdims=True)


def place_kernel(core_ref, mine_ref, got_ref, *rest):
    write_ref, read_ref = rest[-2:]

    @pl.when(core_ref[0] == 0)
    def _():
        write_ref[...] = mine_ref[...]
        read_ref[...] = got_ref[...]

    @pl.when(core_ref[0] != 0)
    def _():
        write_ref[...] = got_ref[...]
        read_ref[...] = mine_ref[...]


def edge_kernel(after_ref, w_ref, dx_ref, out_ref):
    rows = dx_ref.shape[0]
    weights = w_ref[...]
    after = after_ref[...]
    out_ref[: rows - 3] = dx_ref[: rows - 3]
    for row in range(3):
        fix = weights[0] * after[row]
        for tap in range(1, row + 1):
            fix = fix + weights[tap] * after[row - tap]
        at = rows - 3 + row
        out_ref[at] = (dx_ref[at].astype(F32) + fix).astype(BF16)


def unpack(sent):
    decay = sent[0, :, LANES, :].astype(F32) + sent[0, :, LANES + 1, :].astype(F32)
    return sent[0, :, :LANES, :].astype(F32), sent[1, :, :LANES, :].astype(F32), decay[:, None, :]


def pack(forward, backward, decay):
    high = lax.reduce_precision(decay, 8, 7)
    rows = jnp.concatenate([high, decay - high, jnp.zeros(decay.shape[:1] + (6, LANES), F32)], axis=1)
    return jnp.stack([jnp.concatenate([forward, rows], axis=1), jnp.concatenate([backward, rows], axis=1)]).astype(BF16)


def seq_exchange(total):
    count = lax.axis_size("seq")
    index = lax.axis_index("seq")
    forward, backward, decay = unpack(total)
    entering = jnp.zeros_like(forward)
    leaving = jnp.zeros_like(backward)
    ahead = jnp.ones_like(decay)
    behind = jnp.ones_like(decay)
    distance = 1
    while distance < count:
        route = [(i, i ^ distance) for i in range(count)]
        upper = (index // distance) % 2 == 1
        last = 2 * distance >= count
        if last:
            got = lax.ppermute(jnp.where(upper, backward, forward).astype(BF16), "seq", route).astype(F32)
            entering = entering + jnp.where(upper, ahead * got, 0.0)
            leaving = leaving + jnp.where(upper, 0.0, behind * got)
        else:
            got_f, got_b, got_d = unpack(lax.ppermute(total, "seq", route))
            entering = entering + jnp.where(upper, ahead * got_f, 0.0)
            leaving = leaving + jnp.where(upper, 0.0, behind * got_b)
            ahead = jnp.where(upper, ahead * got_d, ahead)
            behind = jnp.where(upper, behind, behind * got_d)
            forward = jnp.where(upper, forward + decay * got_f, got_f + got_d * forward)
            backward = jnp.where(upper, got_b + got_d * backward, backward + decay * got_b)
            decay = decay * got_d
            total = pack(forward, backward, decay)
        distance *= 2
    return entering, leaving


def passed_along(block, axis, distance):
    devices = range(lax.axis_size(axis))
    route = [(i - distance, i) for i in devices if i - distance in devices]
    return lax.ppermute(block, axis, route)


def swap_sum(value, axis):
    count = lax.axis_size(axis)
    distance = 1
    while distance < count:
        value = value + lax.ppermute(value, axis, [(i, i ^ distance) for i in range(count)])
        distance *= 2
    return value


def on_device(x, taps, step_size, decay_log, write_in, read_in, skip_gain, out_grad):
    count, heads_j, width = x.shape
    groups = decay_log.shape[1]
    pairs = groups // 2
    spans = count // SPAN
    heads = 2 * heads_j
    rim = taps.shape[0] - 1
    n_head = lax.axis_size("head")
    core = (lax.axis_index("head") % 2).astype(jnp.int32).reshape(1)
    halo = passed_along(x[count - rim :], "seq", 1)
    per = 4 if spans % 4 == 0 else 1
    gather = jnp.asarray(gather_matrix(heads_j, groups), BF16)
    parts, rows = pl.pallas_call(
        scales_kernel,
        grid=(spans // per,),
        in_specs=[
            pl.BlockSpec((per * SPAN, heads_j, groups), lambda i: (i, 0, 0)),
            pl.BlockSpec((heads_j, groups), lambda i: (0, 0)),
            pl.BlockSpec(gather.shape, lambda i: (0, 0)),
        ],
        out_specs=[
            pl.BlockSpec((pairs, per * SPAN, LANES), lambda i: (0, i, 0)),
            pl.BlockSpec((heads_j * groups, per * SPAN), lambda i: (0, i)),
        ],
        out_shape=[
            jax.ShapeDtypeStruct((pairs, count, LANES), BF16),
            jax.ShapeDtypeStruct((heads_j * groups, count), F32),
        ],
        name="scales",
    )(step_size, decay_log, gather)
    skips = jnp.broadcast_to(skip_gain[:, :, None], (heads_j, groups, HALF)).reshape(heads_j, width)
    a_m, dt_m, e_m, f_m, df_m = (jnp.asarray(spread_matrix(q, heads_j), BF16) for q in range(5))
    heads_m = jnp.asarray(head_matrix(heads_j), BF16)

    def fixed(array):
        return pl.BlockSpec(array.shape, lambda i: (0,) * array.ndim)

    per = 2 if spans % 2 == 0 else 1
    size = per * SPAN
    end = spans // per - 1
    totals, values, slopes, s_all, r_all, froms, tos = [], [], [], [], [], [], []
    chain = parts
    for p in range(pairs):
        u, slope, s_loc, r_loc, from_start, to_end, total = pl.pallas_call(
            states_kernel,
            grid=(spans // per,),
            in_specs=[
                pl.BlockSpec((size, heads_j, LANES), lambda i, p=p: (i, 0, p)),
                pl.BlockSpec((rim, heads_j, LANES), lambda i, p=p: (0, 0, p)),
                pl.BlockSpec((4, heads_j, LANES), lambda i, p=p: (0, 0, p)),
                pl.BlockSpec((size, 2 * LANES), lambda i, p=p: (i, p)),
                pl.BlockSpec((1, size, LANES), lambda i, p=p: (p, i, 0)),
                pl.BlockSpec((size, heads_j, LANES), lambda i, p=p: (end - i, 0, p)),
                pl.BlockSpec((size, 2 * LANES), lambda i, p=p: (end - i, p)),
                pl.BlockSpec((1, size, LANES), lambda i, p=p: (p, end - i, 0)),
                fixed(e_m), fixed(df_m),
                pl.BlockSpec(memory_space=pl.ANY),
            ],
            out_specs=[
                pl.BlockSpec((heads_j, size, LANES), lambda i: (0, i, 0)),
                pl.BlockSpec((heads_j, size, LANES), lambda i: (0, i, 0)),
                pl.BlockSpec((per, heads_j, LANES, LANES), lambda i: (i, 0, 0, 0)),
                pl.BlockSpec((per, heads_j, LANES, LANES), lambda i: (end - i, 0, 0, 0)),
                pl.BlockSpec((per, heads_j, LANES), lambda i: (i, 0, 0)),
                pl.BlockSpec((per, heads_j, LANES), lambda i: (end - i, 0, 0)),
                pl.BlockSpec((2, heads_j, LANES + EDGE, LANES), lambda i: (0, 0, 0, 0)),
            ],
            out_shape=[
                jax.ShapeDtypeStruct((heads_j, count, LANES), BF16),
                jax.ShapeDtypeStruct((heads_j, count, LANES), BF16),
                jax.ShapeDtypeStruct((spans, heads_j, LANES, LANES), BF16),
                jax.ShapeDtypeStruct((spans, heads_j, LANES, LANES), BF16),
                jax.ShapeDtypeStruct((spans, heads_j, LANES), F32),
                jax.ShapeDtypeStruct((spans, heads_j, LANES), F32),
                jax.ShapeDtypeStruct((2, heads_j, LANES + EDGE, LANES), BF16),
            ],
            scratch_shapes=[
                pltpu.VMEM((heads_j, size + EDGE, LANES), F32),
                pltpu.VMEM((heads_j, LANES, LANES), F32),
                pltpu.VMEM((heads_j, LANES, LANES), F32),
                pltpu.VMEM((heads_j, LANES), F32),
                pltpu.VMEM((heads_j, LANES), F32),
            ],
            name=f"states{p}",
        )(x, halo, taps, write_in, parts, out_grad, read_in, parts, e_m, df_m, chain)
        chain = s_loc
        totals.append(total)
        values.append(u)
        slopes.append(slope)
        s_all.append(s_loc)
        r_all.append(r_loc)
        froms.append(from_start)
        tos.append(to_end)

    both = [seq_exchange(total) for total in totals]
    last = spans - 1
    mixed = dx = write_grad = read_grad = None
    sums, edges = [], []
    smem = pl.BlockSpec(memory_space=pltpu.SMEM)
    anywhere = pl.BlockSpec(memory_space=pl.ANY)
    for p in range(pairs):
        entering, leaving = both[p]
        operands = [core, x, values[p], slopes[p], out_grad, write_in, read_in, parts, rows, s_all[p], r_all[p],
                    entering, leaving, froms[p], tos[p], taps, skips, heads_m, a_m, dt_m, e_m, f_m, df_m, chain]
        time3 = pl.BlockSpec((SPAN, heads_j, LANES), lambda i, p=p: (last - i, 0, p))
        time2 = pl.BlockSpec((SPAN, 2 * LANES), lambda i, p=p: (last - i, p))
        own3 = pl.BlockSpec((heads_j, SPAN, LANES), lambda i: (0, last - i, 0))
        own2 = pl.BlockSpec((SPAN, 2 * LANES), lambda i: (last - i, 0))
        state = pl.BlockSpec((1, heads_j, LANES, LANES), lambda i: (last - i, 0, 0, 0))
        lane_row = pl.BlockSpec((1, heads_j, LANES), lambda i: (last - i, 0, 0))
        in_specs = [
            smem, time3, own3, own3, time3, time2, time2,
            pl.BlockSpec((1, SPAN, LANES), lambda i, p=p: (p, last - i, 0)),
            pl.BlockSpec((heads_j * groups, SPAN), lambda i: (0, last - i)),
            state, state, fixed(entering), fixed(leaving), lane_row, lane_row,
            pl.BlockSpec((4, heads_j, LANES), lambda i, p=p: (0, 0, p)),
            pl.BlockSpec((heads_j, LANES), lambda i, p=p: (0, p)),
            fixed(heads_m), fixed(a_m), fixed(dt_m), fixed(e_m), fixed(f_m), fixed(df_m), anywhere,
        ]
        aliases = {}
        if p > 0:
            aliases = {len(operands): 0, len(operands) + 1: 1}
            operands += [mixed, dx]
            in_specs += [anywhere] * 2
        mixed, dx, keep, send, total, edge = pl.pallas_call(
            functools.partial(main_kernel, 2 * p),
            grid=(spans,),
            in_specs=in_specs,
            out_specs=[
                time3, time3, own2, own2,
                pl.BlockSpec((5, heads_j, LANES), lambda i: (0, 0, 0)),
                pl.BlockSpec((heads_j, EDGE, LANES), lambda i: (0, 0, 0)),
            ],
            out_shape=[
                jax.ShapeDtypeStruct(x.shape, BF16),
                jax.ShapeDtypeStruct(x.shape, BF16),
                jax.ShapeDtypeStruct((count, 2 * LANES), BF16),
                jax.ShapeDtypeStruct((count, 2 * LANES), BF16),
                jax.ShapeDtypeStruct((5, heads_j, LANES), F32),
                jax.ShapeDtypeStruct((heads_j, EDGE, LANES), F32),
            ],
            scratch_shapes=[
                pltpu.VMEM((heads_j, SPAN + EDGE, LANES), F32),
                pltpu.VMEM((5, heads_j, EDGE, LANES), F32),
            ],
            input_output_aliases=aliases,
            name=f"main{p}",
        )(*operands)
        sums.append(total)
        edges.append(edge)
        cores = [(i, i ^ 1) for i in range(n_head)]
        mine = keep + lax.ppermute(send, "head", cores)
        distance = 2
        while distance < n_head:
            mine = mine + lax.ppermute(mine, "head", [(i, i ^ distance) for i in range(n_head)])
            distance *= 2
        got = lax.ppermute(mine, "head", cores)
        operands, in_specs, aliases = [core, mine, got], None, {}
        big = per * 3 * SPAN if spans % (per * 3) == 0 else SPAN
        block = pl.BlockSpec((big, 2 * LANES), lambda i: (i, 0))
        in_specs = [smem, block, block]
        if p > 0:
            operands += [write_grad, read_grad]
            in_specs += [anywhere] * 2
            aliases = {3: 0, 4: 1}
        write_grad, read_grad = pl.pallas_call(
            place_kernel,
            grid=(count // big,),
            in_specs=in_specs,
            out_specs=[pl.BlockSpec((big, 2 * LANES), lambda i, p=p: (i, p))] * 2,
            out_shape=[jax.ShapeDtypeStruct((count, groups * LANES), BF16)] * 2,
            input_output_aliases=aliases,
            name=f"place{p}",
        )(*operands)

    edge = jnp.transpose(jnp.concatenate(edges, axis=-1)[:, :rim, :], (1, 0, 2))
    after = passed_along(edge, "seq", -1)
    tail_spec = pl.BlockSpec((EDGE, heads_j, width), lambda i: (count // EDGE - 1, 0, 0))
    dx = pl.pallas_call(
        edge_kernel,
        grid=(1,),
        in_specs=[fixed(after), fixed(taps), tail_spec],
        out_specs=tail_spec,
        out_shape=jax.ShapeDtypeStruct(x.shape, BF16),
        input_output_aliases={2: 0},
        name="edge",
    )(after, taps, dx)
    before = halo.astype(F32)
    sums = jnp.concatenate(sums, axis=-1)
    extra = []
    for tap in range(5):
        piece = jnp.zeros_like(sums[0])
        for row in range(rim - tap):
            piece = piece + edge[row] * before[row + tap]
        extra.append(piece)
    sums = swap_sum(sums + jnp.stack(extra), "seq")
    conv_grad = sums[:4]
    decay_grad = LN2 * sums[4].reshape(heads_j, groups, HALF).sum(-1)
    return (mixed, dx, conv_grad, decay_grad, write_grad, read_grad)


def solution(mesh):
    return jax.shard_map(
        on_device,
        mesh=mesh,
        in_specs=(
            P("seq", "head", None),
            P(None, "head", None),
            P("seq", "head", None),
            P("head", None),
            P("seq", None),
            P("seq", None),
            P("head", None),
            P("seq", "head", None),
        ),
        out_specs=(
            P("seq", "head", None),
            P("seq", "head", None),
            P(None, "head", None),
            P("head", None),
            P("seq", None),
            P("seq", None),
        ),
        check_vma=False,
    )
```

```python
import functools

import jax
import jax.numpy as jnp
import numpy as np
from jax import lax
from jax.experimental import pallas as pl
from jax.experimental.pallas import tpu as pltpu
from jax.sharding import PartitionSpec as P

SPAN = 128
LANES = 128
HALF = 64
EDGE = 8
F32 = jnp.float32
BF16 = jnp.bfloat16
NT = (((1,), (1,)), ((), ()))
TN = (((0,), (0,)), ((), ()))
LOG2E = 1.4426950408889634
LN2 = 0.6931471805599453
PARTS = (3, 2, 2, 2, 2)


def cost(microseconds):
    return pl.CostEstimate(flops=int(microseconds * 1.15e9), transcendentals=0, bytes_accessed=0)


def dot(a, b, dims=None):
    if dims is None:
        return jnp.dot(a, b, preferred_element_type=F32)
    return lax.dot_general(a, b, dims, preferred_element_type=F32)


def low_half(rows):
    return lax.broadcasted_iota(jnp.int32, (rows, LANES), 1) < HALF


def split_parts(value, count):
    parts = []
    for _ in range(count - 1):
        part = value.astype(BF16)
        parts.append(part)
        value = value - part.astype(F32)
    parts.append(value.astype(BF16))
    return parts


def part_lane(quantity, part, head, heads):
    return (sum(PARTS[:quantity]) + part) * heads + head


def gather_matrix(heads_j, groups):
    heads, pairs, count = 2 * heads_j, groups // 2, sum(PARTS)
    matrix = np.zeros((count * heads_j * groups, pairs * LANES), np.float32)
    for part in range(count):
        for j in range(heads_j):
            for g in range(groups):
                matrix[part * heads_j * groups + j * groups + g, (g // 2) * LANES + part * heads + 2 * j + g % 2] = 1.0
    return matrix


def spread_matrix(quantity, heads_j):
    heads = 2 * heads_j
    matrix = np.zeros((LANES, heads_j * LANES), np.float32)
    for part in range(PARTS[quantity]):
        for h in range(heads):
            matrix[part_lane(quantity, part, h, heads), h * HALF : (h + 1) * HALF] = 1.0
    return matrix


def head_matrix(heads_j):
    heads = 2 * heads_j
    matrix = np.zeros((LANES, heads * LANES), np.float32)
    for part in range(PARTS[0]):
        for h in range(heads):
            matrix[part_lane(0, part, h, heads), h * LANES : (h + 1) * LANES] = 1.0
    return matrix


def scales_kernel(dt_ref, log_ref, gather_ref, parts_ref, rows_ref):
    count, heads_j, groups = dt_ref.shape
    every = heads_j * groups
    steps = jnp.swapaxes(dt_ref[...], 0, 1)
    steps = jnp.concatenate([steps[j] for j in range(heads_j)], axis=1)
    rates = -LOG2E * jnp.exp(log_ref[...])
    rates = jnp.concatenate([rates[j : j + 1] for j in range(heads_j)], axis=1)
    lower = (
        lax.broadcasted_iota(jnp.int32, (SPAN, SPAN), 0) >= lax.broadcasted_iota(jnp.int32, (SPAN, SPAN), 1)
    ).astype(BF16)
    for at in range(0, count, SPAN):
        dt = steps[at : at + SPAN]
        logs = jnp.concatenate(split_parts(dt * rates, 3), axis=1)
        summed = dot(lower, logs)
        cumul = summed[:, :every] + summed[:, every : 2 * every] + summed[:, 2 * every :]
        lead = jnp.exp2(cumul)
        tail = jnp.exp2(cumul[SPAN - 1 : SPAN] - cumul)
        parts = []
        for value, number in zip((cumul, dt, lead, tail, dt * tail), PARTS, strict=True):
            parts += split_parts(value, number)
        placed = dot(jnp.concatenate(parts, axis=1), gather_ref[...]).astype(BF16)
        for p in range(parts_ref.shape[0]):
            parts_ref[p, at : at + SPAN, :] = placed[:, p * LANES : (p + 1) * LANES]
        rows_ref[:, at : at + SPAN] = cumul.T


def states_kernel(
    x_ref, halo_ref, w_ref, b_ref, partf_ref, y_ref, c_ref, partr_ref, lead_ref, tail_ref,
    u_ref, slope_ref, s_ref, r_ref, from_ref, to_ref, total_ref, x_buf, s_acc, r_acc, f_acc, t_acc,
):
    step = pl.program_id(0)
    rows, heads_j, _ = x_ref.shape
    low = low_half(SPAN)

    @pl.when(step == 0)
    def _():
        s_acc[...] = jnp.zeros_like(s_acc)
        r_acc[...] = jnp.zeros_like(r_acc)
        f_acc[...] = jnp.ones_like(f_acc)
        t_acc[...] = jnp.ones_like(t_acc)
        halo = halo_ref[...].astype(F32)
        for j in range(heads_j):
            for row in range(3):
                x_buf[j, EDGE - 3 + row : EDGE - 2 + row, :] = halo[row, j : j + 1, :]

    @pl.when(step > 0)
    def _():
        x_buf[:, 0:EDGE, :] = x_buf[:, rows : rows + EDGE, :]

    x_buf[:, EDGE : EDGE + rows, :] = jnp.swapaxes(x_ref[...], 0, 1).astype(F32)
    weights = w_ref[...]
    grads_all = jnp.swapaxes(y_ref[...], 0, 1)
    number = rows // SPAN
    for k in range(number):
        here = slice(k * SPAN, (k + 1) * SPAN)
        m = number - 1 - k
        there = slice(m * SPAN, (m + 1) * SPAN)
        partf = partf_ref[0, here, :]
        tails = dot(partf, tail_ref[...])
        leads = dot(jnp.concatenate([partr_ref[0, there, :], partf[SPAN - EDGE :]], axis=0), lead_ref[...])
        s_ref[k] = s_acc[...].astype(BF16)
        r_ref[m] = r_acc[...].astype(BF16)
        from_ref[k] = f_acc[...]
        to_ref[m] = t_acc[...]
        wrote, read = [], []
        for j in range(heads_j):
            lanes = slice(j * LANES, (j + 1) * LANES)
            base = EDGE - 3 + k * SPAN
            v = weights[0, j : j + 1, :] * x_buf[j, base : base + SPAN, :]
            for tap in range(1, 4):
                v = v + weights[tap, j : j + 1, :] * x_buf[j, base + tap : base + tap + SPAN, :]
            gate = 0.5 + 0.5 * jnp.tanh(0.5 * v)
            u = v * gate
            u_ref[j, here, :] = u.astype(BF16)
            slope_ref[j, here, :] = (gate + u * (1.0 - gate)).astype(BF16)
            wrote.append((u * tails[:, lanes]).astype(BF16))
            read.append((grads_all[j, there].astype(F32) * leads[:SPAN, lanes]).astype(BF16))
        own_s = dot(b_ref[here, :], jnp.concatenate(wrote, axis=1), TN)
        own_r = dot(c_ref[there, :], jnp.concatenate(read, axis=1), TN)
        for j in range(heads_j):
            lanes = slice(j * LANES, (j + 1) * LANES)
            keep = leads[SPAN + EDGE - 1 : SPAN + EDGE, lanes]
            s_acc[j] = keep * s_acc[j] + jnp.where(low, own_s[:LANES, lanes], own_s[LANES:, lanes])
            f_acc[j : j + 1, :] = f_acc[j : j + 1, :] * keep
            keep = leads[SPAN - 1 : SPAN, lanes]
            r_acc[j] = keep * r_acc[j] + jnp.where(low, own_r[:LANES, lanes], own_r[LANES:, lanes])
            t_acc[j : j + 1, :] = t_acc[j : j + 1, :] * keep

    @pl.when(step == pl.num_programs(0) - 1)
    def _():
        total_ref[0, :, :LANES, :] = s_acc[...].astype(BF16)
        total_ref[1, :, :LANES, :] = r_acc[...].astype(BF16)
        for j in range(heads_j):
            decay = f_acc[j : j + 1, :]
            high = decay.astype(BF16).astype(F32)
            pair = jnp.concatenate([high, decay - high, jnp.zeros((6, LANES), F32)], axis=0)
            total_ref[0, j, LANES:, :] = pair.astype(BF16)
            total_ref[1, j, LANES:, :] = pair.astype(BF16)


def fold(value):
    return jnp.sum(value.reshape(value.shape[0] // 8, 8, value.shape[1]), axis=0)


def main_kernel(
    head0, core_ref, x_ref, u_ref, slope_ref, y_ref, b_ref, c_ref, part_ref, row_ref, s_ref, r_ref,
    near_in, near_out, reach_ref, far_ref, from_ref, to_ref, w_ref, skip_ref, heads_ref, a_ref, dt_ref, *rest,
):
    mixed_ref, dx_ref, keep_ref, send_ref, sums_ref, edge_ref, dv_buf, acc, enter_ref, leave_ref = rest[-10:]
    step = pl.program_id(0)
    span, heads_j, _ = x_ref.shape
    groups = row_ref.shape[0] // heads_j
    low = low_half(span)
    causal = lax.broadcasted_iota(jnp.int32, (span, span), 0) >= lax.broadcasted_iota(
        jnp.int32, (span, span), 1
    )

    @pl.when(step == 0)
    def _():
        acc[...] = jnp.zeros_like(acc)
        dv_buf[:, span : span + EDGE, :] = jnp.zeros((heads_j, EDGE, LANES), F32)
        far = far_ref[...].astype(F32)

        @pl.when(core_ref[1] == 1)
        def _():
            enter_ref[...] = near_in[...] + reach_ref[0][:, None, :] * far
            leave_ref[...] = near_out[...]

        @pl.when(core_ref[1] == 0)
        def _():
            enter_ref[...] = near_in[...]
            leave_ref[...] = near_out[...] + reach_ref[1][:, None, :] * far

    @pl.when(step > 0)
    def _():
        dv_buf[:, span : span + EDGE, :] = dv_buf[:, 0:EDGE, :]

    xs = jnp.swapaxes(x_ref[...], 0, 1)
    grads = jnp.swapaxes(y_ref[...], 0, 1)
    b_all = b_ref[...]
    c_all = c_ref[...]
    weights = w_ref[...]
    skips = skip_ref[...]
    part = part_ref[0]
    zero = jnp.zeros((span, LANES), BF16)
    def diagonal(array):
        return jnp.concatenate(
            [jnp.concatenate([array[:, :LANES], zero], axis=1), jnp.concatenate([zero, array[:, LANES:]], axis=1)],
            axis=0,
        )

    b_diag = diagonal(b_all)
    scores = dot(c_all, b_diag, NT)
    a_all = dot(part, a_ref[...])
    dt_all = dot(part, dt_ref[...])
    score_grads = [None, None]
    states, rstates, state_cat, rstate_cat = [], [], [], []
    for j in range(heads_j):
        state = s_ref[0, j].astype(F32) + from_ref[0, j : j + 1, :] * enter_ref[j]
        rstate = r_ref[0, j].astype(F32) + to_ref[0, j : j + 1, :] * leave_ref[j]
        states.append(fold(state * rstate))
        state = state.astype(BF16)
        rstate = rstate.astype(BF16)
        state_cat.append(jnp.concatenate([jnp.where(low, state, zero), jnp.where(low, zero, state)], axis=0))
        rstate_cat.append(jnp.concatenate([jnp.where(low, rstate, zero), jnp.where(low, zero, rstate)], axis=0))
    state_cat = jnp.concatenate(state_cat, axis=1)
    rstate_cat = jnp.concatenate(rstate_cat, axis=1)
    carried_all = dot(c_all, state_cat)
    back_all = dot(b_all, rstate_cat)
    out_rows, leads, tails = [], [], []
    for j in range(heads_j):
        lanes = slice(j * LANES, (j + 1) * LANES)
        a_b = a_all[:, lanes]
        dt_b = dt_all[:, lanes]
        a_last = a_b[span - 1 : span]
        e_b = jnp.exp2(a_b)
        f_b = jnp.exp2(a_last - a_b)
        e_last = e_b[span - 1 : span]
        heads_b = dot(part, heads_ref[:, 2 * j * LANES : 2 * (j + 1) * LANES])
        u = u_ref[j].astype(F32)
        dy16 = grads[j]
        dy = dy16.astype(F32)
        val16 = (u * dt_b).astype(BF16)
        val = val16.astype(F32)
        tails.append((val * f_b).astype(BF16))
        leads.append((dy * e_b).astype(BF16))
        dy_two = jnp.concatenate([jnp.where(low, dy16, zero), jnp.where(low, zero, dy16)], axis=0)
        val_two = jnp.concatenate([jnp.where(low, val16, zero), jnp.where(low, zero, val16)], axis=0)
        products = dot(dy16, val_two, NT)
        mixes = []
        for g in range(2):
            at = j * groups + head0 + g
            inside = slice(g * LANES, (g + 1) * LANES)
            spread = heads_b[:, inside] - row_ref[at : at + 1, :]
            decay = jnp.exp2(jnp.where(causal, spread, -jnp.inf))
            mixes.append((scores[:, inside] * decay).astype(BF16))
            weighted = decay * products[:, inside]
            score_grads[g] = weighted if score_grads[g] is None else score_grads[g] + weighted
        inner = dot(jnp.concatenate(mixes, axis=1), val_two)
        dval = dot(jnp.concatenate(mixes, axis=0), dy_two, TN)
        carried = carried_all[:, lanes] * e_b
        back = back_all[:, lanes] * f_b
        out = inner + carried
        dval_full = dval + back
        log_part = a_b * (dy * out - val * dval_full) + a_last * (val * back)
        acc[4, j] = acc[4, j] + fold(log_part) + states[j] * (a_last * e_last)
        skip = skips[j : j + 1, :]
        out_rows.append((out + skip * u).astype(BF16))
        dv_buf[j, 0:span, :] = (dt_b * dval_full + skip * dy) * slope_ref[j].astype(F32)
    mixed_ref[...] = jnp.swapaxes(jnp.stack(out_rows, axis=0), 0, 1)
    dc_inter = dot(jnp.concatenate(leads, axis=1), state_cat, NT)
    db_inter = dot(jnp.concatenate(tails, axis=1), rstate_cat, NT)
    dx_rows = []
    for j in range(heads_j):
        x = xs[j].astype(F32)
        total = None
        for tap in range(4):
            shifted = dv_buf[j, 3 - tap : 3 - tap + span, :]
            piece = weights[tap, j : j + 1, :] * shifted
            total = piece if total is None else total + piece
            acc[tap, j] = acc[tap, j] + fold(shifted * x)
        dx_rows.append(total.astype(BF16))
    dx_ref[...] = jnp.swapaxes(jnp.stack(dx_rows, axis=0), 0, 1)
    flows = [flow.astype(BF16) for flow in score_grads]
    dc = (dot(jnp.concatenate(flows, axis=1), b_diag) + dc_inter).astype(BF16)
    db = (dot(jnp.concatenate(flows, axis=0), diagonal(c_all), TN) + db_inter).astype(BF16)

    @pl.when(core_ref[0] == 0)
    def _():
        keep_ref[...] = db
        send_ref[...] = dc

    @pl.when(core_ref[0] != 0)
    def _():
        keep_ref[...] = dc
        send_ref[...] = db

    @pl.when(step == pl.num_programs(0) - 1)
    def _():
        edge_ref[...] = dv_buf[:, 0:EDGE, :]
        for tap in range(5):
            for j in range(heads_j):
                sums_ref[tap, j : j + 1, :] = jnp.sum(acc[tap, j], axis=0, keepdims=True)


def place_kernel(core_ref, mine_ref, got_ref, *rest):
    write_ref, read_ref = rest[-2:]

    @pl.when(core_ref[0] == 0)
    def _():
        write_ref[...] = mine_ref[...]
        read_ref[...] = got_ref[...]

    @pl.when(core_ref[0] != 0)
    def _():
        write_ref[...] = got_ref[...]
        read_ref[...] = mine_ref[...]


def edge_kernel(after_ref, w_ref, dx_ref, out_ref):
    rows = dx_ref.shape[0]
    weights = w_ref[...]
    after = after_ref[...]
    out_ref[: rows - 3] = dx_ref[: rows - 3]
    for row in range(3):
        fix = weights[0] * after[row]
        for tap in range(1, row + 1):
            fix = fix + weights[tap] * after[row - tap]
        at = rows - 3 + row
        out_ref[at] = (dx_ref[at].astype(F32) + fix).astype(BF16)


def halves_of(ref):
    decay = ref[0, :, LANES, :].astype(F32) + ref[0, :, LANES + 1, :].astype(F32)
    return ref[0, :, :LANES, :].astype(F32), ref[1, :, :LANES, :].astype(F32), decay


def combine_kernel(first, last, bits_ref, mine_ref, got_ref, *refs):
    if not first:
        enter_ref, leave_ref, reach_ref = refs[:3]
    send_ref, enter_out, leave_out, reach_out = refs[-4:]

    def write(forward, backward, decay):
        if last:

            @pl.when(bits_ref[1] == 1)
            def _():
                send_ref[...] = backward.astype(BF16)

            @pl.when(bits_ref[1] == 0)
            def _():
                send_ref[...] = forward.astype(BF16)
        else:
            high = decay.astype(BF16).astype(F32)
            send_ref[0, :, :LANES, :] = forward.astype(BF16)
            send_ref[1, :, :LANES, :] = backward.astype(BF16)
            zeros = jnp.zeros((6, LANES), F32)
            for j in range(decay.shape[0]):
                rows = jnp.concatenate([high[j : j + 1], decay[j : j + 1] - high[j : j + 1], zeros], axis=0)
                send_ref[0, j, LANES:, :] = rows.astype(BF16)
                send_ref[1, j, LANES:, :] = rows.astype(BF16)

    own_f, own_b, own_d = halves_of(mine_ref)
    got_f, got_b, got_d = halves_of(got_ref)
    wide, got_wide = own_d[:, None, :], got_d[:, None, :]

    @pl.when(bits_ref[0] == 1)
    def _():
        if first:
            enter_out[...] = got_f
            leave_out[...] = jnp.zeros_like(got_b)
            reach_out[0] = got_d
            reach_out[1] = jnp.ones_like(got_d)
        else:
            enter_out[...] = enter_ref[...] + reach_ref[0][:, None, :] * got_f
            leave_out[...] = leave_ref[...]
            reach_out[0] = reach_ref[0] * got_d
            reach_out[1] = reach_ref[1]
        write(own_f + wide * got_f, got_b + got_wide * own_b, own_d * got_d)

    @pl.when(bits_ref[0] == 0)
    def _():
        if first:
            enter_out[...] = jnp.zeros_like(got_f)
            leave_out[...] = got_b
            reach_out[0] = jnp.ones_like(got_d)
            reach_out[1] = got_d
        else:
            enter_out[...] = enter_ref[...]
            leave_out[...] = leave_ref[...] + reach_ref[1][:, None, :] * got_b
            reach_out[0] = reach_ref[0]
            reach_out[1] = reach_ref[1] * got_d
        write(got_f + got_wide * own_f, own_b + wide * got_b, own_d * got_d)


class Exchange:
    def __init__(self, total):
        self.count = lax.axis_size("seq")
        self.sent = total
        self.shape = (total.shape[1], LANES, LANES)
        self.distance = 1
        self.known = ()
        self.got = None

    def bit(self, distance):
        return (lax.axis_index("seq") // distance % 2).astype(jnp.int32)

    def swap(self):
        self.got = lax.ppermute(self.sent, "seq", [(i, i ^ self.distance) for i in range(self.count)])

    def finished(self):
        return 2 * self.distance >= self.count

    def combine(self):
        bits = jnp.stack([self.bit(self.distance), self.bit(2 * self.distance)])
        last = 4 * self.distance >= self.count
        operands = (self.sent, self.got, *self.known)
        send = self.shape if last else self.sent.shape
        self.sent, *self.known = pl.pallas_call(
            functools.partial(combine_kernel, not self.known, last),
            in_specs=[pl.BlockSpec(memory_space=pltpu.SMEM)] + [pl.BlockSpec(memory_space=pltpu.VMEM)] * len(operands),
            out_specs=[pl.BlockSpec(memory_space=pltpu.VMEM)] * 4,
            out_shape=[
                jax.ShapeDtypeStruct(send, BF16),
                jax.ShapeDtypeStruct(self.shape, F32),
                jax.ShapeDtypeStruct(self.shape, F32),
                jax.ShapeDtypeStruct((2, self.shape[0], LANES), F32),
            ],
            cost_estimate=cost(1),
            name="combine",
        )(bits, *operands)
        self.distance *= 2


def behind(value, *others):
    return lax.optimization_barrier((value, *others))[0]


def passed_along(block, axis, distance):
    devices = range(lax.axis_size(axis))
    route = [(i - distance, i) for i in devices if i - distance in devices]
    return lax.ppermute(block, axis, route)


def swap_sum(value, axis):
    count = lax.axis_size(axis)
    distance = 1
    while distance < count:
        value = value + lax.ppermute(value, axis, [(i, i ^ distance) for i in range(count)])
        distance *= 2
    return value


def on_device(x, taps, step_size, decay_log, write_in, read_in, skip_gain, out_grad):
    count, heads_j, width = x.shape
    groups = decay_log.shape[1]
    pairs = groups // 2
    spans = count // SPAN
    heads = 2 * heads_j
    rim = taps.shape[0] - 1
    n_head = lax.axis_size("head")
    n_seq = lax.axis_size("seq")
    core = jnp.stack([lax.axis_index("head") % 2, lax.axis_index("seq") // (n_seq // 2) % 2]).astype(jnp.int32)
    halo = passed_along(x[count - rim :], "seq", 1)
    per = 4 if spans % 4 == 0 else 1
    gather = jnp.asarray(gather_matrix(heads_j, groups), BF16)
    parts, rows = pl.pallas_call(
        scales_kernel,
        grid=(spans // per,),
        in_specs=[
            pl.BlockSpec((per * SPAN, heads_j, groups), lambda i: (i, 0, 0)),
            pl.BlockSpec((heads_j, groups), lambda i: (0, 0)),
            pl.BlockSpec(gather.shape, lambda i: (0, 0)),
        ],
        out_specs=[
            pl.BlockSpec((pairs, per * SPAN, LANES), lambda i: (0, i, 0)),
            pl.BlockSpec((heads_j * groups, per * SPAN), lambda i: (0, i)),
        ],
        out_shape=[
            jax.ShapeDtypeStruct((pairs, count, LANES), BF16),
            jax.ShapeDtypeStruct((heads_j * groups, count), F32),
        ],
        cost_estimate=cost(7),
        name="scales",
    )(step_size, decay_log, gather)
    skips = jnp.broadcast_to(skip_gain[:, :, None], (heads_j, groups, HALF)).reshape(heads_j, width)
    a_m, dt_m, e_m, df_m = (jnp.asarray(spread_matrix(q, heads_j), BF16) for q in (0, 1, 2, 4))
    heads_m = jnp.asarray(head_matrix(heads_j), BF16)

    def fixed(array):
        return pl.BlockSpec(array.shape, lambda i: (0,) * array.ndim)

    per = 2 if spans % 2 == 0 else 1
    size = per * SPAN
    end = spans // per - 1
    values, slopes, s_all, r_all, froms, tos = [], [], [], [], [], []
    exchanges = []

    def advance(*after):
        waits = list(after)
        for e in exchanges:
            if e.got is not None and not e.finished():
                e.combine()
                waits.append(e.sent)
                e.got = None
        for e in exchanges:
            if e.got is None:
                e.swap()
        return waits

    waits = [parts]
    for p in range(pairs):
        u, slope, s_loc, r_loc, from_start, to_end, total = pl.pallas_call(
            states_kernel,
            grid=(spans // per,),
            in_specs=[
                pl.BlockSpec((size, heads_j, LANES), lambda i, p=p: (i, 0, p)),
                pl.BlockSpec((rim, heads_j, LANES), lambda i, p=p: (0, 0, p)),
                pl.BlockSpec((4, heads_j, LANES), lambda i, p=p: (0, 0, p)),
                pl.BlockSpec((size, 2 * LANES), lambda i, p=p: (i, p)),
                pl.BlockSpec((1, size, LANES), lambda i, p=p: (p, i, 0)),
                pl.BlockSpec((size, heads_j, LANES), lambda i, p=p: (end - i, 0, p)),
                pl.BlockSpec((size, 2 * LANES), lambda i, p=p: (end - i, p)),
                pl.BlockSpec((1, size, LANES), lambda i, p=p: (p, end - i, 0)),
                fixed(e_m), fixed(df_m),
            ],
            out_specs=[
                pl.BlockSpec((heads_j, size, LANES), lambda i: (0, i, 0)),
                pl.BlockSpec((heads_j, size, LANES), lambda i: (0, i, 0)),
                pl.BlockSpec((per, heads_j, LANES, LANES), lambda i: (i, 0, 0, 0)),
                pl.BlockSpec((per, heads_j, LANES, LANES), lambda i: (end - i, 0, 0, 0)),
                pl.BlockSpec((per, heads_j, LANES), lambda i: (i, 0, 0)),
                pl.BlockSpec((per, heads_j, LANES), lambda i: (end - i, 0, 0)),
                pl.BlockSpec((2, heads_j, LANES + EDGE, LANES), lambda i: (0, 0, 0, 0)),
            ],
            out_shape=[
                jax.ShapeDtypeStruct((heads_j, count, LANES), BF16),
                jax.ShapeDtypeStruct((heads_j, count, LANES), BF16),
                jax.ShapeDtypeStruct((spans, heads_j, LANES, LANES), BF16),
                jax.ShapeDtypeStruct((spans, heads_j, LANES, LANES), BF16),
                jax.ShapeDtypeStruct((spans, heads_j, LANES), F32),
                jax.ShapeDtypeStruct((spans, heads_j, LANES), F32),
                jax.ShapeDtypeStruct((2, heads_j, LANES + EDGE, LANES), BF16),
            ],
            scratch_shapes=[
                pltpu.VMEM((heads_j, size + EDGE, LANES), F32),
                pltpu.VMEM((heads_j, LANES, LANES), F32),
                pltpu.VMEM((heads_j, LANES, LANES), F32),
                pltpu.VMEM((heads_j, LANES), F32),
                pltpu.VMEM((heads_j, LANES), F32),
            ],
            cost_estimate=cost(9),
            name=f"states{p}",
        )(x, halo, behind(taps, *waits), write_in, parts, out_grad, read_in, parts, e_m, df_m)
        waits = advance(s_loc)
        exchanges.append(Exchange(total))
        exchanges[-1].swap()
        values.append(u)
        slopes.append(slope)
        s_all.append(s_loc)
        r_all.append(r_loc)
        froms.append(from_start)
        tos.append(to_end)

    last = spans - 1
    mixed = dx = write_grad = read_grad = None
    sums, edges, arrived = [], [], []
    smem = pl.BlockSpec(memory_space=pltpu.SMEM)
    anywhere = pl.BlockSpec(memory_space=pl.ANY)
    for p in range(pairs):
        near_in, near_out, reach = exchanges[p].known
        far = exchanges[p].got
        operands = [core, x, values[p], slopes[p], out_grad, write_in, read_in, parts, rows, s_all[p], r_all[p],
                    near_in, near_out, reach, far, froms[p], tos[p], behind(taps, *waits), skips, heads_m, a_m, dt_m]
        time3 = pl.BlockSpec((SPAN, heads_j, LANES), lambda i, p=p: (last - i, 0, p))
        time2 = pl.BlockSpec((SPAN, 2 * LANES), lambda i, p=p: (last - i, p))
        own3 = pl.BlockSpec((heads_j, SPAN, LANES), lambda i: (0, last - i, 0))
        own2 = pl.BlockSpec((SPAN, 2 * LANES), lambda i: (last - i, 0))
        state = pl.BlockSpec((1, heads_j, LANES, LANES), lambda i: (last - i, 0, 0, 0))
        lane_row = pl.BlockSpec((1, heads_j, LANES), lambda i: (last - i, 0, 0))
        in_specs = [
            smem, time3, own3, own3, time3, time2, time2,
            pl.BlockSpec((1, SPAN, LANES), lambda i, p=p: (p, last - i, 0)),
            pl.BlockSpec((heads_j * groups, SPAN), lambda i: (0, last - i)),
            state, state, fixed(near_in), fixed(near_out), fixed(reach), fixed(far), lane_row, lane_row,
            pl.BlockSpec((4, heads_j, LANES), lambda i, p=p: (0, 0, p)),
            pl.BlockSpec((heads_j, LANES), lambda i, p=p: (0, p)),
            fixed(heads_m), fixed(a_m), fixed(dt_m),
        ]
        aliases = {}
        if p > 0:
            aliases = {len(operands): 0, len(operands) + 1: 1}
            operands += [mixed, dx]
            in_specs += [anywhere] * 2
        mixed, dx, keep, send, total, edge = pl.pallas_call(
            functools.partial(main_kernel, 2 * p),
            grid=(spans,),
            in_specs=in_specs,
            out_specs=[
                time3, time3, own2, own2,
                pl.BlockSpec((5, heads_j, LANES), lambda i: (0, 0, 0)),
                pl.BlockSpec((heads_j, EDGE, LANES), lambda i: (0, 0, 0)),
            ],
            out_shape=[
                jax.ShapeDtypeStruct(x.shape, BF16),
                jax.ShapeDtypeStruct(x.shape, BF16),
                jax.ShapeDtypeStruct((count, 2 * LANES), BF16),
                jax.ShapeDtypeStruct((count, 2 * LANES), BF16),
                jax.ShapeDtypeStruct((5, heads_j, LANES), F32),
                jax.ShapeDtypeStruct((heads_j, EDGE, LANES), F32),
            ],
            scratch_shapes=[
                pltpu.VMEM((heads_j, SPAN + EDGE, LANES), F32),
                pltpu.VMEM((5, heads_j, EDGE, LANES), F32),
                pltpu.VMEM((heads_j, LANES, LANES), F32),
                pltpu.VMEM((heads_j, LANES, LANES), F32),
            ],
            input_output_aliases=aliases,
            cost_estimate=cost(20),
            name=f"main{p}",
        )(*operands)
        sums.append(total)
        edges.append(edge)
        cores = [(i, i ^ 1) for i in range(n_head)]
        send = behind(send, *advance(), *arrived)
        mine = keep + lax.ppermute(send, "head", cores)
        waits = [mine]
        arrived = []
        distance = 2
        while distance < n_head:
            mine = mine + lax.ppermute(mine, "head", [(i, i ^ distance) for i in range(n_head)])
            distance *= 2
        arrived.append(mine)
        got = lax.ppermute(mine, "head", cores)
        operands, in_specs, aliases = [core, mine, got], None, {}
        big = per * 3 * SPAN if spans % (per * 3) == 0 else SPAN
        block = pl.BlockSpec((big, 2 * LANES), lambda i: (i, 0))
        in_specs = [smem, block, block]
        if p > 0:
            operands += [write_grad, read_grad]
            in_specs += [anywhere] * 2
            aliases = {3: 0, 4: 1}
        write_grad, read_grad = pl.pallas_call(
            place_kernel,
            grid=(count // big,),
            in_specs=in_specs,
            out_specs=[pl.BlockSpec((big, 2 * LANES), lambda i, p=p: (i, p))] * 2,
            out_shape=[jax.ShapeDtypeStruct((count, groups * LANES), BF16)] * 2,
            input_output_aliases=aliases,
            cost_estimate=cost(2),
            name=f"place{p}",
        )(*operands)

    edge = jnp.transpose(jnp.concatenate(edges, axis=-1)[:, :rim, :], (1, 0, 2))
    after = passed_along(edge, "seq", -1)
    tail_spec = pl.BlockSpec((EDGE, heads_j, width), lambda i: (count // EDGE - 1, 0, 0))
    dx = pl.pallas_call(
        edge_kernel,
        grid=(1,),
        in_specs=[fixed(after), fixed(taps), tail_spec],
        out_specs=tail_spec,
        out_shape=jax.ShapeDtypeStruct(x.shape, BF16),
        input_output_aliases={2: 0},
        name="edge",
    )(after, taps, dx)
    before = halo.astype(F32)
    sums = jnp.concatenate(sums, axis=-1)
    extra = []
    for tap in range(5):
        piece = jnp.zeros_like(sums[0])
        for row in range(rim - tap):
            piece = piece + edge[row] * before[row + tap]
        extra.append(piece)
    sums = swap_sum(sums + jnp.stack(extra), "seq")
    conv_grad = sums[:4]
    decay_grad = LN2 * sums[4].reshape(heads_j, groups, HALF).sum(-1)
    return (mixed, dx, conv_grad, decay_grad, write_grad, read_grad)


def solution(mesh):
    return jax.shard_map(
        on_device,
        mesh=mesh,
        in_specs=(
            P("seq", "head", None),
            P(None, "head", None),
            P("seq", "head", None),
            P("head", None),
            P("seq", None),
            P("seq", None),
            P("head", None),
            P("seq", "head", None),
        ),
        out_specs=(
            P("seq", "head", None),
            P("seq", "head", None),
            P(None, "head", None),
            P("head", None),
            P("seq", None),
            P("seq", None),
        ),
        check_vma=False,
    )
```

```python
import functools

import jax
import jax.numpy as jnp
import numpy as np
from jax import lax
from jax.experimental import pallas as pl
from jax.experimental.pallas import tpu as pltpu
from jax.sharding import PartitionSpec as P

SPAN = 128
LANES = 128
HALF = 64
EDGE = 8
F32 = jnp.float32
BF16 = jnp.bfloat16
NT = (((1,), (1,)), ((), ()))
TN = (((0,), (0,)), ((), ()))
LOG2E = 1.4426950408889634
LN2 = 0.6931471805599453
PARTS = (3, 2, 2, 2)


def cost(microseconds):
    return pl.CostEstimate(flops=int(microseconds * 1.15e9), transcendentals=0, bytes_accessed=0)


def dot(a, b, dims=None):
    if dims is None:
        return jnp.dot(a, b, preferred_element_type=F32)
    return lax.dot_general(a, b, dims, preferred_element_type=F32)


def low_half(rows):
    return lax.broadcasted_iota(jnp.int32, (rows, LANES), 1) < HALF


def split_parts(value, count):
    parts = []
    for _ in range(count - 1):
        part = value.astype(BF16)
        parts.append(part)
        value = value - part.astype(F32)
    parts.append(value.astype(BF16))
    return parts


def part_lane(quantity, part, head, heads):
    return (sum(PARTS[:quantity]) + part) * heads + head


def gather_matrix(heads_j, groups):
    heads, pairs, count = 2 * heads_j, groups // 2, sum(PARTS)
    matrix = np.zeros((count * heads_j * groups, pairs * LANES), np.float32)
    for part in range(count):
        for j in range(heads_j):
            for g in range(groups):
                matrix[part * heads_j * groups + j * groups + g, (g // 2) * LANES + part * heads + 2 * j + g % 2] = 1.0
    return matrix


def spread_matrix(quantity, heads_j):
    heads = 2 * heads_j
    matrix = np.zeros((LANES, heads_j * LANES), np.float32)
    for part in range(PARTS[quantity]):
        for h in range(heads):
            matrix[part_lane(quantity, part, h, heads), h * HALF : (h + 1) * HALF] = 1.0
    return matrix


def head_matrix(heads_j):
    heads = 2 * heads_j
    matrix = np.zeros((LANES, heads * LANES), np.float32)
    for part in range(PARTS[0]):
        for h in range(heads):
            matrix[part_lane(0, part, h, heads), h * LANES : (h + 1) * LANES] = 1.0
    return matrix


def scales_kernel(dt_ref, log_ref, gather_ref, parts_ref, rows_ref):
    every, count = dt_ref.shape
    rates = -LOG2E * jnp.exp(log_ref[...])
    upper = (
        lax.broadcasted_iota(jnp.int32, (SPAN, SPAN), 0) <= lax.broadcasted_iota(jnp.int32, (SPAN, SPAN), 1)
    ).astype(BF16)
    for at in range(0, count, SPAN):
        dt = dt_ref[:, at : at + SPAN]
        summed = dot(jnp.concatenate(split_parts(dt * rates, 3), axis=0), upper)
        cumul = summed[:every] + summed[every : 2 * every] + summed[2 * every :]
        tail = jnp.exp2(cumul[:, SPAN - 1 : SPAN] - cumul)
        parts = []
        for value, number in zip((cumul, dt, jnp.exp2(cumul), dt * tail), PARTS, strict=True):
            parts += split_parts(value, number)
        placed = dot(jnp.concatenate(parts, axis=0), gather_ref[...], TN).astype(BF16)
        for p in range(parts_ref.shape[0]):
            parts_ref[p, at : at + SPAN, :] = placed[:, p * LANES : (p + 1) * LANES]
        rows_ref[at // SPAN] = cumul


def states_kernel(
    x_ref, halo_ref, w_ref, b_ref, partf_ref, y_ref, c_ref, partr_ref, lead_ref, tail_ref,
    u_ref, slope_ref, s_ref, r_ref, from_ref, to_ref, total_ref, x_buf, s_acc, r_acc, f_acc, t_acc,
):
    step = pl.program_id(0)
    rows, heads_j, _ = x_ref.shape
    low = low_half(SPAN)

    @pl.when(step == 0)
    def _():
        s_acc[...] = jnp.zeros_like(s_acc)
        r_acc[...] = jnp.zeros_like(r_acc)
        f_acc[...] = jnp.ones_like(f_acc)
        t_acc[...] = jnp.ones_like(t_acc)
        halo = halo_ref[...].astype(F32)
        for j in range(heads_j):
            for row in range(3):
                x_buf[j, EDGE - 3 + row : EDGE - 2 + row, :] = halo[row, j : j + 1, :]

    @pl.when(step > 0)
    def _():
        x_buf[:, 0:EDGE, :] = x_buf[:, rows : rows + EDGE, :]

    x_buf[:, EDGE : EDGE + rows, :] = jnp.swapaxes(x_ref[...], 0, 1).astype(F32)
    weights = w_ref[...]
    number = rows // SPAN
    def one(k):
        m = number - 1 - k
        start = k * SPAN
        here = pl.ds(start, SPAN)
        there = pl.ds(m * SPAN, SPAN)
        grads_all = jnp.swapaxes(y_ref[there], 0, 1)
        partf = partf_ref[0, here, :]
        tails = dot(partf, tail_ref[...])
        leads = dot(jnp.concatenate([partr_ref[0, there, :], partf[SPAN - EDGE :]], axis=0), lead_ref[...])
        s_ref[k] = s_acc[...].astype(BF16)
        r_ref[m] = r_acc[...].astype(BF16)
        from_ref[k] = f_acc[...]
        to_ref[m] = t_acc[...]
        wrote, read = [], []
        for j in range(heads_j):
            lanes = slice(j * LANES, (j + 1) * LANES)
            at = start + EDGE - 3
            v = 0.5 * weights[0, j : j + 1, :] * x_buf[j, at : at + SPAN, :]
            for tap in range(1, 4):
                v = v + 0.5 * weights[tap, j : j + 1, :] * x_buf[j, at + tap : at + tap + SPAN, :]
            gate = 1.0 + jnp.tanh(v)
            u = v * gate
            u_ref[j, k] = u.astype(BF16)
            slope_ref[j, k] = (gate + u * (2.0 - gate)).astype(BF16)
            wrote.append((u * tails[:, lanes]).astype(BF16))
            read.append((grads_all[j].astype(F32) * leads[:SPAN, lanes]).astype(BF16))
        own_s = dot(b_ref[here, :], jnp.concatenate(wrote, axis=1), TN)
        own_r = dot(c_ref[there, :], jnp.concatenate(read, axis=1), TN)
        for j in range(heads_j):
            lanes = slice(j * LANES, (j + 1) * LANES)
            keep = leads[SPAN + EDGE - 1 : SPAN + EDGE, lanes]
            s_acc[j] = keep * s_acc[j] + jnp.where(low, own_s[:LANES, lanes], own_s[LANES:, lanes])
            f_acc[j] = f_acc[j] * keep
            keep = leads[SPAN - 1 : SPAN, lanes]
            r_acc[j] = keep * r_acc[j] + jnp.where(low, own_r[:LANES, lanes], own_r[LANES:, lanes])
            t_acc[j] = t_acc[j] * keep

    for turn in range(number):
        one(turn)

    @pl.when(step == pl.num_programs(0) - 1)
    def _():
        total_ref[0, :, :LANES, :] = s_acc[...].astype(BF16)
        total_ref[1, :, :LANES, :] = r_acc[...].astype(BF16)
        for j in range(heads_j):
            decay = f_acc[j][0:1]
            high = decay.astype(BF16).astype(F32)
            pair = jnp.concatenate([high, decay - high, jnp.zeros((6, LANES), F32)], axis=0)
            total_ref[0, j, LANES:, :] = pair.astype(BF16)
            total_ref[1, j, LANES:, :] = pair.astype(BF16)


def fold(value):
    return jnp.sum(value.reshape(value.shape[0] // 8, 8, value.shape[1]), axis=0)


def main_kernel(
    head0, core_ref, x_ref, u_ref, slope_ref, y_ref, b_ref, c_ref, part_ref, row_ref, s_ref, r_ref,
    near_in, near_out, reach_ref, far_ref, from_ref, to_ref, w_ref, skip_ref, heads_ref, a_ref, dt_ref, *rest,
):
    mixed_ref, dx_ref, keep_ref, send_ref, sums_ref, edge_ref, dv_buf, acc, enter_ref, leave_ref = rest[-10:]
    step = pl.program_id(0)
    size, heads_j, _ = x_ref.shape
    span = SPAN
    number = size // span
    groups = row_ref.shape[1] // heads_j
    low = low_half(span)
    causal = lax.broadcasted_iota(jnp.int32, (span, span), 0) >= lax.broadcasted_iota(
        jnp.int32, (span, span), 1
    )

    @pl.when(step == 0)
    def _():
        acc[...] = jnp.zeros_like(acc)
        dv_buf[:, size : size + EDGE, :] = jnp.zeros((heads_j, EDGE, LANES), F32)
        far = far_ref[...].astype(F32)

        @pl.when(core_ref[1] == 1)
        def _():
            enter_ref[...] = near_in[...] + reach_ref[0][:, None, :] * far
            leave_ref[...] = near_out[...]

        @pl.when(core_ref[1] == 0)
        def _():
            enter_ref[...] = near_in[...]
            leave_ref[...] = near_out[...] + reach_ref[1][:, None, :] * far

    @pl.when(step > 0)
    def _():
        dv_buf[:, size : size + EDGE, :] = dv_buf[:, 0:EDGE, :]

    def one(turn):
        k = number - 1 - turn
        base = k * span
        here = pl.ds(base, span)
        xs = jnp.swapaxes(x_ref[here], 0, 1)
        grads = jnp.swapaxes(y_ref[here], 0, 1)
        b_all = b_ref[here, :]
        c_all = c_ref[here, :]
        weights = w_ref[...]
        skips = skip_ref[...]
        part = part_ref[0, here, :]
        zero = jnp.zeros((span, LANES), BF16)
        def diagonal(array):
            return jnp.concatenate(
                [jnp.concatenate([array[:, :LANES], zero], axis=1), jnp.concatenate([zero, array[:, LANES:]], axis=1)],
                axis=0,
            )

        b_diag = diagonal(b_all)
        scores = dot(c_all, b_diag, NT)
        a_all = dot(part, a_ref[...])
        dt_all = dot(part, dt_ref[...])
        score_grads = [None, None]
        logs = row_ref[k]
        states, rstates, state_cat, rstate_cat = [], [], [], []
        for j in range(heads_j):
            state = s_ref[k, j].astype(F32) + from_ref[k, j][0:1] * enter_ref[j]
            rstate = r_ref[k, j].astype(F32) + to_ref[k, j][0:1] * leave_ref[j]
            states.append(fold(state * rstate))
            state = state.astype(BF16)
            rstate = rstate.astype(BF16)
            state_cat.append(jnp.concatenate([jnp.where(low, state, zero), jnp.where(low, zero, state)], axis=0))
            rstate_cat.append(jnp.concatenate([jnp.where(low, rstate, zero), jnp.where(low, zero, rstate)], axis=0))
        state_cat = jnp.concatenate(state_cat, axis=1)
        rstate_cat = jnp.concatenate(rstate_cat, axis=1)
        carried_all = dot(c_all, state_cat)
        back_all = dot(b_all, rstate_cat)
        out_rows, leads, tails = [], [], []
        for j in range(heads_j):
            lanes = slice(j * LANES, (j + 1) * LANES)
            a_b = a_all[:, lanes]
            dt_b = dt_all[:, lanes]
            a_last = a_b[span - 1 : span]
            e_b = jnp.exp2(a_b)
            f_b = jnp.exp2(a_last - a_b)
            e_last = e_b[span - 1 : span]
            heads_b = dot(part, heads_ref[:, 2 * j * LANES : 2 * (j + 1) * LANES])
            u = u_ref[j, k].astype(F32)
            dy = grads[j].astype(F32)
            dy16 = dy.astype(BF16)
            val16 = (u * dt_b).astype(BF16)
            val = val16.astype(F32)
            tails.append((val * f_b).astype(BF16))
            leads.append((dy * e_b).astype(BF16))
            dy_two = jnp.concatenate([jnp.where(low, dy16, zero), jnp.where(low, zero, dy16)], axis=0)
            val_two = jnp.concatenate([jnp.where(low, val16, zero), jnp.where(low, zero, val16)], axis=0)
            products = dot(dy16, val_two, NT)
            mixes = []
            for g in range(2):
                at = j * groups + head0 + g
                inside = slice(g * LANES, (g + 1) * LANES)
                spread = heads_b[:, inside] - logs[at : at + 1]
                decay = jnp.exp2(jnp.where(causal, spread, -jnp.inf))
                mixes.append((scores[:, inside] * decay).astype(BF16))
                weighted = decay * products[:, inside]
                score_grads[g] = weighted if score_grads[g] is None else score_grads[g] + weighted
            inner = dot(jnp.concatenate(mixes, axis=1), val_two)
            dval = dot(jnp.concatenate(mixes, axis=0), dy_two, TN)
            carried = carried_all[:, lanes] * e_b
            back = back_all[:, lanes] * f_b
            out = inner + carried
            dval_full = dval + back
            log_part = a_b * (dy * out - val * dval_full) + a_last * (val * back)
            acc[4, j] = acc[4, j] + fold(log_part) + states[j] * (a_last * e_last)
            skip = skips[j : j + 1, :]
            out_rows.append((out + skip * u).astype(BF16))
            dv_buf[j, here, :] = (dt_b * dval_full + skip * dy) * (0.5 * slope_ref[j, k].astype(F32))
        mixed_ref[here] = jnp.swapaxes(jnp.stack(out_rows, axis=0), 0, 1)
        dc_inter = dot(jnp.concatenate(leads, axis=1), state_cat, NT)
        db_inter = dot(jnp.concatenate(tails, axis=1), rstate_cat, NT)
        dx_rows = []
        for j in range(heads_j):
            x = xs[j].astype(F32)
            at = base + 3
            total = None
            for tap in range(4):
                shifted = dv_buf[j, at - tap : at - tap + span, :]
                piece = weights[tap, j : j + 1, :] * shifted
                total = piece if total is None else total + piece
                acc[tap, j] = acc[tap, j] + fold(shifted * x)
            dx_rows.append(total.astype(BF16))
        dx_ref[here] = jnp.swapaxes(jnp.stack(dx_rows, axis=0), 0, 1)
        flows = [flow.astype(BF16) for flow in score_grads]
        dc = (dot(jnp.concatenate(flows, axis=1), b_diag) + dc_inter).astype(BF16)
        db = (dot(jnp.concatenate(flows, axis=0), diagonal(c_all), TN) + db_inter).astype(BF16)

        @pl.when(core_ref[0] == 0)
        def _():
            keep_ref[here, :] = db
            send_ref[here, :] = dc

        @pl.when(core_ref[0] != 0)
        def _():
            keep_ref[here, :] = dc
            send_ref[here, :] = db

    for turn in range(number):
        one(turn)

    @pl.when(step == pl.num_programs(0) - 1)
    def _():
        edge_ref[...] = dv_buf[:, 0:EDGE, :]
        for tap in range(5):
            for j in range(heads_j):
                sums_ref[tap, j : j + 1, :] = jnp.sum(acc[tap, j], axis=0, keepdims=True)


def place_kernel(core_ref, mine_ref, got_ref, *rest):
    write_ref, read_ref, token_ref = rest[-3:]
    token_ref[...] = jnp.zeros_like(token_ref)

    @pl.when(core_ref[0] == 0)
    def _():
        write_ref[...] = mine_ref[...]
        read_ref[...] = got_ref[...]

    @pl.when(core_ref[0] != 0)
    def _():
        write_ref[...] = got_ref[...]
        read_ref[...] = mine_ref[...]


def edge_kernel(after_ref, w_ref, dx_ref, out_ref):
    rows = dx_ref.shape[0]
    weights = w_ref[...]
    after = after_ref[...]
    out_ref[: rows - 3] = dx_ref[: rows - 3]
    for row in range(3):
        fix = weights[0] * after[row]
        for tap in range(1, row + 1):
            fix = fix + weights[tap] * after[row - tap]
        at = rows - 3 + row
        out_ref[at] = (dx_ref[at].astype(F32) + fix).astype(BF16)


def halves_of(ref):
    decay = ref[0, :, LANES, :].astype(F32) + ref[0, :, LANES + 1, :].astype(F32)
    return ref[0, :, :LANES, :].astype(F32), ref[1, :, :LANES, :].astype(F32), decay


def combine_kernel(first, last, bits_ref, mine_ref, got_ref, *refs):
    if not first:
        enter_ref, leave_ref, reach_ref = refs[:3]
    send_ref, enter_out, leave_out, reach_out = refs[-4:]

    def write(forward, backward, decay):
        if last:

            @pl.when(bits_ref[1] == 1)
            def _():
                send_ref[...] = backward.astype(BF16)

            @pl.when(bits_ref[1] == 0)
            def _():
                send_ref[...] = forward.astype(BF16)
        else:
            high = decay.astype(BF16).astype(F32)
            send_ref[0, :, :LANES, :] = forward.astype(BF16)
            send_ref[1, :, :LANES, :] = backward.astype(BF16)
            zeros = jnp.zeros((6, LANES), F32)
            for j in range(decay.shape[0]):
                rows = jnp.concatenate([high[j : j + 1], decay[j : j + 1] - high[j : j + 1], zeros], axis=0)
                send_ref[0, j, LANES:, :] = rows.astype(BF16)
                send_ref[1, j, LANES:, :] = rows.astype(BF16)

    own_f, own_b, own_d = halves_of(mine_ref)
    got_f, got_b, got_d = halves_of(got_ref)
    wide, got_wide = own_d[:, None, :], got_d[:, None, :]

    @pl.when(bits_ref[0] == 1)
    def _():
        if first:
            enter_out[...] = got_f
            leave_out[...] = jnp.zeros_like(got_b)
            reach_out[0] = got_d
            reach_out[1] = jnp.ones_like(got_d)
        else:
            enter_out[...] = enter_ref[...] + reach_ref[0][:, None, :] * got_f
            leave_out[...] = leave_ref[...]
            reach_out[0] = reach_ref[0] * got_d
            reach_out[1] = reach_ref[1]
        write(own_f + wide * got_f, got_b + got_wide * own_b, own_d * got_d)

    @pl.when(bits_ref[0] == 0)
    def _():
        if first:
            enter_out[...] = jnp.zeros_like(got_f)
            leave_out[...] = got_b
            reach_out[0] = jnp.ones_like(got_d)
            reach_out[1] = got_d
        else:
            enter_out[...] = enter_ref[...]
            leave_out[...] = leave_ref[...] + reach_ref[1][:, None, :] * got_b
            reach_out[0] = reach_ref[0]
            reach_out[1] = reach_ref[1] * got_d
        write(got_f + got_wide * own_f, own_b + wide * got_b, own_d * got_d)


class Exchange:
    def __init__(self, total):
        self.count = lax.axis_size("seq")
        self.sent = total
        self.shape = (total.shape[1], LANES, LANES)
        self.distance = 1
        self.known = ()
        self.got = None
        self.held = False

    def bit(self, distance):
        return (lax.axis_index("seq") // distance % 2).astype(jnp.int32)

    def swap(self):
        self.got = lax.ppermute(self.sent, "seq", [(i, i ^ self.distance) for i in range(self.count)])

    def finished(self):
        return 2 * self.distance >= self.count

    def combine(self, *after):
        bits = jnp.stack([self.bit(self.distance), self.bit(2 * self.distance)])
        last = 4 * self.distance >= self.count
        operands = (self.sent, self.got, *self.known)
        send = self.shape if last else self.sent.shape
        self.sent, *self.known = pl.pallas_call(
            functools.partial(combine_kernel, not self.known, last),
            in_specs=[pl.BlockSpec(memory_space=pltpu.SMEM)] + [pl.BlockSpec(memory_space=pltpu.VMEM)] * len(operands)
            + [pl.BlockSpec(memory_space=pl.ANY)] * len(after),
            out_specs=[pl.BlockSpec(memory_space=pltpu.VMEM)] * 4,
            out_shape=[
                jax.ShapeDtypeStruct(send, BF16),
                jax.ShapeDtypeStruct(self.shape, F32),
                jax.ShapeDtypeStruct(self.shape, F32),
                jax.ShapeDtypeStruct((2, self.shape[0], LANES), F32),
            ],
            cost_estimate=cost(1),
            name="combine",
        )(bits, *operands, *after)
        self.distance *= 2


def passed_along(block, axis, distance):
    devices = range(lax.axis_size(axis))
    route = [(i - distance, i) for i in devices if i - distance in devices]
    return lax.ppermute(block, axis, route)


def swap_sum(value, axis):
    count = lax.axis_size(axis)
    distance = 1
    while distance < count:
        value = value + lax.ppermute(value, axis, [(i, i ^ distance) for i in range(count)])
        distance *= 2
    return value


STATES_SPANS = 3
MAIN_SPANS = 1


def at_most(limit, spans):
    return max(n for n in range(1, limit + 1) if spans % n == 0)


def fixed(array):
    return pl.BlockSpec(array.shape, lambda i: (0,) * array.ndim)


def states_call(p, waits, x, halo, taps, write_in, parts, out_grad, read_in, e_m, df_m):
    count, heads_j, _ = x.shape
    spans = count // SPAN
    per = at_most(STATES_SPANS, spans)
    size = per * SPAN
    end = spans // per - 1
    def kernel(*refs):
        states_kernel(*refs[:10], *refs[10 + len(waits) :])

    return pl.pallas_call(
        kernel,
        grid=(spans // per,),
        in_specs=[
            pl.BlockSpec((size, heads_j, LANES), lambda i: (i, 0, p)),
            pl.BlockSpec((halo.shape[0], heads_j, LANES), lambda i: (0, 0, p)),
            pl.BlockSpec((4, heads_j, LANES), lambda i: (0, 0, p)),
            pl.BlockSpec((size, 2 * LANES), lambda i: (i, p)),
            pl.BlockSpec((1, size, LANES), lambda i: (p, i, 0)),
            pl.BlockSpec((size, heads_j, LANES), lambda i: (end - i, 0, p)),
            pl.BlockSpec((size, 2 * LANES), lambda i: (end - i, p)),
            pl.BlockSpec((1, size, LANES), lambda i: (p, end - i, 0)),
            fixed(e_m), fixed(df_m),
        ] + [pl.BlockSpec(memory_space=pl.ANY)] * len(waits),
        out_specs=[
            pl.BlockSpec((heads_j, per, SPAN, LANES), lambda i: (0, i, 0, 0)),
            pl.BlockSpec((heads_j, per, SPAN, LANES), lambda i: (0, i, 0, 0)),
            pl.BlockSpec((per, heads_j, LANES, LANES), lambda i: (i, 0, 0, 0)),
            pl.BlockSpec((per, heads_j, LANES, LANES), lambda i: (end - i, 0, 0, 0)),
            pl.BlockSpec((per, heads_j, EDGE, LANES), lambda i: (i, 0, 0, 0)),
            pl.BlockSpec((per, heads_j, EDGE, LANES), lambda i: (end - i, 0, 0, 0)),
            pl.BlockSpec((2, heads_j, LANES + EDGE, LANES), lambda i: (0, 0, 0, 0)),
        ],
        out_shape=[
            jax.ShapeDtypeStruct((heads_j, spans, SPAN, LANES), BF16),
            jax.ShapeDtypeStruct((heads_j, spans, SPAN, LANES), BF16),
            jax.ShapeDtypeStruct((spans, heads_j, LANES, LANES), BF16),
            jax.ShapeDtypeStruct((spans, heads_j, LANES, LANES), BF16),
            jax.ShapeDtypeStruct((spans, heads_j, EDGE, LANES), F32),
            jax.ShapeDtypeStruct((spans, heads_j, EDGE, LANES), F32),
            jax.ShapeDtypeStruct((2, heads_j, LANES + EDGE, LANES), BF16),
        ],
        scratch_shapes=[
            pltpu.VMEM((heads_j, size + EDGE, LANES), F32),
            pltpu.VMEM((heads_j, LANES, LANES), F32),
            pltpu.VMEM((heads_j, LANES, LANES), F32),
            pltpu.VMEM((heads_j, EDGE, LANES), F32),
            pltpu.VMEM((heads_j, EDGE, LANES), F32),
        ],
        cost_estimate=cost(9),
        name=f"states{p}",
    )(x, halo, taps, write_in, parts, out_grad, read_in, parts, e_m, df_m, *waits)


def main_call(
    p, waits, core, x, value, slope, out_grad, write_in, read_in, parts, rows, s_loc, r_loc, near_in,
    near_out, reach, far, from_start, to_end, taps, skips, heads_m, a_m, dt_m, mixed, dx,
):
    count, heads_j, _ = x.shape
    spans = count // SPAN
    per = at_most(MAIN_SPANS, spans)
    size = per * SPAN
    last = spans // per - 1
    operands = [core, x, value, slope, out_grad, write_in, read_in, parts, rows, s_loc, r_loc,
                near_in, near_out, reach, far, from_start, to_end, taps, skips, heads_m, a_m, dt_m, *waits]
    time3 = pl.BlockSpec((size, heads_j, LANES), lambda i: (last - i, 0, p))
    time2 = pl.BlockSpec((size, 2 * LANES), lambda i: (last - i, p))
    own3 = pl.BlockSpec((heads_j, per, SPAN, LANES), lambda i: (0, last - i, 0, 0))
    own2 = pl.BlockSpec((size, 2 * LANES), lambda i: (last - i, 0))
    state = pl.BlockSpec((per, heads_j, LANES, LANES), lambda i: (last - i, 0, 0, 0))
    lane_row = pl.BlockSpec((per, heads_j, EDGE, LANES), lambda i: (last - i, 0, 0, 0))
    in_specs = [
        pl.BlockSpec(memory_space=pltpu.SMEM), time3, own3, own3, time3, time2, time2,
        pl.BlockSpec((1, size, LANES), lambda i: (p, last - i, 0)),
        pl.BlockSpec((per, rows.shape[1], SPAN), lambda i: (last - i, 0, 0)),
        state, state, fixed(near_in), fixed(near_out), fixed(reach), fixed(far), lane_row, lane_row,
        pl.BlockSpec((4, heads_j, LANES), lambda i: (0, 0, p)),
        pl.BlockSpec((heads_j, LANES), lambda i: (0, p)),
        fixed(heads_m), fixed(a_m), fixed(dt_m),
    ] + [pl.BlockSpec(memory_space=pl.ANY)] * len(waits)
    aliases = {}
    if mixed is not None:
        aliases = {len(operands): 0, len(operands) + 1: 1}
        operands += [mixed, dx]
        in_specs += [pl.BlockSpec(memory_space=pl.ANY)] * 2
    return pl.pallas_call(
        functools.partial(main_kernel, 2 * p),
        grid=(spans // per,),
        in_specs=in_specs,
        out_specs=[
            time3, time3, own2, own2,
            pl.BlockSpec((5, heads_j, LANES), lambda i: (0, 0, 0)),
            pl.BlockSpec((heads_j, EDGE, LANES), lambda i: (0, 0, 0)),
        ],
        out_shape=[
            jax.ShapeDtypeStruct(x.shape, BF16),
            jax.ShapeDtypeStruct(x.shape, BF16),
            jax.ShapeDtypeStruct((count, 2 * LANES), BF16),
            jax.ShapeDtypeStruct((count, 2 * LANES), BF16),
            jax.ShapeDtypeStruct((5, heads_j, LANES), F32),
            jax.ShapeDtypeStruct((heads_j, EDGE, LANES), F32),
        ],
        scratch_shapes=[
            pltpu.VMEM((heads_j, size + EDGE, LANES), F32),
            pltpu.VMEM((5, heads_j, EDGE, LANES), F32),
            pltpu.VMEM((heads_j, LANES, LANES), F32),
            pltpu.VMEM((heads_j, LANES, LANES), F32),
        ],
        input_output_aliases=aliases,
        cost_estimate=cost(20),
        name=f"main{p}",
    )(*operands)


def on_device(x, taps, step_size, decay_log, write_in, read_in, skip_gain, out_grad):
    count, heads_j, width = x.shape
    groups = decay_log.shape[1]
    pairs = groups // 2
    spans = count // SPAN
    heads = 2 * heads_j
    rim = taps.shape[0] - 1
    n_head = lax.axis_size("head")
    n_seq = lax.axis_size("seq")
    core = jnp.stack([lax.axis_index("head") % 2, lax.axis_index("seq") // (n_seq // 2) % 2]).astype(jnp.int32)
    per = 4 if spans % 4 == 0 else 1
    gather = jnp.asarray(gather_matrix(heads_j, groups), BF16)
    parts, rows = pl.pallas_call(
        scales_kernel,
        grid=(spans // per,),
        in_specs=[
            pl.BlockSpec((heads_j * groups, per * SPAN), lambda i: (0, i)),
            pl.BlockSpec((heads_j * groups, 1), lambda i: (0, 0)),
            pl.BlockSpec(gather.shape, lambda i: (0, 0)),
        ],
        out_specs=[
            pl.BlockSpec((pairs, per * SPAN, LANES), lambda i: (0, i, 0)),
            pl.BlockSpec((per, heads_j * groups, SPAN), lambda i: (i, 0, 0)),
        ],
        out_shape=[
            jax.ShapeDtypeStruct((pairs, count, LANES), BF16),
            jax.ShapeDtypeStruct((spans, heads_j * groups, SPAN), F32),
        ],
        cost_estimate=cost(4),
        name="scales",
    )(
        jnp.transpose(step_size, (1, 2, 0)).reshape(heads_j * groups, count),
        decay_log.reshape(heads_j * groups, 1),
        gather,
    )
    halo = passed_along(x[count - rim :], "seq", 1)
    skips = jnp.broadcast_to(skip_gain[:, :, None], (heads_j, groups, HALF)).reshape(heads_j, width)
    a_m, dt_m, e_m, df_m = (jnp.asarray(spread_matrix(q, heads_j), BF16) for q in range(4))
    heads_m = jnp.asarray(head_matrix(heads_j), BF16)

    values, slopes, s_all, r_all, froms, tos = [], [], [], [], [], []
    exchanges = []

    def boundary(token, *others):
        moved = [e for e in exchanges if not e.finished()]
        for e in moved:
            e.combine(token)
        ended = [e for e in exchanges if e.finished() and e.got is not None and not e.held]
        tied = lax.optimization_barrier((token, *[e.sent for e in moved], *[e.got for e in ended], *others))
        for e, value in zip(ended, tied[1 + len(moved) :]):
            e.got, e.held = value, True
        for e, value in zip(moved, tied[1:]):
            e.sent = value
            e.swap()
        return [tied[0], *[e.sent for e in moved]], tied[len(tied) - len(others) :]

    waits = []
    for p in range(pairs):
        u, slope, s_loc, r_loc, from_start, to_end, total = states_call(
            p, waits, x, halo, taps, write_in, parts, out_grad, read_in, e_m, df_m
        )
        waits, (total,) = boundary(from_start, total)
        exchanges.append(Exchange(total))
        exchanges[-1].swap()
        values.append(u)
        slopes.append(slope)
        s_all.append(s_loc)
        r_all.append(r_loc)
        froms.append(from_start)
        tos.append(to_end)

    mixed = dx = None
    cores = [(i, i ^ 1) for i in range(n_head)]
    sums, edges, arrived, summed = [], [], [], []
    smem = pl.BlockSpec(memory_space=pltpu.SMEM)
    anywhere = pl.BlockSpec(memory_space=pl.ANY)
    for p in range(pairs):
        near_in, near_out, reach = exchanges[p].known
        far = exchanges[p].got
        mixed, dx, keep, send, total, edge = main_call(
            p, waits, core, x, values[p], slopes[p], out_grad, write_in, read_in, parts, rows, s_all[p], r_all[p], near_in,
            near_out, reach, far, froms[p], tos[p], taps, skips, heads_m, a_m, dt_m, mixed, dx,
        )
        sums.append(total)
        edges.append(edge)
        waits, tied = boundary(edge, send, *arrived)
        if summed:
            summed[-1] = tied[1]
        mine = keep + lax.ppermute(tied[0], "head", cores)
        waits.append(mine)
        arrived = []
        distance = 2
        while distance < n_head:
            got = lax.ppermute(mine, "head", [(i, i ^ distance) for i in range(n_head)])
            if p == pairs - 1 and 2 * distance >= n_head:
                break
            mine = mine + got
            distance *= 2
        arrived.append(mine)
        if p < pairs - 1:
            summed.append(mine)

    edge = jnp.transpose(jnp.concatenate(edges, axis=-1)[:, :rim, :], (1, 0, 2))
    after = passed_along(edge, "seq", -1)
    big = 6 * SPAN if spans % 6 == 0 else SPAN
    block = pl.BlockSpec((big, 2 * LANES), lambda i: (i, 0))
    token = after
    write_grad = read_grad = None
    for p in range(pairs):
        if p == pairs - 1:
            got, token = lax.optimization_barrier((got, token))
            summed.append(mine + got)
        other = lax.ppermute(summed[p], "head", cores)
        operands, in_specs, aliases = [core, summed[p], other, token], [smem, block, block, anywhere], {}
        if p > 0:
            operands += [write_grad, read_grad]
            in_specs += [anywhere] * 2
            aliases = {4: 0, 5: 1}
        write_grad, read_grad, token = pl.pallas_call(
            place_kernel,
            grid=(count // big,),
            in_specs=in_specs,
            out_specs=[pl.BlockSpec((big, 2 * LANES), lambda i, p=p: (i, p))] * 2
            + [pl.BlockSpec((EDGE, LANES), lambda i: (0, 0))],
            out_shape=[jax.ShapeDtypeStruct((count, groups * LANES), BF16)] * 2
            + [jax.ShapeDtypeStruct((EDGE, LANES), F32)],
            input_output_aliases=aliases,
            cost_estimate=cost(2),
            name=f"place{p}",
        )(*operands)

    tail_spec = pl.BlockSpec((EDGE, heads_j, width), lambda i: (count // EDGE - 1, 0, 0))
    dx = pl.pallas_call(
        edge_kernel,
        grid=(1,),
        in_specs=[fixed(after), fixed(taps), tail_spec],
        out_specs=tail_spec,
        out_shape=jax.ShapeDtypeStruct(x.shape, BF16),
        input_output_aliases={2: 0},
        name="edge",
    )(after, taps, dx)
    before = halo.astype(F32)
    sums = jnp.concatenate(sums, axis=-1)
    extra = []
    for tap in range(5):
        piece = jnp.zeros_like(sums[0])
        for row in range(rim - tap):
            piece = piece + edge[row] * before[row + tap]
        extra.append(piece)
    sums = swap_sum(sums + jnp.stack(extra), "seq")
    conv_grad = sums[:4]
    decay_grad = LN2 * sums[4].reshape(heads_j, groups, HALF).sum(-1)
    return (mixed, dx, conv_grad, decay_grad, write_grad, read_grad)


def solution(mesh):
    return jax.shard_map(
        on_device,
        mesh=mesh,
        in_specs=(
            P("seq", "head", None),
            P(None, "head", None),
            P("seq", "head", None),
            P("head", None),
            P("seq", None),
            P("seq", None),
            P("head", None),
            P("seq", "head", None),
        ),
        out_specs=(
            P("seq", "head", None),
            P("seq", "head", None),
            P(None, "head", None),
            P("head", None),
            P("seq", None),
            P("seq", None),
        ),
        check_vma=False,
    )
```

```python
import functools

import jax
import jax.numpy as jnp
import numpy as np
from jax import lax
from jax.experimental import pallas as pl
from jax.experimental.pallas import tpu as pltpu
from jax.sharding import PartitionSpec as P

SPAN = 128
LANES = 128
HALF = 64
EDGE = 8
F32 = jnp.float32
BF16 = jnp.bfloat16
NT = (((1,), (1,)), ((), ()))
TN = (((0,), (0,)), ((), ()))
LOG2E = 1.4426950408889634
LN2 = 0.6931471805599453
PARTS = (3, 2, 2, 2)


def cost(microseconds):
    return pl.CostEstimate(flops=int(microseconds * 1.15e9), transcendentals=0, bytes_accessed=0)


def dot(a, b, dims=None):
    if dims is None:
        return jnp.dot(a, b, preferred_element_type=F32)
    return lax.dot_general(a, b, dims, preferred_element_type=F32)


def low_half(rows):
    return lax.broadcasted_iota(jnp.int32, (rows, LANES), 1) < HALF


def split_parts(value, count):
    parts = []
    for _ in range(count - 1):
        part = value.astype(BF16)
        parts.append(part)
        value = value - part.astype(F32)
    parts.append(value.astype(BF16))
    return parts


def part_lane(quantity, part, head, heads):
    return (sum(PARTS[:quantity]) + part) * heads + head


def gather_matrix(heads_j, groups):
    heads, pairs, count = 2 * heads_j, groups // 2, sum(PARTS)
    matrix = np.zeros((count * heads_j * groups, pairs * LANES), np.float32)
    for part in range(count):
        for j in range(heads_j):
            for g in range(groups):
                matrix[part * heads_j * groups + j * groups + g, (g // 2) * LANES + part * heads + 2 * j + g % 2] = 1.0
    return matrix


def spread_matrix(quantity, heads_j):
    heads = 2 * heads_j
    matrix = np.zeros((LANES, heads_j * LANES), np.float32)
    for part in range(PARTS[quantity]):
        for h in range(heads):
            matrix[part_lane(quantity, part, h, heads), h * HALF : (h + 1) * HALF] = 1.0
    return matrix


def head_matrix(heads_j):
    heads = 2 * heads_j
    matrix = np.zeros((LANES, heads * LANES), np.float32)
    for part in range(PARTS[0]):
        for h in range(heads):
            matrix[part_lane(0, part, h, heads), h * LANES : (h + 1) * LANES] = 1.0
    return matrix


def scales_kernel(dt_ref, log_ref, gather_ref, parts_ref, rows_ref):
    every, count = dt_ref.shape
    heads_j, groups = log_ref.shape
    logs = log_ref[...]
    own = lax.broadcasted_iota(jnp.int32, (groups, groups), 0) == lax.broadcasted_iota(jnp.int32, (groups, groups), 1)
    logs = [jnp.sum(jnp.where(own, logs[j : j + 1], 0.0), axis=1, keepdims=True) for j in range(heads_j)]
    rates = -LOG2E * jnp.exp(jnp.concatenate(logs, axis=0))
    upper = (
        lax.broadcasted_iota(jnp.int32, (SPAN, SPAN), 0) <= lax.broadcasted_iota(jnp.int32, (SPAN, SPAN), 1)
    ).astype(BF16)
    for at in range(0, count, SPAN):
        dt = dt_ref[:, at : at + SPAN]
        summed = dot(jnp.concatenate(split_parts(dt * rates, 3), axis=0), upper)
        cumul = summed[:every] + summed[every : 2 * every] + summed[2 * every :]
        tail = jnp.exp2(cumul[:, SPAN - 1 : SPAN] - cumul)
        parts = []
        for value, number in zip((cumul, dt, jnp.exp2(cumul), dt * tail), PARTS, strict=True):
            parts += split_parts(value, number)
        placed = dot(jnp.concatenate(parts, axis=0), gather_ref[...], TN).astype(BF16)
        for p in range(parts_ref.shape[0]):
            parts_ref[p, at : at + SPAN, :] = placed[:, p * LANES : (p + 1) * LANES]
        rows_ref[at // SPAN] = cumul


def states_kernel(
    x_ref, halo_ref, w_ref, b_ref, partf_ref, y_ref, c_ref, partr_ref, lead_ref, tail_ref,
    u_ref, slope_ref, s_ref, r_ref, from_ref, to_ref, total_ref, x_buf, s_acc, r_acc, f_acc, t_acc,
):
    step = pl.program_id(0)
    rows, heads_j, _ = x_ref.shape
    low = low_half(SPAN)

    @pl.when(step == 0)
    def _():
        s_acc[...] = jnp.zeros_like(s_acc)
        r_acc[...] = jnp.zeros_like(r_acc)
        f_acc[...] = jnp.ones_like(f_acc)
        t_acc[...] = jnp.ones_like(t_acc)
        halo = halo_ref[...].astype(F32)
        for j in range(heads_j):
            for row in range(3):
                x_buf[j, EDGE - 3 + row : EDGE - 2 + row, :] = halo[row, j : j + 1, :]

    @pl.when(step > 0)
    def _():
        x_buf[:, 0:EDGE, :] = x_buf[:, rows : rows + EDGE, :]

    x_buf[:, EDGE : EDGE + rows, :] = jnp.swapaxes(x_ref[...], 0, 1).astype(F32)
    weights = w_ref[...]
    number = rows // SPAN
    def one(k):
        m = number - 1 - k
        start = k * SPAN
        here = pl.ds(start, SPAN)
        there = pl.ds(m * SPAN, SPAN)
        grads_all = jnp.swapaxes(y_ref[there], 0, 1)
        partf = partf_ref[0, here, :]
        tails = dot(partf, tail_ref[...])
        leads = dot(jnp.concatenate([partr_ref[0, there, :], partf[SPAN - EDGE :]], axis=0), lead_ref[...])
        s_ref[k] = s_acc[...].astype(BF16)
        r_ref[m] = r_acc[...].astype(BF16)
        from_ref[k] = f_acc[...]
        to_ref[m] = t_acc[...]
        wrote, read = [], []
        for j in range(heads_j):
            lanes = slice(j * LANES, (j + 1) * LANES)
            at = start + EDGE - 3
            v = 0.5 * weights[0, j : j + 1, :] * x_buf[j, at : at + SPAN, :]
            for tap in range(1, 4):
                v = v + 0.5 * weights[tap, j : j + 1, :] * x_buf[j, at + tap : at + tap + SPAN, :]
            gate = 1.0 + jnp.tanh(v)
            u = v * gate
            u_ref[j, k] = u.astype(BF16)
            slope_ref[j, k] = (gate + u * (2.0 - gate)).astype(BF16)
            wrote.append((u * tails[:, lanes]).astype(BF16))
            read.append((grads_all[j].astype(F32) * leads[:SPAN, lanes]).astype(BF16))
        own_s = dot(b_ref[here, :], jnp.concatenate(wrote, axis=1), TN)
        own_r = dot(c_ref[there, :], jnp.concatenate(read, axis=1), TN)
        for j in range(heads_j):
            lanes = slice(j * LANES, (j + 1) * LANES)
            keep = leads[SPAN + EDGE - 1 : SPAN + EDGE, lanes]
            s_acc[j] = keep * s_acc[j] + jnp.where(low, own_s[:LANES, lanes], own_s[LANES:, lanes])
            f_acc[j] = f_acc[j] * keep
            keep = leads[SPAN - 1 : SPAN, lanes]
            r_acc[j] = keep * r_acc[j] + jnp.where(low, own_r[:LANES, lanes], own_r[LANES:, lanes])
            t_acc[j] = t_acc[j] * keep

    for turn in range(number):
        one(turn)

    @pl.when(step == pl.num_programs(0) - 1)
    def _():
        total_ref[0, :, :LANES, :] = s_acc[...].astype(BF16)
        total_ref[1, :, :LANES, :] = r_acc[...].astype(BF16)
        for j in range(heads_j):
            decay = f_acc[j][0:1]
            high = decay.astype(BF16).astype(F32)
            pair = jnp.concatenate([high, decay - high, jnp.zeros((6, LANES), F32)], axis=0)
            total_ref[0, j, LANES:, :] = pair.astype(BF16)
            total_ref[1, j, LANES:, :] = pair.astype(BF16)


def fold(value):
    return jnp.sum(value.reshape(value.shape[0] // 8, 8, value.shape[1]), axis=0)


def main_kernel(
    head0, core_ref, x_ref, u_ref, slope_ref, y_ref, b_ref, c_ref, part_ref, row_ref, s_ref, r_ref,
    enter_ref, leave_ref, from_ref, to_ref, w_ref, skip_ref, heads_ref, a_ref, dt_ref, *rest,
):
    mixed_ref, dx_ref, keep_ref, send_ref, sums_ref, edge_ref, dv_buf, acc = rest[-8:]
    step = pl.program_id(0)
    size, heads_j, _ = x_ref.shape
    span = SPAN
    number = size // span
    groups = row_ref.shape[1] // heads_j
    low = low_half(span)
    causal = lax.broadcasted_iota(jnp.int32, (span, span), 0) >= lax.broadcasted_iota(
        jnp.int32, (span, span), 1
    )

    @pl.when(step == 0)
    def _():
        acc[...] = jnp.zeros_like(acc)
        dv_buf[:, size : size + EDGE, :] = jnp.zeros((heads_j, EDGE, LANES), F32)

    @pl.when(step > 0)
    def _():
        dv_buf[:, size : size + EDGE, :] = dv_buf[:, 0:EDGE, :]

    def one(turn):
        k = number - 1 - turn
        base = k * span
        here = pl.ds(base, span)
        xs = jnp.swapaxes(x_ref[here], 0, 1)
        grads = jnp.swapaxes(y_ref[here], 0, 1)
        b_all = b_ref[here, :]
        c_all = c_ref[here, :]
        weights = w_ref[...]
        skips = skip_ref[...]
        part = part_ref[0, here, :]
        zero = jnp.zeros((span, LANES), BF16)
        def diagonal(array):
            return jnp.concatenate(
                [jnp.concatenate([array[:, :LANES], zero], axis=1), jnp.concatenate([zero, array[:, LANES:]], axis=1)],
                axis=0,
            )

        b_diag = diagonal(b_all)
        scores = dot(c_all, b_diag, NT)
        a_all = dot(part, a_ref[...])
        dt_all = dot(part, dt_ref[...])
        score_grads = [None, None]
        logs = row_ref[k]
        states, rstates, state_cat, rstate_cat = [], [], [], []
        for j in range(heads_j):
            state = s_ref[k, j].astype(F32) + from_ref[k, j][0:1] * enter_ref[j]
            rstate = r_ref[k, j].astype(F32) + to_ref[k, j][0:1] * leave_ref[j]
            states.append(fold(state * rstate))
            state = state.astype(BF16)
            rstate = rstate.astype(BF16)
            state_cat.append(jnp.concatenate([jnp.where(low, state, zero), jnp.where(low, zero, state)], axis=0))
            rstate_cat.append(jnp.concatenate([jnp.where(low, rstate, zero), jnp.where(low, zero, rstate)], axis=0))
        state_cat = jnp.concatenate(state_cat, axis=1)
        rstate_cat = jnp.concatenate(rstate_cat, axis=1)
        carried_all = dot(c_all, state_cat)
        back_all = dot(b_all, rstate_cat)
        out_rows, leads, tails = [], [], []
        for j in range(heads_j):
            lanes = slice(j * LANES, (j + 1) * LANES)
            a_b = a_all[:, lanes]
            dt_b = dt_all[:, lanes]
            a_last = a_b[span - 1 : span]
            e_b = jnp.exp2(a_b)
            f_b = jnp.exp2(a_last - a_b)
            e_last = e_b[span - 1 : span]
            heads_b = dot(part, heads_ref[:, 2 * j * LANES : 2 * (j + 1) * LANES])
            u = u_ref[j, k].astype(F32)
            dy = grads[j].astype(F32)
            dy16 = dy.astype(BF16)
            val16 = (u * dt_b).astype(BF16)
            val = val16.astype(F32)
            tails.append((val * f_b).astype(BF16))
            leads.append((dy * e_b).astype(BF16))
            dy_two = jnp.concatenate([jnp.where(low, dy16, zero), jnp.where(low, zero, dy16)], axis=0)
            val_two = jnp.concatenate([jnp.where(low, val16, zero), jnp.where(low, zero, val16)], axis=0)
            products = dot(dy16, val_two, NT)
            mixes = []
            for g in range(2):
                at = j * groups + head0 + g
                inside = slice(g * LANES, (g + 1) * LANES)
                spread = heads_b[:, inside] - logs[at : at + 1]
                decay = jnp.exp2(jnp.where(causal, spread, -jnp.inf))
                mixes.append((scores[:, inside] * decay).astype(BF16))
                weighted = decay * products[:, inside]
                score_grads[g] = weighted if score_grads[g] is None else score_grads[g] + weighted
            inner = dot(jnp.concatenate(mixes, axis=1), val_two)
            dval = dot(jnp.concatenate(mixes, axis=0), dy_two, TN)
            carried = carried_all[:, lanes] * e_b
            back = back_all[:, lanes] * f_b
            out = inner + carried
            dval_full = dval + back
            log_part = a_b * (dy * out - val * dval_full) + a_last * (val * back)
            acc[4, j] = acc[4, j] + fold(log_part) + states[j] * (a_last * e_last)
            skip = skips[j : j + 1, :]
            out_rows.append((out + skip * u).astype(BF16))
            dv_buf[j, here, :] = (dt_b * dval_full + skip * dy) * (0.5 * slope_ref[j, k].astype(F32))
        mixed_ref[here] = jnp.swapaxes(jnp.stack(out_rows, axis=0), 0, 1)
        dc_inter = dot(jnp.concatenate(leads, axis=1), state_cat, NT)
        db_inter = dot(jnp.concatenate(tails, axis=1), rstate_cat, NT)
        dx_rows = []
        for j in range(heads_j):
            x = xs[j].astype(F32)
            at = base + 3
            total = None
            for tap in range(4):
                shifted = dv_buf[j, at - tap : at - tap + span, :]
                piece = weights[tap, j : j + 1, :] * shifted
                total = piece if total is None else total + piece
                acc[tap, j] = acc[tap, j] + fold(shifted * x)
            dx_rows.append(total.astype(BF16))
        dx_ref[here] = jnp.swapaxes(jnp.stack(dx_rows, axis=0), 0, 1)
        flows = [flow.astype(BF16) for flow in score_grads]
        dc = (dot(jnp.concatenate(flows, axis=1), b_diag) + dc_inter).astype(BF16)
        db = (dot(jnp.concatenate(flows, axis=0), diagonal(c_all), TN) + db_inter).astype(BF16)

        @pl.when(core_ref[0] == 0)
        def _():
            keep_ref[here, :] = db
            send_ref[here, :] = dc

        @pl.when(core_ref[0] != 0)
        def _():
            keep_ref[here, :] = dc
            send_ref[here, :] = db

    for turn in range(number):
        one(turn)

    @pl.when(step == pl.num_programs(0) - 1)
    def _():
        edge_ref[...] = dv_buf[:, 0:EDGE, :]
        for tap in range(5):
            for j in range(heads_j):
                sums_ref[tap, j : j + 1, :] = jnp.sum(acc[tap, j], axis=0, keepdims=True)


def place_kernel(core_ref, mine_ref, got_ref, *rest):
    write_ref, read_ref, token_ref = rest[-3:]
    token_ref[...] = jnp.zeros_like(token_ref)

    @pl.when(core_ref[0] == 0)
    def _():
        write_ref[...] = mine_ref[...]
        read_ref[...] = got_ref[...]

    @pl.when(core_ref[0] != 0)
    def _():
        write_ref[...] = got_ref[...]
        read_ref[...] = mine_ref[...]


def edge_kernel(after_ref, w_ref, dx_ref, out_ref):
    rows = dx_ref.shape[0]
    weights = w_ref[...]
    after = after_ref[...]
    out_ref[: rows - 3] = dx_ref[: rows - 3]
    for row in range(3):
        fix = weights[0] * after[row]
        for tap in range(1, row + 1):
            fix = fix + weights[tap] * after[row - tap]
        at = rows - 3 + row
        out_ref[at] = (dx_ref[at].astype(F32) + fix).astype(BF16)


def halves_of(ref):
    decay = ref[0, :, LANES, :].astype(F32) + ref[0, :, LANES + 1, :].astype(F32)
    return ref[0, :, :LANES, :].astype(F32), ref[1, :, :LANES, :].astype(F32), decay


def combine_kernel(first, last, bits_ref, mine_ref, got_ref, *refs):
    if not first:
        enter_ref, leave_ref, reach_ref = refs[:3]
    send_ref, enter_out, leave_out, reach_out = refs[-4:]

    def write(forward, backward, decay):
        if last:

            @pl.when(bits_ref[1] == 1)
            def _():
                send_ref[...] = backward.astype(BF16)

            @pl.when(bits_ref[1] == 0)
            def _():
                send_ref[...] = forward.astype(BF16)
        else:
            high = decay.astype(BF16).astype(F32)
            send_ref[0, :, :LANES, :] = forward.astype(BF16)
            send_ref[1, :, :LANES, :] = backward.astype(BF16)
            zeros = jnp.zeros((6, LANES), F32)
            for j in range(decay.shape[0]):
                rows = jnp.concatenate([high[j : j + 1], decay[j : j + 1] - high[j : j + 1], zeros], axis=0)
                send_ref[0, j, LANES:, :] = rows.astype(BF16)
                send_ref[1, j, LANES:, :] = rows.astype(BF16)

    own_f, own_b, own_d = halves_of(mine_ref)
    got_f, got_b, got_d = halves_of(got_ref)
    wide, got_wide = own_d[:, None, :], got_d[:, None, :]

    @pl.when(bits_ref[0] == 1)
    def _():
        if first:
            enter_out[...] = got_f
            leave_out[...] = jnp.zeros_like(got_b)
            reach_out[0] = got_d
            reach_out[1] = jnp.ones_like(got_d)
        else:
            enter_out[...] = enter_ref[...] + reach_ref[0][:, None, :] * got_f
            leave_out[...] = leave_ref[...]
            reach_out[0] = reach_ref[0] * got_d
            reach_out[1] = reach_ref[1]
        write(own_f + wide * got_f, got_b + got_wide * own_b, own_d * got_d)

    @pl.when(bits_ref[0] == 0)
    def _():
        if first:
            enter_out[...] = jnp.zeros_like(got_f)
            leave_out[...] = got_b
            reach_out[0] = jnp.ones_like(got_d)
            reach_out[1] = got_d
        else:
            enter_out[...] = enter_ref[...]
            leave_out[...] = leave_ref[...] + reach_ref[1][:, None, :] * got_b
            reach_out[0] = reach_ref[0]
            reach_out[1] = reach_ref[1] * got_d
        write(got_f + got_wide * own_f, own_b + wide * got_b, own_d * got_d)


class Exchange:
    def __init__(self, total):
        self.count = lax.axis_size("seq")
        self.sent = total
        self.shape = (total.shape[1], LANES, LANES)
        self.distance = 1
        self.known = ()
        self.got = None

    def bit(self, distance):
        return (lax.axis_index("seq") // distance % 2).astype(jnp.int32)

    def swap(self):
        self.got = lax.ppermute(self.sent, "seq", [(i, i ^ self.distance) for i in range(self.count)])

    def finish(self, after):
        while not self.finished():
            self.combine(after)
            self.swap()
        near_in, near_out, after = lax.optimization_barrier((self.known[0], self.known[1], after))
        reach = self.known[2][:, :, None, :]
        upper = self.bit(self.distance) == 1
        far = self.got.astype(F32)
        enter = near_in + jnp.where(upper, reach[0] * far, 0.0)
        leave = near_out + jnp.where(upper, 0.0, reach[1] * far)
        return enter, leave, after

    def finished(self):
        return 2 * self.distance >= self.count

    def combine(self, *after):
        bits = jnp.stack([self.bit(self.distance), self.bit(2 * self.distance)])
        last = 4 * self.distance >= self.count
        operands = (self.sent, self.got, *self.known)
        send = self.shape if last else self.sent.shape
        self.sent, *self.known = pl.pallas_call(
            functools.partial(combine_kernel, not self.known, last),
            in_specs=[pl.BlockSpec(memory_space=pltpu.SMEM)] + [pl.BlockSpec(memory_space=pltpu.VMEM)] * len(operands)
            + [pl.BlockSpec(memory_space=pl.ANY)] * len(after),
            out_specs=[pl.BlockSpec(memory_space=pltpu.VMEM)] * 4,
            out_shape=[
                jax.ShapeDtypeStruct(send, BF16),
                jax.ShapeDtypeStruct(self.shape, F32),
                jax.ShapeDtypeStruct(self.shape, F32),
                jax.ShapeDtypeStruct((2, self.shape[0], LANES), F32),
            ],
            cost_estimate=cost(1),
            name="combine",
        )(bits, *operands, *after)
        self.distance *= 2


def passed_along(block, axis, distance):
    devices = range(lax.axis_size(axis))
    route = [(i - distance, i) for i in devices if i - distance in devices]
    return lax.ppermute(block, axis, route)


def swap_sum(value, axis):
    count = lax.axis_size(axis)
    distance = 1
    while distance < count:
        value = value + lax.ppermute(value, axis, [(i, i ^ distance) for i in range(count)])
        distance *= 2
    return value


SCALES_SPANS = 6
STATES_SPANS = 3
MAIN_SPANS = 1


def at_most(limit, spans):
    return max(n for n in range(1, limit + 1) if spans % n == 0)


def fixed(array):
    return pl.BlockSpec(array.shape, lambda i: (0,) * array.ndim)


def states_call(p, waits, x, halo, taps, write_in, parts, out_grad, read_in, e_m, df_m):
    count, heads_j, _ = x.shape
    spans = count // SPAN
    per = at_most(STATES_SPANS, spans)
    size = per * SPAN
    end = spans // per - 1
    def kernel(*refs):
        states_kernel(*refs[:10], *refs[10 + len(waits) :])

    return pl.pallas_call(
        kernel,
        grid=(spans // per,),
        in_specs=[
            pl.BlockSpec((size, heads_j, LANES), lambda i: (i, 0, p)),
            pl.BlockSpec((halo.shape[0], heads_j, LANES), lambda i: (0, 0, p)),
            pl.BlockSpec((4, heads_j, LANES), lambda i: (0, 0, p)),
            pl.BlockSpec((size, 2 * LANES), lambda i: (i, p)),
            pl.BlockSpec((1, size, LANES), lambda i: (p, i, 0)),
            pl.BlockSpec((size, heads_j, LANES), lambda i: (end - i, 0, p)),
            pl.BlockSpec((size, 2 * LANES), lambda i: (end - i, p)),
            pl.BlockSpec((1, size, LANES), lambda i: (p, end - i, 0)),
            fixed(e_m), fixed(df_m),
        ] + [pl.BlockSpec(memory_space=pl.ANY)] * len(waits),
        out_specs=[
            pl.BlockSpec((heads_j, per, SPAN, LANES), lambda i: (0, i, 0, 0)),
            pl.BlockSpec((heads_j, per, SPAN, LANES), lambda i: (0, i, 0, 0)),
            pl.BlockSpec((per, heads_j, LANES, LANES), lambda i: (i, 0, 0, 0)),
            pl.BlockSpec((per, heads_j, LANES, LANES), lambda i: (end - i, 0, 0, 0)),
            pl.BlockSpec((per, heads_j, EDGE, LANES), lambda i: (i, 0, 0, 0)),
            pl.BlockSpec((per, heads_j, EDGE, LANES), lambda i: (end - i, 0, 0, 0)),
            pl.BlockSpec((2, heads_j, LANES + EDGE, LANES), lambda i: (0, 0, 0, 0)),
        ],
        out_shape=[
            jax.ShapeDtypeStruct((heads_j, spans, SPAN, LANES), BF16),
            jax.ShapeDtypeStruct((heads_j, spans, SPAN, LANES), BF16),
            jax.ShapeDtypeStruct((spans, heads_j, LANES, LANES), BF16),
            jax.ShapeDtypeStruct((spans, heads_j, LANES, LANES), BF16),
            jax.ShapeDtypeStruct((spans, heads_j, EDGE, LANES), F32),
            jax.ShapeDtypeStruct((spans, heads_j, EDGE, LANES), F32),
            jax.ShapeDtypeStruct((2, heads_j, LANES + EDGE, LANES), BF16),
        ],
        scratch_shapes=[
            pltpu.VMEM((heads_j, size + EDGE, LANES), F32),
            pltpu.VMEM((heads_j, LANES, LANES), F32),
            pltpu.VMEM((heads_j, LANES, LANES), F32),
            pltpu.VMEM((heads_j, EDGE, LANES), F32),
            pltpu.VMEM((heads_j, EDGE, LANES), F32),
        ],
        cost_estimate=cost(9),
        name=f"states{p}",
    )(x, halo, taps, write_in, parts, out_grad, read_in, parts, e_m, df_m, *waits)


def main_call(
    p, waits, core, x, value, slope, out_grad, write_in, read_in, parts, rows, s_loc, r_loc, enter,
    leave, from_start, to_end, taps, skips, heads_m, a_m, dt_m, mixed, dx,
):
    count, heads_j, _ = x.shape
    spans = count // SPAN
    per = at_most(MAIN_SPANS, spans)
    size = per * SPAN
    last = spans // per - 1
    operands = [core, x, value, slope, out_grad, write_in, read_in, parts, rows, s_loc, r_loc,
                enter, leave, from_start, to_end, taps, skips, heads_m, a_m, dt_m, *waits]
    time3 = pl.BlockSpec((size, heads_j, LANES), lambda i: (last - i, 0, p))
    time2 = pl.BlockSpec((size, 2 * LANES), lambda i: (last - i, p))
    own3 = pl.BlockSpec((heads_j, per, SPAN, LANES), lambda i: (0, last - i, 0, 0))
    own2 = pl.BlockSpec((size, 2 * LANES), lambda i: (last - i, 0))
    state = pl.BlockSpec((per, heads_j, LANES, LANES), lambda i: (last - i, 0, 0, 0))
    lane_row = pl.BlockSpec((per, heads_j, EDGE, LANES), lambda i: (last - i, 0, 0, 0))
    in_specs = [
        pl.BlockSpec(memory_space=pltpu.SMEM), time3, own3, own3, time3, time2, time2,
        pl.BlockSpec((1, size, LANES), lambda i: (p, last - i, 0)),
        pl.BlockSpec((per, rows.shape[1], SPAN), lambda i: (last - i, 0, 0)),
        state, state, fixed(enter), fixed(leave), lane_row, lane_row,
        pl.BlockSpec((4, heads_j, LANES), lambda i: (0, 0, p)),
        pl.BlockSpec((heads_j, LANES), lambda i: (0, p)),
        fixed(heads_m), fixed(a_m), fixed(dt_m),
    ] + [pl.BlockSpec(memory_space=pl.ANY)] * len(waits)
    aliases = {}
    if mixed is not None:
        aliases = {len(operands): 0, len(operands) + 1: 1}
        operands += [mixed, dx]
        in_specs += [pl.BlockSpec(memory_space=pl.ANY)] * 2
    return pl.pallas_call(
        functools.partial(main_kernel, 2 * p),
        grid=(spans // per,),
        in_specs=in_specs,
        out_specs=[
            time3, time3, own2, own2,
            pl.BlockSpec((5, heads_j, LANES), lambda i: (0, 0, 0)),
            pl.BlockSpec((heads_j, EDGE, LANES), lambda i: (0, 0, 0)),
        ],
        out_shape=[
            jax.ShapeDtypeStruct(x.shape, BF16),
            jax.ShapeDtypeStruct(x.shape, BF16),
            jax.ShapeDtypeStruct((count, 2 * LANES), BF16),
            jax.ShapeDtypeStruct((count, 2 * LANES), BF16),
            jax.ShapeDtypeStruct((5, heads_j, LANES), F32),
            jax.ShapeDtypeStruct((heads_j, EDGE, LANES), F32),
        ],
        scratch_shapes=[
            pltpu.VMEM((heads_j, size + EDGE, LANES), F32),
            pltpu.VMEM((5, heads_j, EDGE, LANES), F32),
        ],
        input_output_aliases=aliases,
        cost_estimate=cost(20),
        name=f"main{p}",
    )(*operands)


def on_device(x, taps, step_size, decay_log, write_in, read_in, skip_gain, out_grad):
    count, heads_j, width = x.shape
    groups = decay_log.shape[1]
    pairs = groups // 2
    spans = count // SPAN
    heads = 2 * heads_j
    rim = taps.shape[0] - 1
    n_head = lax.axis_size("head")
    core = (lax.axis_index("head") % 2).astype(jnp.int32).reshape(1)
    per = at_most(SCALES_SPANS, spans)
    gather = jnp.asarray(gather_matrix(heads_j, groups), BF16)
    parts, rows = pl.pallas_call(
        scales_kernel,
        grid=(spans // per,),
        in_specs=[
            pl.BlockSpec((heads_j * groups, per * SPAN), lambda i: (0, i)),
            pl.BlockSpec((heads_j, groups), lambda i: (0, 0)),
            pl.BlockSpec(gather.shape, lambda i: (0, 0)),
        ],
        out_specs=[
            pl.BlockSpec((pairs, per * SPAN, LANES), lambda i: (0, i, 0)),
            pl.BlockSpec((per, heads_j * groups, SPAN), lambda i: (i, 0, 0)),
        ],
        out_shape=[
            jax.ShapeDtypeStruct((pairs, count, LANES), BF16),
            jax.ShapeDtypeStruct((spans, heads_j * groups, SPAN), F32),
        ],
        cost_estimate=cost(4),
        name="scales",
    )(
        jnp.transpose(step_size, (1, 2, 0)).reshape(heads_j * groups, count),
        decay_log,
        gather,
    )
    halo = passed_along(x[count - rim :], "seq", 1)
    skips = jnp.broadcast_to(skip_gain[:, :, None], (heads_j, groups, HALF)).reshape(heads_j, width)
    a_m, dt_m, e_m, df_m = (jnp.asarray(spread_matrix(q, heads_j), BF16) for q in range(4))
    heads_m = jnp.asarray(head_matrix(heads_j), BF16)

    values, slopes, s_all, r_all, froms, tos = [], [], [], [], [], []
    exchanges = []

    def boundary(token, *others):
        moved = [e for e in exchanges if not e.finished()]
        for e in moved:
            e.combine(token)
        tied = lax.optimization_barrier((token, *[e.sent for e in moved], *others))
        for e, value in zip(moved, tied[1:]):
            e.sent = value
            e.swap()
        return [tied[0], *[e.sent for e in moved]], tied[len(tied) - len(others) :]

    waits = []
    for p in range(pairs):
        u, slope, s_loc, r_loc, from_start, to_end, total = states_call(
            p, waits, x, halo, taps, write_in, parts, out_grad, read_in, e_m, df_m
        )
        ready = exchanges[0].finish(from_start) if p == pairs - 1 else ()
        waits, (total, *ready) = boundary(from_start, total, *ready)
        exchanges.append(Exchange(total))
        exchanges[-1].swap()
        values.append(u)
        slopes.append(slope)
        s_all.append(s_loc)
        r_all.append(r_loc)
        froms.append(from_start)
        tos.append(to_end)

    mixed = dx = None
    cores = [(i, i ^ 1) for i in range(n_head)]
    sums, edges, arrived, summed = [], [], [], []
    smem = pl.BlockSpec(memory_space=pltpu.SMEM)
    anywhere = pl.BlockSpec(memory_space=pl.ANY)
    for p in range(pairs):
        enter, leave, token = ready
        mixed, dx, keep, send, total, edge = main_call(
            p, [*waits, token], core, x, values[p], slopes[p], out_grad, write_in, read_in, parts, rows, s_all[p], r_all[p], enter,
            leave, froms[p], tos[p], taps, skips, heads_m, a_m, dt_m, mixed, dx,
        )
        sums.append(total)
        edges.append(edge)
        ready = exchanges[p + 1].finish(edge) if p < pairs - 1 else ()
        waits, (send, *tied) = boundary(edge, send, *ready, *arrived)
        ready = tied[: len(ready)]
        if summed:
            summed[-1] = tied[-1]
        mine = keep + lax.ppermute(send, "head", cores)
        waits.append(mine)
        arrived = []
        distance = 2
        while distance < n_head:
            got = lax.ppermute(mine, "head", [(i, i ^ distance) for i in range(n_head)])
            if p == pairs - 1 and 2 * distance >= n_head:
                break
            mine = mine + got
            distance *= 2
        arrived.append(mine)
        if p < pairs - 1:
            summed.append(mine)

    edge = jnp.transpose(jnp.concatenate(edges, axis=-1)[:, :rim, :], (1, 0, 2))
    after = passed_along(edge, "seq", -1)
    before = halo.astype(F32)
    sums = jnp.concatenate(sums, axis=-1)
    extra = []
    for tap in range(5):
        piece = jnp.zeros_like(sums[0])
        for row in range(rim - tap):
            piece = piece + edge[row] * before[row + tap]
        extra.append(piece)
    sums = swap_sum(sums + jnp.stack(extra), "seq")
    big = 6 * SPAN if spans % 6 == 0 else SPAN
    block = pl.BlockSpec((big, 2 * LANES), lambda i: (i, 0))
    token = after
    write_grad = read_grad = None
    for p in range(pairs):
        if p == pairs - 1:
            got, token, sums = lax.optimization_barrier((got, token, sums))
            summed.append(mine + got)
        other = lax.ppermute(summed[p], "head", cores)
        operands, in_specs, aliases = [core, summed[p], other, token], [smem, block, block, anywhere], {}
        if p > 0:
            operands += [write_grad, read_grad]
            in_specs += [anywhere] * 2
            aliases = {4: 0, 5: 1}
        write_grad, read_grad, token = pl.pallas_call(
            place_kernel,
            grid=(count // big,),
            in_specs=in_specs,
            out_specs=[pl.BlockSpec((big, 2 * LANES), lambda i, p=p: (i, p))] * 2
            + [pl.BlockSpec((EDGE, LANES), lambda i: (0, 0))],
            out_shape=[jax.ShapeDtypeStruct((count, groups * LANES), BF16)] * 2
            + [jax.ShapeDtypeStruct((EDGE, LANES), F32)],
            input_output_aliases=aliases,
            cost_estimate=cost(2),
            name=f"place{p}",
        )(*operands)

    tail_spec = pl.BlockSpec((EDGE, heads_j, width), lambda i: (count // EDGE - 1, 0, 0))
    dx = pl.pallas_call(
        edge_kernel,
        grid=(1,),
        in_specs=[fixed(after), fixed(taps), tail_spec],
        out_specs=tail_spec,
        out_shape=jax.ShapeDtypeStruct(x.shape, BF16),
        input_output_aliases={2: 0},
        name="edge",
    )(after, taps, dx)
    conv_grad = sums[:4]
    decay_grad = LN2 * sums[4].reshape(heads_j, groups, HALF).sum(-1)
    return (mixed, dx, conv_grad, decay_grad, write_grad, read_grad)


def solution(mesh):
    return jax.shard_map(
        on_device,
        mesh=mesh,
        in_specs=(
            P("seq", "head", None),
            P(None, "head", None),
            P("seq", "head", None),
            P("head", None),
            P("seq", None),
            P("seq", None),
            P("head", None),
            P("seq", "head", None),
        ),
        out_specs=(
            P("seq", "head", None),
            P("seq", "head", None),
            P(None, "head", None),
            P("head", None),
            P("seq", None),
            P("seq", None),
        ),
        check_vma=False,
    )
```

```python
import functools

import jax
import jax.numpy as jnp
import numpy as np
from jax import lax
from jax.experimental import pallas as pl
from jax.experimental.pallas import tpu as pltpu
from jax.sharding import PartitionSpec as P

SPAN = 128
LANES = 128
HALF = 64
EDGE = 8
F32 = jnp.float32
BF16 = jnp.bfloat16
NT = (((1,), (1,)), ((), ()))
TN = (((0,), (0,)), ((), ()))
LOG2E = 1.4426950408889634
LN2 = 0.6931471805599453
PARTS = (3, 2, 2, 2)


def cost(microseconds):
    return pl.CostEstimate(flops=int(microseconds * 1.15e9), transcendentals=0, bytes_accessed=0)


def dot(a, b, dims=None):
    if dims is None:
        return jnp.dot(a, b, preferred_element_type=F32)
    return lax.dot_general(a, b, dims, preferred_element_type=F32)


def low_half(rows):
    return lax.broadcasted_iota(jnp.int32, (rows, LANES), 1) < HALF


def split_parts(value, count):
    parts = []
    for _ in range(count - 1):
        part = value.astype(BF16)
        parts.append(part)
        value = value - part.astype(F32)
    parts.append(value.astype(BF16))
    return parts


def part_lane(quantity, part, head, heads):
    return (sum(PARTS[:quantity]) + part) * heads + head


def gather_matrix(heads_j, groups):
    heads, pairs, count = 2 * heads_j, groups // 2, sum(PARTS)
    matrix = np.zeros((count * heads_j * groups, pairs * LANES), np.float32)
    for part in range(count):
        for j in range(heads_j):
            for g in range(groups):
                matrix[part * heads_j * groups + j * groups + g, (g // 2) * LANES + part * heads + 2 * j + g % 2] = 1.0
    return matrix


def spread_matrix(quantity, heads_j):
    heads = 2 * heads_j
    matrix = np.zeros((LANES, heads_j * LANES), np.float32)
    for part in range(PARTS[quantity]):
        for h in range(heads):
            matrix[part_lane(quantity, part, h, heads), h * HALF : (h + 1) * HALF] = 1.0
    return matrix


def head_matrix(heads_j):
    heads = 2 * heads_j
    matrix = np.zeros((LANES, heads * LANES), np.float32)
    for part in range(PARTS[0]):
        for h in range(heads):
            matrix[part_lane(0, part, h, heads), h * LANES : (h + 1) * LANES] = 1.0
    return matrix


def scales_kernel(dt_ref, log_ref, gather_ref, parts_ref, rows_ref):
    every, count = dt_ref.shape
    heads_j, groups = log_ref.shape
    logs = log_ref[...]
    own = lax.broadcasted_iota(jnp.int32, (groups, groups), 0) == lax.broadcasted_iota(jnp.int32, (groups, groups), 1)
    logs = [jnp.sum(jnp.where(own, logs[j : j + 1], 0.0), axis=1, keepdims=True) for j in range(heads_j)]
    rates = -LOG2E * jnp.exp(jnp.concatenate(logs, axis=0))
    upper = (
        lax.broadcasted_iota(jnp.int32, (SPAN, SPAN), 0) <= lax.broadcasted_iota(jnp.int32, (SPAN, SPAN), 1)
    ).astype(BF16)
    for at in range(0, count, SPAN):
        dt = dt_ref[:, at : at + SPAN]
        summed = dot(jnp.concatenate(split_parts(dt * rates, 3), axis=0), upper)
        cumul = summed[:every] + summed[every : 2 * every] + summed[2 * every :]
        tail = jnp.exp2(cumul[:, SPAN - 1 : SPAN] - cumul)
        parts = []
        for value, number in zip((cumul, dt, jnp.exp2(cumul), dt * tail), PARTS, strict=True):
            parts += split_parts(value, number)
        placed = dot(jnp.concatenate(parts, axis=0), gather_ref[...], TN).astype(BF16)
        for p in range(parts_ref.shape[0]):
            parts_ref[p, at : at + SPAN, :] = placed[:, p * LANES : (p + 1) * LANES]
        rows_ref[at // SPAN] = cumul


def states_kernel(
    x_ref, halo_ref, w_ref, b_ref, partf_ref, y_ref, c_ref, partr_ref, lead_ref, tail_ref,
    u_ref, slope_ref, s_ref, r_ref, from_ref, to_ref, total_ref, x_buf, s_acc, r_acc, f_acc, t_acc,
):
    step = pl.program_id(0)
    rows, heads_j, _ = x_ref.shape
    low = low_half(SPAN)

    @pl.when(step == 0)
    def _():
        s_acc[...] = jnp.zeros_like(s_acc)
        r_acc[...] = jnp.zeros_like(r_acc)
        f_acc[...] = jnp.ones_like(f_acc)
        t_acc[...] = jnp.ones_like(t_acc)
        halo = halo_ref[...].astype(F32)
        for j in range(heads_j):
            for row in range(3):
                x_buf[j, EDGE - 3 + row : EDGE - 2 + row, :] = halo[row, j : j + 1, :]

    @pl.when(step > 0)
    def _():
        x_buf[:, 0:EDGE, :] = x_buf[:, rows : rows + EDGE, :]

    x_buf[:, EDGE : EDGE + rows, :] = jnp.swapaxes(x_ref[...], 0, 1).astype(F32)
    weights = w_ref[...]
    number = rows // SPAN
    def one(k):
        m = number - 1 - k
        start = k * SPAN
        here = pl.ds(start, SPAN)
        there = pl.ds(m * SPAN, SPAN)
        grads_all = jnp.swapaxes(y_ref[there], 0, 1)
        partf = partf_ref[0, here, :]
        tails = dot(partf, tail_ref[...])
        leads = dot(jnp.concatenate([partr_ref[0, there, :], partf[SPAN - EDGE :]], axis=0), lead_ref[...])
        s_ref[k] = s_acc[...].astype(BF16)
        r_ref[m] = r_acc[...].astype(BF16)
        from_ref[k] = f_acc[...]
        to_ref[m] = t_acc[...]
        wrote, read = [], []
        for j in range(heads_j):
            lanes = slice(j * LANES, (j + 1) * LANES)
            at = start + EDGE - 3
            v = 0.5 * weights[0, j : j + 1, :] * x_buf[j, at : at + SPAN, :]
            for tap in range(1, 4):
                v = v + 0.5 * weights[tap, j : j + 1, :] * x_buf[j, at + tap : at + tap + SPAN, :]
            gate = 1.0 + jnp.tanh(v)
            u = v * gate
            u_ref[j, k] = u.astype(BF16)
            slope_ref[j, k] = (gate + u * (2.0 - gate)).astype(BF16)
            wrote.append((u * tails[:, lanes]).astype(BF16))
            read.append((grads_all[j].astype(F32) * leads[:SPAN, lanes]).astype(BF16))
        own_s = dot(b_ref[here, :], jnp.concatenate(wrote, axis=1), TN)
        own_r = dot(c_ref[there, :], jnp.concatenate(read, axis=1), TN)
        for j in range(heads_j):
            lanes = slice(j * LANES, (j + 1) * LANES)
            keep = leads[SPAN + EDGE - 1 : SPAN + EDGE, lanes]
            s_acc[j] = keep * s_acc[j] + jnp.where(low, own_s[:LANES, lanes], own_s[LANES:, lanes])
            f_acc[j] = f_acc[j] * keep
            keep = leads[SPAN - 1 : SPAN, lanes]
            r_acc[j] = keep * r_acc[j] + jnp.where(low, own_r[:LANES, lanes], own_r[LANES:, lanes])
            t_acc[j] = t_acc[j] * keep

    for turn in range(number):
        one(turn)

    @pl.when(step == pl.num_programs(0) - 1)
    def _():
        total_ref[0, :, :LANES, :] = s_acc[...].astype(BF16)
        total_ref[1, :, :LANES, :] = r_acc[...].astype(BF16)
        for j in range(heads_j):
            decay = f_acc[j][0:1]
            high = decay.astype(BF16).astype(F32)
            pair = jnp.concatenate([high, decay - high, jnp.zeros((6, LANES), F32)], axis=0)
            total_ref[0, j, LANES:, :] = pair.astype(BF16)
            total_ref[1, j, LANES:, :] = pair.astype(BF16)


def fold(value):
    return jnp.sum(value.reshape(value.shape[0] // 8, 8, value.shape[1]), axis=0)


def main_kernel(
    head0, core_ref, x_ref, u_ref, slope_ref, y_ref, b_ref, c_ref, part_ref, row_ref, s_ref, r_ref,
    enter_ref, leave_ref, from_ref, to_ref, w_ref, skip_ref, heads_ref, a_ref, dt_ref, *rest,
):
    mixed_ref, dx_ref, keep_ref, send_ref, sums_ref, edge_ref, dv_buf, acc = rest[-8:]
    step = pl.program_id(0)
    size, heads_j, _ = x_ref.shape
    span = SPAN
    number = size // span
    groups = row_ref.shape[1] // heads_j
    low = low_half(span)
    causal = lax.broadcasted_iota(jnp.int32, (span, span), 0) >= lax.broadcasted_iota(
        jnp.int32, (span, span), 1
    )

    @pl.when(step == 0)
    def _():
        acc[...] = jnp.zeros_like(acc)
        dv_buf[:, 0:EDGE, :] = jnp.zeros((heads_j, EDGE, LANES), F32)

    def one(turn, nothing):
        k = number - 1 - turn
        base = pl.multiple_of(k * span, span)
        dv_buf[:, span : span + EDGE, :] = dv_buf[:, 0:EDGE, :]
        here = pl.ds(base, span)
        xs = jnp.swapaxes(x_ref[here], 0, 1)
        grads = jnp.swapaxes(y_ref[here], 0, 1)
        b_all = b_ref[here, :]
        c_all = c_ref[here, :]
        weights = w_ref[...]
        skips = skip_ref[...]
        part = part_ref[0, here, :]
        zero = jnp.zeros((span, LANES), BF16)
        def diagonal(array):
            return jnp.concatenate(
                [jnp.concatenate([array[:, :LANES], zero], axis=1), jnp.concatenate([zero, array[:, LANES:]], axis=1)],
                axis=0,
            )

        b_diag = diagonal(b_all)
        scores16 = dot(c_all, b_diag, NT).astype(BF16)
        a_all = dot(part, a_ref[...])
        dt_all = dot(part, dt_ref[...])
        score_grads = [None, None]
        logs = row_ref[k]
        states, rstates, state_cat, rstate_cat = [], [], [], []
        for j in range(heads_j):
            state = s_ref[k, j].astype(F32) + from_ref[k, j][0:1] * enter_ref[j]
            rstate = r_ref[k, j].astype(F32) + to_ref[k, j][0:1] * leave_ref[j]
            states.append(fold(state * rstate))
            state = state.astype(BF16)
            rstate = rstate.astype(BF16)
            state_cat.append(jnp.concatenate([jnp.where(low, state, zero), jnp.where(low, zero, state)], axis=0))
            rstate_cat.append(jnp.concatenate([jnp.where(low, rstate, zero), jnp.where(low, zero, rstate)], axis=0))
        state_cat = jnp.concatenate(state_cat, axis=1)
        rstate_cat = jnp.concatenate(rstate_cat, axis=1)
        out_rows, leads, tails = [], [], []
        for j in range(heads_j):
            lanes = slice(j * LANES, (j + 1) * LANES)
            a_b = a_all[:, lanes]
            dt_b = dt_all[:, lanes]
            a_last = a_b[span - 1 : span]
            e_b = jnp.exp2(a_b)
            f_b = jnp.exp2(a_last - a_b)
            e_last = e_b[span - 1 : span]
            heads_b = dot(part, heads_ref[:, 2 * j * LANES : 2 * (j + 1) * LANES])
            u = u_ref[j, k].astype(F32)
            dy = grads[j].astype(F32)
            dy16 = dy.astype(BF16)
            val16 = (u * dt_b).astype(BF16)
            val = val16.astype(F32)
            tails.append((val * f_b).astype(BF16))
            leads.append((dy * e_b).astype(BF16))
            dy_two = jnp.concatenate([jnp.where(low, dy16, zero), jnp.where(low, zero, dy16)], axis=0)
            val_two = jnp.concatenate([jnp.where(low, val16, zero), jnp.where(low, zero, val16)], axis=0)
            products = dot(dy16, val_two, NT)
            mixes = []
            for g in range(2):
                at = j * groups + head0 + g
                inside = slice(g * LANES, (g + 1) * LANES)
                spread = heads_b[:, inside] - logs[at : at + 1]
                decay = jnp.exp2(jnp.where(causal, spread, -jnp.inf))
                mixes.append(scores16[:, inside] * decay.astype(BF16))
                weighted = decay * products[:, inside]
                score_grads[g] = weighted if score_grads[g] is None else score_grads[g] + weighted
            inner = dot(jnp.concatenate(mixes, axis=1), val_two)
            dval = dot(jnp.concatenate(mixes, axis=0), dy_two, TN)
            carried = dot(c_all, state_cat[:, lanes]) * e_b
            back = dot(b_all, rstate_cat[:, lanes]) * f_b
            out = inner + carried
            dval_full = dval + back
            log_part = a_b * (dy * out - val * dval_full)
            acc[4, j] = acc[4, j] + fold(log_part) + fold(val * back) * a_last + states[j] * (a_last * e_last)
            skip = skips[j : j + 1, :]
            out_rows.append((out + skip * u).astype(BF16))
            dv_buf[j, 0:span, :] = (dt_b * dval_full + skip * dy) * (0.5 * slope_ref[j, k].astype(F32))
        mixed_ref[here] = jnp.swapaxes(jnp.stack(out_rows, axis=0), 0, 1)
        dc_inter = dot(jnp.concatenate(leads, axis=1), state_cat, NT)
        db_inter = dot(jnp.concatenate(tails, axis=1), rstate_cat, NT)
        dx_rows = []
        for j in range(heads_j):
            x = xs[j].astype(F32)
            total = None
            for tap in range(4):
                shifted = dv_buf[j, 3 - tap : 3 - tap + span, :]
                piece = weights[tap, j : j + 1, :] * shifted
                total = piece if total is None else total + piece
                acc[tap, j] = acc[tap, j] + fold(shifted * x)
            dx_rows.append(total.astype(BF16))
        dx_ref[here] = jnp.swapaxes(jnp.stack(dx_rows, axis=0), 0, 1)
        flows = [flow.astype(BF16) for flow in score_grads]
        dc = (dot(jnp.concatenate(flows, axis=1), b_diag) + dc_inter).astype(BF16)
        db = (dot(jnp.concatenate(flows, axis=0), diagonal(c_all), TN) + db_inter).astype(BF16)

        @pl.when(core_ref[0] == 0)
        def _():
            keep_ref[here, :] = db
            send_ref[here, :] = dc

        @pl.when(core_ref[0] != 0)
        def _():
            keep_ref[here, :] = dc
            send_ref[here, :] = db

        return nothing

    lax.fori_loop(0, number, one, 0)

    @pl.when(step == pl.num_programs(0) - 1)
    def _():
        edge_ref[...] = dv_buf[:, 0:EDGE, :]
        for tap in range(5):
            for j in range(heads_j):
                sums_ref[tap, j : j + 1, :] = jnp.sum(acc[tap, j], axis=0, keepdims=True)


def place_kernel(number, core_ref, *refs):
    mine, got = refs[:number], refs[number : 2 * number]
    write_ref, read_ref, token_ref = refs[-3:]
    token_ref[...] = jnp.zeros_like(token_ref)

    @pl.when(core_ref[0] == 0)
    def _():
        for n in range(number):
            lanes = slice(2 * n * LANES, 2 * (n + 1) * LANES)
            write_ref[:, lanes] = mine[n][...]
            read_ref[:, lanes] = got[n][...]

    @pl.when(core_ref[0] != 0)
    def _():
        for n in range(number):
            lanes = slice(2 * n * LANES, 2 * (n + 1) * LANES)
            write_ref[:, lanes] = got[n][...]
            read_ref[:, lanes] = mine[n][...]


def place_call(core, mine, got, token, write_grad, read_grad, at, count, groups):
    number = len(mine)
    rows = at_most(4, count // SPAN) * SPAN
    anywhere = pl.BlockSpec(memory_space=pl.ANY)
    block = pl.BlockSpec((rows, 2 * LANES), lambda i: (i, 0))
    operands = [core, *mine, *got, token]
    in_specs = [pl.BlockSpec(memory_space=pltpu.SMEM)] + [block] * (2 * number) + [anywhere]
    aliases = {}
    if write_grad is not None:
        aliases = {len(operands): 0, len(operands) + 1: 1}
        operands += [write_grad, read_grad]
        in_specs += [anywhere] * 2
    return pl.pallas_call(
        functools.partial(place_kernel, number),
        grid=(count // rows,),
        in_specs=in_specs,
        out_specs=[pl.BlockSpec((rows, 2 * number * LANES), lambda i: (i, at))] * 2
        + [pl.BlockSpec((EDGE, LANES), lambda i: (0, 0))],
        out_shape=[jax.ShapeDtypeStruct((count, groups * LANES), BF16)] * 2 + [jax.ShapeDtypeStruct((EDGE, LANES), F32)],
        input_output_aliases=aliases,
        cost_estimate=cost(2 * number),
        name="place",
    )(*operands)


def edge_kernel(after_ref, w_ref, dx_ref, out_ref):
    rows = dx_ref.shape[0]
    weights = w_ref[...]
    after = after_ref[...]
    out_ref[: rows - 3] = dx_ref[: rows - 3]
    for row in range(3):
        fix = weights[0] * after[row]
        for tap in range(1, row + 1):
            fix = fix + weights[tap] * after[row - tap]
        at = rows - 3 + row
        out_ref[at] = (dx_ref[at].astype(F32) + fix).astype(BF16)


def halves_of(ref):
    decay = ref[0, :, LANES, :].astype(F32) + ref[0, :, LANES + 1, :].astype(F32)
    return ref[0, :, :LANES, :].astype(F32), ref[1, :, :LANES, :].astype(F32), decay


def combine_kernel(first, last, bits_ref, mine_ref, got_ref, *refs):
    if not first:
        enter_ref, leave_ref, reach_ref = refs[:3]
    send_ref, enter_out, leave_out, reach_out = refs[-4:]

    def write(forward, backward, decay):
        if last:

            @pl.when(bits_ref[1] == 1)
            def _():
                send_ref[...] = backward.astype(BF16)

            @pl.when(bits_ref[1] == 0)
            def _():
                send_ref[...] = forward.astype(BF16)
        else:
            high = decay.astype(BF16).astype(F32)
            send_ref[0, :, :LANES, :] = forward.astype(BF16)
            send_ref[1, :, :LANES, :] = backward.astype(BF16)
            zeros = jnp.zeros((6, LANES), F32)
            for j in range(decay.shape[0]):
                rows = jnp.concatenate([high[j : j + 1], decay[j : j + 1] - high[j : j + 1], zeros], axis=0)
                send_ref[0, j, LANES:, :] = rows.astype(BF16)
                send_ref[1, j, LANES:, :] = rows.astype(BF16)

    own_f, own_b, own_d = halves_of(mine_ref)
    got_f, got_b, got_d = halves_of(got_ref)
    wide, got_wide = own_d[:, None, :], got_d[:, None, :]

    @pl.when(bits_ref[0] == 1)
    def _():
        if first:
            enter_out[...] = got_f.astype(BF16)
            leave_out[...] = jnp.zeros_like(leave_out)
            reach_out[0] = got_d
            reach_out[1] = jnp.ones_like(got_d)
        else:
            enter_out[...] = (enter_ref[...].astype(F32) + reach_ref[0][:, None, :] * got_f).astype(BF16)
            leave_out[...] = leave_ref[...]
            reach_out[0] = reach_ref[0] * got_d
            reach_out[1] = reach_ref[1]
        write(own_f + wide * got_f, got_b + got_wide * own_b, own_d * got_d)

    @pl.when(bits_ref[0] == 0)
    def _():
        if first:
            enter_out[...] = jnp.zeros_like(enter_out)
            leave_out[...] = got_b.astype(BF16)
            reach_out[0] = jnp.ones_like(got_d)
            reach_out[1] = got_d
        else:
            enter_out[...] = enter_ref[...]
            leave_out[...] = (leave_ref[...].astype(F32) + reach_ref[1][:, None, :] * got_b).astype(BF16)
            reach_out[0] = reach_ref[0]
            reach_out[1] = reach_ref[1] * got_d
        write(got_f + got_wide * own_f, own_b + wide * got_b, own_d * got_d)


class Exchange:
    def __init__(self, total):
        self.count = lax.axis_size("seq")
        self.sent = total
        self.shape = (total.shape[1], LANES, LANES)
        self.distance = 1
        self.known = ()
        self.got = None

    def bit(self, distance):
        return (lax.axis_index("seq") // distance % 2).astype(jnp.int32)

    def swap(self):
        self.got = lax.ppermute(self.sent, "seq", [(i, i ^ self.distance) for i in range(self.count)])

    def finish(self, after):
        while not self.finished():
            combine([self], after)
            self.swap()
        near_in, near_out, after = lax.optimization_barrier((self.known[0], self.known[1], after))
        reach = self.known[2][:, :, None, :]
        upper = self.bit(self.distance) == 1
        far = self.got.astype(F32)
        enter = near_in.astype(F32) + jnp.where(upper, reach[0] * far, 0.0)
        leave = near_out.astype(F32) + jnp.where(upper, 0.0, reach[1] * far)
        return enter, leave, after

    def finished(self):
        return 2 * self.distance >= self.count

    def step(self):
        bits = jnp.stack([self.bit(self.distance), self.bit(2 * self.distance)])
        last = 4 * self.distance >= self.count
        shapes = [
            jax.ShapeDtypeStruct(self.shape if last else self.sent.shape, BF16),
            jax.ShapeDtypeStruct(self.shape, BF16),
            jax.ShapeDtypeStruct(self.shape, BF16),
            jax.ShapeDtypeStruct((2, self.shape[0], LANES), F32),
        ]
        return [bits, self.sent, self.got, *self.known], shapes, (not self.known, last)


def combine(exchanges, *after):
    steps = [e.step() for e in exchanges]
    operands = [value for step in steps for value in step[0]]
    shapes = [shape for step in steps for shape in step[1]]
    vmem, smem = pl.BlockSpec(memory_space=pltpu.VMEM), pl.BlockSpec(memory_space=pltpu.SMEM)

    def kernel(*refs):
        ins, outs = refs[: len(operands)], refs[len(operands) + len(after) :]
        for n, (values, _, form) in enumerate(steps):
            combine_kernel(*form, *ins[: len(values)], *outs[4 * n : 4 * n + 4])
            ins = ins[len(values) :]

    results = pl.pallas_call(
        kernel,
        in_specs=[spec for step in steps for spec in [smem] + [vmem] * (len(step[0]) - 1)]
        + [pl.BlockSpec(memory_space=pl.ANY)] * len(after),
        out_specs=[vmem] * len(shapes),
        out_shape=shapes,
        cost_estimate=cost(2),
        name="combine",
    )(*operands, *after)
    for n, e in enumerate(exchanges):
        e.sent, *e.known = results[4 * n : 4 * n + 4]
        e.distance *= 2


def passed_along(block, axis, distance):
    devices = range(lax.axis_size(axis))
    route = [(i - distance, i) for i in devices if i - distance in devices]
    return lax.ppermute(block, axis, route)


def swap_sum(value, axis):
    count = lax.axis_size(axis)
    distance = 1
    while distance < count:
        value = value + lax.ppermute(value, axis, [(i, i ^ distance) for i in range(count)])
        distance *= 2
    return value


SCALES_SPANS = 6
STATES_SPANS = 3
MAIN_SPANS = 1


def at_most(limit, spans):
    return max(n for n in range(1, limit + 1) if spans % n == 0)


def fixed(array):
    return pl.BlockSpec(array.shape, lambda i: (0,) * array.ndim)


def states_call(p, waits, x, halo, taps, write_in, parts, out_grad, read_in, e_m, df_m):
    count, heads_j, _ = x.shape
    spans = count // SPAN
    per = at_most(STATES_SPANS, spans)
    size = per * SPAN
    end = spans // per - 1
    def kernel(*refs):
        states_kernel(*refs[:10], *refs[10 + len(waits) :])

    return pl.pallas_call(
        kernel,
        grid=(spans // per,),
        in_specs=[
            pl.BlockSpec((size, heads_j, LANES), lambda i: (i, 0, p)),
            pl.BlockSpec((halo.shape[0], heads_j, LANES), lambda i: (0, 0, p)),
            pl.BlockSpec((4, heads_j, LANES), lambda i: (0, 0, p)),
            pl.BlockSpec((size, 2 * LANES), lambda i: (i, p)),
            pl.BlockSpec((1, size, LANES), lambda i: (p, i, 0)),
            pl.BlockSpec((size, heads_j, LANES), lambda i: (end - i, 0, p)),
            pl.BlockSpec((size, 2 * LANES), lambda i: (end - i, p)),
            pl.BlockSpec((1, size, LANES), lambda i: (p, end - i, 0)),
            fixed(e_m), fixed(df_m),
        ] + [pl.BlockSpec(memory_space=pl.ANY)] * len(waits),
        out_specs=[
            pl.BlockSpec((heads_j, per, SPAN, LANES), lambda i: (0, i, 0, 0)),
            pl.BlockSpec((heads_j, per, SPAN, LANES), lambda i: (0, i, 0, 0)),
            pl.BlockSpec((per, heads_j, LANES, LANES), lambda i: (i, 0, 0, 0)),
            pl.BlockSpec((per, heads_j, LANES, LANES), lambda i: (end - i, 0, 0, 0)),
            pl.BlockSpec((per, heads_j, EDGE, LANES), lambda i: (i, 0, 0, 0)),
            pl.BlockSpec((per, heads_j, EDGE, LANES), lambda i: (end - i, 0, 0, 0)),
            pl.BlockSpec((2, heads_j, LANES + EDGE, LANES), lambda i: (0, 0, 0, 0)),
        ],
        out_shape=[
            jax.ShapeDtypeStruct((heads_j, spans, SPAN, LANES), BF16),
            jax.ShapeDtypeStruct((heads_j, spans, SPAN, LANES), BF16),
            jax.ShapeDtypeStruct((spans, heads_j, LANES, LANES), BF16),
            jax.ShapeDtypeStruct((spans, heads_j, LANES, LANES), BF16),
            jax.ShapeDtypeStruct((spans, heads_j, EDGE, LANES), F32),
            jax.ShapeDtypeStruct((spans, heads_j, EDGE, LANES), F32),
            jax.ShapeDtypeStruct((2, heads_j, LANES + EDGE, LANES), BF16),
        ],
        scratch_shapes=[
            pltpu.VMEM((heads_j, size + EDGE, LANES), F32),
            pltpu.VMEM((heads_j, LANES, LANES), F32),
            pltpu.VMEM((heads_j, LANES, LANES), F32),
            pltpu.VMEM((heads_j, EDGE, LANES), F32),
            pltpu.VMEM((heads_j, EDGE, LANES), F32),
        ],
        cost_estimate=cost(9),
        name=f"states{p}",
    )(x, halo, taps, write_in, parts, out_grad, read_in, parts, e_m, df_m, *waits)


def main_call(
    p, waits, core, x, value, slope, out_grad, write_in, read_in, parts, rows, s_loc, r_loc, enter,
    leave, from_start, to_end, taps, skips, heads_m, a_m, dt_m, mixed, dx,
):
    count, heads_j, _ = x.shape
    spans = count // SPAN
    per = at_most(MAIN_SPANS, spans)
    size = per * SPAN
    last = spans // per - 1
    operands = [core, x, value, slope, out_grad, write_in, read_in, parts, rows, s_loc, r_loc,
                enter, leave, from_start, to_end, taps, skips, heads_m, a_m, dt_m, *waits]
    time3 = pl.BlockSpec((size, heads_j, LANES), lambda i: (last - i, 0, p))
    time2 = pl.BlockSpec((size, 2 * LANES), lambda i: (last - i, p))
    own3 = pl.BlockSpec((heads_j, per, SPAN, LANES), lambda i: (0, last - i, 0, 0))
    own2 = pl.BlockSpec((size, 2 * LANES), lambda i: (last - i, 0))
    state = pl.BlockSpec((per, heads_j, LANES, LANES), lambda i: (last - i, 0, 0, 0))
    lane_row = pl.BlockSpec((per, heads_j, EDGE, LANES), lambda i: (last - i, 0, 0, 0))
    in_specs = [
        pl.BlockSpec(memory_space=pltpu.SMEM), time3, own3, own3, time3, time2, time2,
        pl.BlockSpec((1, size, LANES), lambda i: (p, last - i, 0)),
        pl.BlockSpec((per, rows.shape[1], SPAN), lambda i: (last - i, 0, 0)),
        state, state, fixed(enter), fixed(leave), lane_row, lane_row,
        pl.BlockSpec((4, heads_j, LANES), lambda i: (0, 0, p)),
        pl.BlockSpec((heads_j, LANES), lambda i: (0, p)),
        fixed(heads_m), fixed(a_m), fixed(dt_m),
    ] + [pl.BlockSpec(memory_space=pl.ANY)] * len(waits)
    aliases = {}
    if mixed is not None:
        aliases = {len(operands): 0, len(operands) + 1: 1}
        operands += [mixed, dx]
        in_specs += [pl.BlockSpec(memory_space=pl.ANY)] * 2
    return pl.pallas_call(
        functools.partial(main_kernel, 2 * p),
        grid=(spans // per,),
        in_specs=in_specs,
        out_specs=[
            time3, time3, own2, own2,
            pl.BlockSpec((5, heads_j, LANES), lambda i: (0, 0, 0)),
            pl.BlockSpec((heads_j, EDGE, LANES), lambda i: (0, 0, 0)),
        ],
        out_shape=[
            jax.ShapeDtypeStruct(x.shape, BF16),
            jax.ShapeDtypeStruct(x.shape, BF16),
            jax.ShapeDtypeStruct((count, 2 * LANES), BF16),
            jax.ShapeDtypeStruct((count, 2 * LANES), BF16),
            jax.ShapeDtypeStruct((5, heads_j, LANES), F32),
            jax.ShapeDtypeStruct((heads_j, EDGE, LANES), F32),
        ],
        scratch_shapes=[
            pltpu.VMEM((heads_j, SPAN + EDGE, LANES), F32),
            pltpu.VMEM((5, heads_j, EDGE, LANES), F32),
        ],
        input_output_aliases=aliases,
        cost_estimate=cost(20),
        name=f"main{p}",
    )(*operands)


def on_device(x, taps, step_size, decay_log, write_in, read_in, skip_gain, out_grad):
    count, heads_j, width = x.shape
    groups = decay_log.shape[1]
    pairs = groups // 2
    spans = count // SPAN
    heads = 2 * heads_j
    rim = taps.shape[0] - 1
    n_head = lax.axis_size("head")
    core = (lax.axis_index("head") % 2).astype(jnp.int32).reshape(1)
    per = at_most(SCALES_SPANS, spans)
    gather = jnp.asarray(gather_matrix(heads_j, groups), BF16)
    parts, rows = pl.pallas_call(
        scales_kernel,
        grid=(spans // per,),
        in_specs=[
            pl.BlockSpec((heads_j * groups, per * SPAN), lambda i: (0, i)),
            pl.BlockSpec((heads_j, groups), lambda i: (0, 0)),
            pl.BlockSpec(gather.shape, lambda i: (0, 0)),
        ],
        out_specs=[
            pl.BlockSpec((pairs, per * SPAN, LANES), lambda i: (0, i, 0)),
            pl.BlockSpec((per, heads_j * groups, SPAN), lambda i: (i, 0, 0)),
        ],
        out_shape=[
            jax.ShapeDtypeStruct((pairs, count, LANES), BF16),
            jax.ShapeDtypeStruct((spans, heads_j * groups, SPAN), F32),
        ],
        cost_estimate=cost(4),
        name="scales",
    )(
        jnp.transpose(step_size, (1, 2, 0)).reshape(heads_j * groups, count),
        decay_log,
        gather,
    )
    rim_in, parts = lax.optimization_barrier((x[count - rim :], parts))
    halo = passed_along(rim_in, "seq", 1)
    skips = jnp.broadcast_to(skip_gain[:, :, None], (heads_j, groups, HALF)).reshape(heads_j, width)
    a_m, dt_m, e_m, df_m = (jnp.asarray(spread_matrix(q, heads_j), BF16) for q in range(4))
    heads_m = jnp.asarray(head_matrix(heads_j), BF16)

    values, slopes, s_all, r_all, froms, tos = [], [], [], [], [], []
    exchanges = []

    def boundary(token, *others):
        moved = [e for e in exchanges if not e.finished()]
        if moved:
            combine(moved, token)
        tied = lax.optimization_barrier((token, *[e.sent for e in moved], *others))
        for e, value in zip(moved, tied[1:]):
            e.sent = value
            e.swap()
        return [tied[0], *[e.sent for e in moved]], tied[len(tied) - len(others) :]

    waits = []
    for p in range(pairs):
        u, slope, s_loc, r_loc, from_start, to_end, total = states_call(
            p, waits, x, halo, taps, write_in, parts, out_grad, read_in, e_m, df_m
        )
        ready = exchanges[0].finish(from_start) if p == pairs - 1 else ()
        waits, (total, *ready) = boundary(from_start, total, *ready)
        exchanges.append(Exchange(total))
        exchanges[-1].swap()
        values.append(u)
        slopes.append(slope)
        s_all.append(s_loc)
        r_all.append(r_loc)
        froms.append(from_start)
        tos.append(to_end)

    mixed = dx = None
    cores = [(i, i ^ 1) for i in range(n_head)]
    sums, edges, arrived, summed = [], [], [], []
    for p in range(pairs):
        enter, leave, token = ready
        mixed, dx, keep, send, total, edge = main_call(
            p, [*waits, token], core, x, values[p], slopes[p], out_grad, write_in, read_in, parts, rows, s_all[p], r_all[p], enter,
            leave, froms[p], tos[p], taps, skips, heads_m, a_m, dt_m, mixed, dx,
        )
        sums.append(total)
        edges.append(edge)
        ready = exchanges[p + 1].finish(edge) if p < pairs - 1 else ()
        waits, (send, *tied) = boundary(edge, send, *ready, *arrived)
        ready = tied[: len(ready)]
        if summed:
            summed[-1] = tied[-1]
        mine = keep + lax.ppermute(send, "head", cores)
        waits.append(mine)
        arrived = []
        distance = 2
        while distance < n_head:
            got = lax.ppermute(mine, "head", [(i, i ^ distance) for i in range(n_head)])
            if p == pairs - 1 and 2 * distance >= n_head:
                break
            mine = mine + got
            distance *= 2
        arrived.append(mine)
        if p < pairs - 1:
            summed.append(mine)

    edge = jnp.transpose(jnp.concatenate(edges, axis=-1)[:, :rim, :], (1, 0, 2))
    after = passed_along(edge, "seq", -1)
    before = halo.astype(F32)
    sums = jnp.concatenate(sums, axis=-1)
    extra = []
    for tap in range(5):
        piece = jnp.zeros_like(sums[0])
        for row in range(rim - tap):
            piece = piece + edge[row] * before[row + tap]
        extra.append(piece)
    sums = swap_sum(sums + jnp.stack(extra), "seq")
    others = [lax.ppermute(value, "head", cores) for value in summed]
    write_grad, read_grad, token = place_call(core, summed, others, after, None, None, 0, count, groups)
    got, token, sums = lax.optimization_barrier((got, token, sums))
    mine = mine + got
    other = lax.ppermute(mine, "head", cores)
    write_grad, read_grad, _ = place_call(core, [mine], [other], token, write_grad, read_grad, pairs - 1, count, groups)
    tail_spec = pl.BlockSpec((EDGE, heads_j, width), lambda i: (count // EDGE - 1, 0, 0))
    dx = pl.pallas_call(
        edge_kernel,
        grid=(1,),
        in_specs=[fixed(after), fixed(taps), tail_spec],
        out_specs=tail_spec,
        out_shape=jax.ShapeDtypeStruct(x.shape, BF16),
        input_output_aliases={2: 0},
        cost_estimate=cost(1),
        name="edge",
    )(after, taps, dx)
    conv_grad = sums[:4]
    decay_grad = LN2 * sums[4].reshape(heads_j, groups, HALF).sum(-1)
    return (mixed, dx, conv_grad, decay_grad, write_grad, read_grad)


def solution(mesh):
    return jax.shard_map(
        on_device,
        mesh=mesh,
        in_specs=(
            P("seq", "head", None),
            P(None, "head", None),
            P("seq", "head", None),
            P("head", None),
            P("seq", None),
            P("seq", None),
            P("head", None),
            P("seq", "head", None),
        ),
        out_specs=(
            P("seq", "head", None),
            P("seq", "head", None),
            P(None, "head", None),
            P("head", None),
            P("seq", None),
            P("seq", None),
        ),
        check_vma=False,
    )
```

```python
import functools

import jax
import jax.numpy as jnp
import numpy as np
from jax import lax
from jax.experimental import pallas as pl
from jax.experimental.pallas import tpu as pltpu
from jax.sharding import PartitionSpec as P

SPAN = 128
LANES = 128
HALF = 64
EDGE = 8
F32 = jnp.float32
BF16 = jnp.bfloat16
NT = (((1,), (1,)), ((), ()))
TN = (((0,), (0,)), ((), ()))
LOG2E = 1.4426950408889634
LN2 = 0.6931471805599453
PARTS = (3, 2, 2, 2)


def cost(microseconds):
    return pl.CostEstimate(flops=int(microseconds * 1.15e9), transcendentals=0, bytes_accessed=0)


def dot(a, b, dims=None):
    if dims is None:
        return jnp.dot(a, b, preferred_element_type=F32)
    return lax.dot_general(a, b, dims, preferred_element_type=F32)


def low_half(rows):
    return lax.broadcasted_iota(jnp.int32, (rows, LANES), 1) < HALF


def split_parts(value, count):
    parts = []
    for _ in range(count - 1):
        part = value.astype(BF16)
        parts.append(part)
        value = value - part.astype(F32)
    parts.append(value.astype(BF16))
    return parts


def part_lane(quantity, part, head, heads):
    return (sum(PARTS[:quantity]) + part) * heads + head


def gather_matrix(heads_j, groups):
    heads, pairs, count = 2 * heads_j, groups // 2, sum(PARTS)
    matrix = np.zeros((count * heads_j * groups, pairs * LANES), np.float32)
    for part in range(count):
        for j in range(heads_j):
            for g in range(groups):
                matrix[part * heads_j * groups + j * groups + g, (g // 2) * LANES + part * heads + 2 * j + g % 2] = 1.0
    return matrix


def spread_matrix(quantity, heads_j):
    heads = 2 * heads_j
    matrix = np.zeros((LANES, heads_j * LANES), np.float32)
    for part in range(PARTS[quantity]):
        for h in range(heads):
            matrix[part_lane(quantity, part, h, heads), h * HALF : (h + 1) * HALF] = 1.0
    return matrix


def head_matrix(heads_j):
    heads = 2 * heads_j
    matrix = np.zeros((LANES, heads * LANES), np.float32)
    for part in range(PARTS[0]):
        for h in range(heads):
            matrix[part_lane(0, part, h, heads), h * LANES : (h + 1) * LANES] = 1.0
    return matrix


def scales_kernel(dt_ref, log_ref, gather_ref, parts_ref, rows_ref):
    every, count = dt_ref.shape
    heads_j, groups = log_ref.shape
    logs = log_ref[...]
    own = lax.broadcasted_iota(jnp.int32, (groups, groups), 0) == lax.broadcasted_iota(jnp.int32, (groups, groups), 1)
    logs = [jnp.sum(jnp.where(own, logs[j : j + 1], 0.0), axis=1, keepdims=True) for j in range(heads_j)]
    rates = -LOG2E * jnp.exp(jnp.concatenate(logs, axis=0))
    upper = (
        lax.broadcasted_iota(jnp.int32, (SPAN, SPAN), 0) <= lax.broadcasted_iota(jnp.int32, (SPAN, SPAN), 1)
    ).astype(BF16)
    for at in range(0, count, SPAN):
        dt = dt_ref[:, at : at + SPAN]
        summed = dot(jnp.concatenate(split_parts(dt * rates, 3), axis=0), upper)
        cumul = summed[:every] + summed[every : 2 * every] + summed[2 * every :]
        tail = jnp.exp2(cumul[:, SPAN - 1 : SPAN] - cumul)
        parts = []
        for value, number in zip((cumul, dt, jnp.exp2(cumul), dt * tail), PARTS, strict=True):
            parts += split_parts(value, number)
        placed = dot(jnp.concatenate(parts, axis=0), gather_ref[...], TN).astype(BF16)
        for p in range(parts_ref.shape[0]):
            parts_ref[p, at : at + SPAN, :] = placed[:, p * LANES : (p + 1) * LANES]
        rows_ref[at // SPAN] = cumul


def states_kernel(
    x_ref, halo_ref, w_ref, b_ref, partf_ref, y_ref, c_ref, partr_ref, lead_ref, tail_ref,
    u_ref, slope_ref, s_ref, r_ref, from_ref, to_ref, total_ref, x_buf, s_acc, r_acc, f_acc, t_acc,
):
    step = pl.program_id(0)
    rows, heads_j, _ = x_ref.shape
    low = low_half(SPAN)

    @pl.when(step == 0)
    def _():
        s_acc[...] = jnp.zeros_like(s_acc)
        r_acc[...] = jnp.zeros_like(r_acc)
        f_acc[...] = jnp.ones_like(f_acc)
        t_acc[...] = jnp.ones_like(t_acc)
        halo = halo_ref[...].astype(F32)
        for j in range(heads_j):
            for row in range(3):
                x_buf[j, EDGE - 3 + row : EDGE - 2 + row, :] = halo[row, j : j + 1, :]

    @pl.when(step > 0)
    def _():
        x_buf[:, 0:EDGE, :] = x_buf[:, rows : rows + EDGE, :]

    x_buf[:, EDGE : EDGE + rows, :] = jnp.swapaxes(x_ref[...], 0, 1).astype(F32)
    weights = w_ref[...]
    number = rows // SPAN
    def one(k):
        m = number - 1 - k
        start = k * SPAN
        here = pl.ds(start, SPAN)
        there = pl.ds(m * SPAN, SPAN)
        grads_all = jnp.swapaxes(y_ref[there], 0, 1)
        partf = partf_ref[0, here, :]
        tails = dot(partf, tail_ref[...])
        leads = dot(jnp.concatenate([partr_ref[0, there, :], partf[SPAN - EDGE :]], axis=0), lead_ref[...])
        s_ref[k] = s_acc[...].astype(BF16)
        r_ref[m] = r_acc[...].astype(BF16)
        from_ref[k] = f_acc[...]
        to_ref[m] = t_acc[...]
        wrote, read = [], []
        for j in range(heads_j):
            lanes = slice(j * LANES, (j + 1) * LANES)
            at = start + EDGE - 3
            v = 0.5 * weights[0, j : j + 1, :] * x_buf[j, at : at + SPAN, :]
            for tap in range(1, 4):
                v = v + 0.5 * weights[tap, j : j + 1, :] * x_buf[j, at + tap : at + tap + SPAN, :]
            gate = 1.0 + jnp.tanh(v)
            u = v * gate
            u_ref[j, k] = u.astype(BF16)
            slope_ref[j, k] = (gate + u * (2.0 - gate)).astype(BF16)
            wrote.append((u * tails[:, lanes]).astype(BF16))
            read.append((grads_all[j].astype(F32) * leads[:SPAN, lanes]).astype(BF16))
        own_s = dot(b_ref[here, :], jnp.concatenate(wrote, axis=1), TN)
        own_r = dot(c_ref[there, :], jnp.concatenate(read, axis=1), TN)
        for j in range(heads_j):
            lanes = slice(j * LANES, (j + 1) * LANES)
            keep = leads[SPAN + EDGE - 1 : SPAN + EDGE, lanes]
            s_acc[j] = keep * s_acc[j] + jnp.where(low, own_s[:LANES, lanes], own_s[LANES:, lanes])
            f_acc[j] = f_acc[j] * keep
            keep = leads[SPAN - 1 : SPAN, lanes]
            r_acc[j] = keep * r_acc[j] + jnp.where(low, own_r[:LANES, lanes], own_r[LANES:, lanes])
            t_acc[j] = t_acc[j] * keep

    for turn in range(number):
        one(turn)

    @pl.when(step == pl.num_programs(0) - 1)
    def _():
        total_ref[0, :, :LANES, :] = s_acc[...].astype(BF16)
        total_ref[1, :, :LANES, :] = r_acc[...].astype(BF16)
        for j in range(heads_j):
            decay = f_acc[j][0:1]
            high = decay.astype(BF16).astype(F32)
            pair = jnp.concatenate([high, decay - high, jnp.zeros((6, LANES), F32)], axis=0)
            total_ref[0, j, LANES:, :] = pair.astype(BF16)
            total_ref[1, j, LANES:, :] = pair.astype(BF16)


def fold(value):
    return jnp.sum(value.reshape(value.shape[0] // 8, 8, value.shape[1]), axis=0)


def main_kernel(
    head0, core_ref, x_ref, u_ref, slope_ref, y_ref, b_ref, c_ref, part_ref, row_ref, s_ref, r_ref,
    enter_ref, leave_ref, from_ref, to_ref, w_ref, skip_ref, heads_ref, a_ref, dt_ref, *rest,
):
    mixed_ref, dx_ref, keep_ref, send_ref, sums_ref, edge_ref, dv_buf, acc = rest[-8:]
    step = pl.program_id(0)
    size, heads_j, _ = x_ref.shape
    span = SPAN
    number = size // span
    groups = row_ref.shape[1] // heads_j
    low = low_half(span)
    causal = lax.broadcasted_iota(jnp.int32, (span, span), 0) >= lax.broadcasted_iota(
        jnp.int32, (span, span), 1
    )

    @pl.when(step == 0)
    def _():
        acc[...] = jnp.zeros_like(acc)
        dv_buf[:, 0:EDGE, :] = jnp.zeros((heads_j, EDGE, LANES), F32)

    def one(turn, nothing):
        k = number - 1 - turn
        base = pl.multiple_of(k * span, span)
        dv_buf[:, span : span + EDGE, :] = dv_buf[:, 0:EDGE, :]
        here = pl.ds(base, span)
        xs = jnp.swapaxes(x_ref[here], 0, 1)
        grads = jnp.swapaxes(y_ref[here], 0, 1)
        b_all = b_ref[here, :]
        c_all = c_ref[here, :]
        weights = w_ref[...]
        skips = skip_ref[...]
        part = part_ref[0, here, :]
        zero = jnp.zeros((span, LANES), BF16)
        def diagonal(array):
            return jnp.concatenate(
                [jnp.concatenate([array[:, :LANES], zero], axis=1), jnp.concatenate([zero, array[:, LANES:]], axis=1)],
                axis=0,
            )

        b_diag = diagonal(b_all)
        scores16 = dot(c_all, b_diag, NT).astype(BF16)
        a_all = dot(part, a_ref[...])
        dt_all = dot(part, dt_ref[...])
        score_grads = [None, None]
        logs = row_ref[k]
        states, rstates, state_cat, rstate_cat = [], [], [], []
        for j in range(heads_j):
            state = s_ref[k, j].astype(F32) + from_ref[k, j][0:1] * enter_ref[j]
            rstate = r_ref[k, j].astype(F32) + to_ref[k, j][0:1] * leave_ref[j]
            states.append(fold(state * rstate))
            state = state.astype(BF16)
            rstate = rstate.astype(BF16)
            state_cat.append(jnp.concatenate([jnp.where(low, state, zero), jnp.where(low, zero, state)], axis=0))
            rstate_cat.append(jnp.concatenate([jnp.where(low, rstate, zero), jnp.where(low, zero, rstate)], axis=0))
        state_cat = jnp.concatenate(state_cat, axis=1)
        rstate_cat = jnp.concatenate(rstate_cat, axis=1)
        out_rows, leads, tails = [], [], []
        for j in range(heads_j):
            lanes = slice(j * LANES, (j + 1) * LANES)
            a_b = a_all[:, lanes]
            dt_b = dt_all[:, lanes]
            a_last = a_b[span - 1 : span]
            e_b = jnp.exp2(a_b)
            f_b = jnp.exp2(a_last - a_b)
            e_last = e_b[span - 1 : span]
            heads_b = dot(part, heads_ref[:, 2 * j * LANES : 2 * (j + 1) * LANES])
            u = u_ref[j, k].astype(F32)
            dy = grads[j].astype(F32)
            dy16 = dy.astype(BF16)
            val16 = (u * dt_b).astype(BF16)
            val = val16.astype(F32)
            tails.append((val * f_b).astype(BF16))
            leads.append((dy * e_b).astype(BF16))
            dy_two = jnp.concatenate([jnp.where(low, dy16, zero), jnp.where(low, zero, dy16)], axis=0)
            val_two = jnp.concatenate([jnp.where(low, val16, zero), jnp.where(low, zero, val16)], axis=0)
            products = dot(dy16, val_two, NT)
            mixes = []
            for g in range(2):
                at = j * groups + head0 + g
                inside = slice(g * LANES, (g + 1) * LANES)
                spread = heads_b[:, inside] - logs[at : at + 1]
                decay = jnp.exp2(jnp.where(causal, spread, -jnp.inf))
                mixes.append(scores16[:, inside] * decay.astype(BF16))
                weighted = decay * products[:, inside]
                score_grads[g] = weighted if score_grads[g] is None else score_grads[g] + weighted
            inner = dot(jnp.concatenate(mixes, axis=1), val_two)
            dval = dot(jnp.concatenate(mixes, axis=0), dy_two, TN)
            carried = dot(c_all, state_cat[:, lanes]) * e_b
            back = dot(b_all, rstate_cat[:, lanes]) * f_b
            out = inner + carried
            dval_full = dval + back
            log_part = a_b * (dy * out - val * dval_full)
            acc[4, j] = acc[4, j] + fold(log_part) + fold(val * back) * a_last + states[j] * (a_last * e_last)
            skip = skips[j : j + 1, :]
            out_rows.append((out + skip * u).astype(BF16))
            dv_buf[j, 0:span, :] = (dt_b * dval_full + skip * dy) * (0.5 * slope_ref[j, k].astype(F32))
        mixed_ref[here] = jnp.swapaxes(jnp.stack(out_rows, axis=0), 0, 1)
        dc_inter = dot(jnp.concatenate(leads, axis=1), state_cat, NT)
        db_inter = dot(jnp.concatenate(tails, axis=1), rstate_cat, NT)
        dx_rows = []
        for j in range(heads_j):
            x = xs[j].astype(F32)
            total = None
            for tap in range(4):
                shifted = dv_buf[j, 3 - tap : 3 - tap + span, :]
                piece = weights[tap, j : j + 1, :] * shifted
                total = piece if total is None else total + piece
                acc[tap, j] = acc[tap, j] + fold(shifted * x)
            dx_rows.append(total.astype(BF16))
        dx_ref[here] = jnp.swapaxes(jnp.stack(dx_rows, axis=0), 0, 1)
        flows = [flow.astype(BF16) for flow in score_grads]
        dc = (dot(jnp.concatenate(flows, axis=1), b_diag) + dc_inter).astype(BF16)
        db = (dot(jnp.concatenate(flows, axis=0), diagonal(c_all), TN) + db_inter).astype(BF16)

        @pl.when(core_ref[0] == 0)
        def _():
            keep_ref[here, :] = db
            send_ref[here, :] = dc

        @pl.when(core_ref[0] != 0)
        def _():
            keep_ref[here, :] = dc
            send_ref[here, :] = db

        return nothing

    lax.fori_loop(0, number, one, 0)

    @pl.when(step == pl.num_programs(0) - 1)
    def _():
        edge_ref[...] = dv_buf[:, 0:EDGE, :]
        for tap in range(5):
            for j in range(heads_j):
                sums_ref[tap, j : j + 1, :] = jnp.sum(acc[tap, j], axis=0, keepdims=True)


def place_kernel(number, core_ref, *refs):
    mine, got = refs[:number], refs[number : 2 * number]
    write_ref, read_ref, token_ref = refs[-3:]
    token_ref[...] = jnp.zeros_like(token_ref)

    @pl.when(core_ref[0] == 0)
    def _():
        for n in range(number):
            lanes = slice(2 * n * LANES, 2 * (n + 1) * LANES)
            write_ref[:, lanes] = mine[n][...]
            read_ref[:, lanes] = got[n][...]

    @pl.when(core_ref[0] != 0)
    def _():
        for n in range(number):
            lanes = slice(2 * n * LANES, 2 * (n + 1) * LANES)
            write_ref[:, lanes] = got[n][...]
            read_ref[:, lanes] = mine[n][...]


def place_call(core, mine, got, token, write_grad, read_grad, at, count, groups):
    number = len(mine)
    rows = at_most(4, count // SPAN) * SPAN
    anywhere = pl.BlockSpec(memory_space=pl.ANY)
    block = pl.BlockSpec((rows, 2 * LANES), lambda i: (i, 0))
    operands = [core, *mine, *got, token]
    in_specs = [pl.BlockSpec(memory_space=pltpu.SMEM)] + [block] * (2 * number) + [anywhere]
    aliases = {}
    if write_grad is not None:
        aliases = {len(operands): 0, len(operands) + 1: 1}
        operands += [write_grad, read_grad]
        in_specs += [anywhere] * 2
    return pl.pallas_call(
        functools.partial(place_kernel, number),
        grid=(count // rows,),
        in_specs=in_specs,
        out_specs=[pl.BlockSpec((rows, 2 * number * LANES), lambda i: (i, at))] * 2
        + [pl.BlockSpec((EDGE, LANES), lambda i: (0, 0))],
        out_shape=[jax.ShapeDtypeStruct((count, groups * LANES), BF16)] * 2 + [jax.ShapeDtypeStruct((EDGE, LANES), F32)],
        input_output_aliases=aliases,
        cost_estimate=cost(2 * number),
        name="place",
    )(*operands)


def edge_kernel(after_ref, w_ref, dx_ref, out_ref):
    rows = dx_ref.shape[0]
    weights = w_ref[...]
    after = after_ref[...]
    out_ref[: rows - 3] = dx_ref[: rows - 3]
    for row in range(3):
        fix = weights[0] * after[row]
        for tap in range(1, row + 1):
            fix = fix + weights[tap] * after[row - tap]
        at = rows - 3 + row
        out_ref[at] = (dx_ref[at].astype(F32) + fix).astype(BF16)


def halves_of(ref):
    decay = ref[0, :, LANES, :].astype(F32) + ref[0, :, LANES + 1, :].astype(F32)
    return ref[0, :, :LANES, :].astype(F32), ref[1, :, :LANES, :].astype(F32), decay


def combine_kernel(first, last, bits_ref, mine_ref, got_ref, *refs):
    if not first:
        enter_ref, leave_ref, reach_ref = refs[:3]
    send_ref, enter_out, leave_out, reach_out = refs[-4:]

    def write(forward, backward, decay):
        if last:

            @pl.when(bits_ref[1] == 1)
            def _():
                send_ref[...] = backward.astype(BF16)

            @pl.when(bits_ref[1] == 0)
            def _():
                send_ref[...] = forward.astype(BF16)
        else:
            high = decay.astype(BF16).astype(F32)
            send_ref[0, :, :LANES, :] = forward.astype(BF16)
            send_ref[1, :, :LANES, :] = backward.astype(BF16)
            zeros = jnp.zeros((6, LANES), F32)
            for j in range(decay.shape[0]):
                rows = jnp.concatenate([high[j : j + 1], decay[j : j + 1] - high[j : j + 1], zeros], axis=0)
                send_ref[0, j, LANES:, :] = rows.astype(BF16)
                send_ref[1, j, LANES:, :] = rows.astype(BF16)

    own_f, own_b, own_d = halves_of(mine_ref)
    got_f, got_b, got_d = halves_of(got_ref)
    wide, got_wide = own_d[:, None, :], got_d[:, None, :]

    @pl.when(bits_ref[0] == 1)
    def _():
        if first:
            enter_out[...] = got_f.astype(BF16)
            leave_out[...] = jnp.zeros_like(leave_out)
            reach_out[0] = got_d
            reach_out[1] = jnp.ones_like(got_d)
        else:
            enter_out[...] = (enter_ref[...].astype(F32) + reach_ref[0][:, None, :] * got_f).astype(BF16)
            leave_out[...] = leave_ref[...]
            reach_out[0] = reach_ref[0] * got_d
            reach_out[1] = reach_ref[1]
        write(own_f + wide * got_f, got_b + got_wide * own_b, own_d * got_d)

    @pl.when(bits_ref[0] == 0)
    def _():
        if first:
            enter_out[...] = jnp.zeros_like(enter_out)
            leave_out[...] = got_b.astype(BF16)
            reach_out[0] = jnp.ones_like(got_d)
            reach_out[1] = got_d
        else:
            enter_out[...] = enter_ref[...]
            leave_out[...] = (leave_ref[...].astype(F32) + reach_ref[1][:, None, :] * got_b).astype(BF16)
            reach_out[0] = reach_ref[0]
            reach_out[1] = reach_ref[1] * got_d
        write(got_f + got_wide * own_f, own_b + wide * got_b, own_d * got_d)


class Exchange:
    def __init__(self, total):
        self.count = lax.axis_size("seq")
        self.sent = total
        self.shape = (total.shape[1], LANES, LANES)
        self.distance = 1
        self.known = ()
        self.got = None

    def bit(self, distance):
        return (lax.axis_index("seq") // distance % 2).astype(jnp.int32)

    def swap(self):
        self.got = lax.ppermute(self.sent, "seq", [(i, i ^ self.distance) for i in range(self.count)])

    def finish(self, after):
        while not self.finished():
            combine([self], after)
            self.swap()
        near_in, near_out, after = lax.optimization_barrier((self.known[0], self.known[1], after))
        reach = self.known[2][:, :, None, :]
        upper = self.bit(self.distance) == 1
        far = self.got.astype(F32)
        enter = near_in.astype(F32) + jnp.where(upper, reach[0] * far, 0.0)
        leave = near_out.astype(F32) + jnp.where(upper, 0.0, reach[1] * far)
        return enter, leave, after

    def finished(self):
        return 2 * self.distance >= self.count

    def step(self):
        bits = jnp.stack([self.bit(self.distance), self.bit(2 * self.distance)])
        last = 4 * self.distance >= self.count
        shapes = [
            jax.ShapeDtypeStruct(self.shape if last else self.sent.shape, BF16),
            jax.ShapeDtypeStruct(self.shape, BF16),
            jax.ShapeDtypeStruct(self.shape, BF16),
            jax.ShapeDtypeStruct((2, self.shape[0], LANES), F32),
        ]
        return [bits, self.sent, self.got, *self.known], shapes, (not self.known, last)


def combine(exchanges, *after):
    steps = [e.step() for e in exchanges]
    operands = [value for step in steps for value in step[0]]
    shapes = [shape for step in steps for shape in step[1]]
    vmem, smem = pl.BlockSpec(memory_space=pltpu.VMEM), pl.BlockSpec(memory_space=pltpu.SMEM)

    def kernel(*refs):
        ins, outs = refs[: len(operands)], refs[len(operands) + len(after) :]
        for n, (values, _, form) in enumerate(steps):
            combine_kernel(*form, *ins[: len(values)], *outs[4 * n : 4 * n + 4])
            ins = ins[len(values) :]

    results = pl.pallas_call(
        kernel,
        in_specs=[spec for step in steps for spec in [smem] + [vmem] * (len(step[0]) - 1)]
        + [pl.BlockSpec(memory_space=pl.ANY)] * len(after),
        out_specs=[vmem] * len(shapes),
        out_shape=shapes,
        cost_estimate=cost(2),
        name="combine",
    )(*operands, *after)
    for n, e in enumerate(exchanges):
        e.sent, *e.known = results[4 * n : 4 * n + 4]
        e.distance *= 2


def passed_along(block, axis, distance):
    devices = range(lax.axis_size(axis))
    route = [(i - distance, i) for i in devices if i - distance in devices]
    return lax.ppermute(block, axis, route)


def swap_sum(value, axis):
    count = lax.axis_size(axis)
    distance = 1
    while distance < count:
        value = value + lax.ppermute(value, axis, [(i, i ^ distance) for i in range(count)])
        distance *= 2
    return value


SCALES_SPANS = 6
STATES_SPANS = 3
MAIN_SPANS = 1


def at_most(limit, spans):
    return max(n for n in range(1, limit + 1) if spans % n == 0)


def fixed(array):
    return pl.BlockSpec(array.shape, lambda i: (0,) * array.ndim)


def states_call(p, waits, x, halo, taps, write_in, parts, out_grad, read_in, e_m, df_m):
    count, heads_j, _ = x.shape
    spans = count // SPAN
    per = at_most(STATES_SPANS, spans)
    size = per * SPAN
    end = spans // per - 1
    def kernel(*refs):
        states_kernel(*refs[:10], *refs[10 + len(waits) :])

    return pl.pallas_call(
        kernel,
        grid=(spans // per,),
        in_specs=[
            pl.BlockSpec((size, heads_j, LANES), lambda i: (i, 0, p)),
            pl.BlockSpec((halo.shape[0], heads_j, LANES), lambda i: (0, 0, p)),
            pl.BlockSpec((4, heads_j, LANES), lambda i: (0, 0, p)),
            pl.BlockSpec((size, 2 * LANES), lambda i: (i, p)),
            pl.BlockSpec((1, size, LANES), lambda i: (p, i, 0)),
            pl.BlockSpec((size, heads_j, LANES), lambda i: (end - i, 0, p)),
            pl.BlockSpec((size, 2 * LANES), lambda i: (end - i, p)),
            pl.BlockSpec((1, size, LANES), lambda i: (p, end - i, 0)),
            fixed(e_m), fixed(df_m),
        ] + [pl.BlockSpec(memory_space=pl.ANY)] * len(waits),
        out_specs=[
            pl.BlockSpec((heads_j, per, SPAN, LANES), lambda i: (0, i, 0, 0)),
            pl.BlockSpec((heads_j, per, SPAN, LANES), lambda i: (0, i, 0, 0)),
            pl.BlockSpec((per, heads_j, LANES, LANES), lambda i: (i, 0, 0, 0)),
            pl.BlockSpec((per, heads_j, LANES, LANES), lambda i: (end - i, 0, 0, 0)),
            pl.BlockSpec((per, heads_j, EDGE, LANES), lambda i: (i, 0, 0, 0)),
            pl.BlockSpec((per, heads_j, EDGE, LANES), lambda i: (end - i, 0, 0, 0)),
            pl.BlockSpec((2, heads_j, LANES + EDGE, LANES), lambda i: (0, 0, 0, 0)),
        ],
        out_shape=[
            jax.ShapeDtypeStruct((heads_j, spans, SPAN, LANES), BF16),
            jax.ShapeDtypeStruct((heads_j, spans, SPAN, LANES), BF16),
            jax.ShapeDtypeStruct((spans, heads_j, LANES, LANES), BF16),
            jax.ShapeDtypeStruct((spans, heads_j, LANES, LANES), BF16),
            jax.ShapeDtypeStruct((spans, heads_j, EDGE, LANES), F32),
            jax.ShapeDtypeStruct((spans, heads_j, EDGE, LANES), F32),
            jax.ShapeDtypeStruct((2, heads_j, LANES + EDGE, LANES), BF16),
        ],
        scratch_shapes=[
            pltpu.VMEM((heads_j, size + EDGE, LANES), F32),
            pltpu.VMEM((heads_j, LANES, LANES), F32),
            pltpu.VMEM((heads_j, LANES, LANES), F32),
            pltpu.VMEM((heads_j, EDGE, LANES), F32),
            pltpu.VMEM((heads_j, EDGE, LANES), F32),
        ],
        cost_estimate=cost(9),
        name=f"states{p}",
    )(x, halo, taps, write_in, parts, out_grad, read_in, parts, e_m, df_m, *waits)


def main_call(
    p, waits, core, x, value, slope, out_grad, write_in, read_in, parts, rows, s_loc, r_loc, enter,
    leave, from_start, to_end, taps, skips, heads_m, a_m, dt_m, mixed, dx,
):
    count, heads_j, _ = x.shape
    spans = count // SPAN
    per = at_most(MAIN_SPANS, spans)
    size = per * SPAN
    last = spans // per - 1
    operands = [core, x, value, slope, out_grad, write_in, read_in, parts, rows, s_loc, r_loc,
                enter, leave, from_start, to_end, taps, skips, heads_m, a_m, dt_m, *waits]
    time3 = pl.BlockSpec((size, heads_j, LANES), lambda i: (last - i, 0, p))
    time2 = pl.BlockSpec((size, 2 * LANES), lambda i: (last - i, p))
    own3 = pl.BlockSpec((heads_j, per, SPAN, LANES), lambda i: (0, last - i, 0, 0))
    own2 = pl.BlockSpec((size, 2 * LANES), lambda i: (last - i, 0))
    state = pl.BlockSpec((per, heads_j, LANES, LANES), lambda i: (last - i, 0, 0, 0))
    lane_row = pl.BlockSpec((per, heads_j, EDGE, LANES), lambda i: (last - i, 0, 0, 0))
    in_specs = [
        pl.BlockSpec(memory_space=pltpu.SMEM), time3, own3, own3, time3, time2, time2,
        pl.BlockSpec((1, size, LANES), lambda i: (p, last - i, 0)),
        pl.BlockSpec((per, rows.shape[1], SPAN), lambda i: (last - i, 0, 0)),
        state, state, fixed(enter), fixed(leave), lane_row, lane_row,
        pl.BlockSpec((4, heads_j, LANES), lambda i: (0, 0, p)),
        pl.BlockSpec((heads_j, LANES), lambda i: (0, p)),
        fixed(heads_m), fixed(a_m), fixed(dt_m),
    ] + [pl.BlockSpec(memory_space=pl.ANY)] * len(waits)
    aliases = {}
    if mixed is not None:
        aliases = {len(operands): 0, len(operands) + 1: 1}
        operands += [mixed, dx]
        in_specs += [pl.BlockSpec(memory_space=pl.ANY)] * 2
    return pl.pallas_call(
        functools.partial(main_kernel, 2 * p),
        grid=(spans // per,),
        in_specs=in_specs,
        out_specs=[
            time3, time3, own2, own2,
            pl.BlockSpec((5, heads_j, LANES), lambda i: (0, 0, 0)),
            pl.BlockSpec((heads_j, EDGE, LANES), lambda i: (0, 0, 0)),
        ],
        out_shape=[
            jax.ShapeDtypeStruct(x.shape, BF16),
            jax.ShapeDtypeStruct(x.shape, BF16),
            jax.ShapeDtypeStruct((count, 2 * LANES), BF16),
            jax.ShapeDtypeStruct((count, 2 * LANES), BF16),
            jax.ShapeDtypeStruct((5, heads_j, LANES), F32),
            jax.ShapeDtypeStruct((heads_j, EDGE, LANES), F32),
        ],
        scratch_shapes=[
            pltpu.VMEM((heads_j, SPAN + EDGE, LANES), F32),
            pltpu.VMEM((5, heads_j, EDGE, LANES), F32),
        ],
        input_output_aliases=aliases,
        cost_estimate=cost(20),
        name=f"main{p}",
    )(*operands)


def on_device(x, taps, step_size, decay_log, write_in, read_in, skip_gain, out_grad):
    count, heads_j, width = x.shape
    groups = decay_log.shape[1]
    pairs = groups // 2
    spans = count // SPAN
    heads = 2 * heads_j
    rim = taps.shape[0] - 1
    n_head = lax.axis_size("head")
    core = (lax.axis_index("head") % 2).astype(jnp.int32).reshape(1)
    per = at_most(SCALES_SPANS, spans)
    gather = jnp.asarray(gather_matrix(heads_j, groups), BF16)
    parts, rows = pl.pallas_call(
        scales_kernel,
        grid=(spans // per,),
        in_specs=[
            pl.BlockSpec((heads_j * groups, per * SPAN), lambda i: (0, i)),
            pl.BlockSpec((heads_j, groups), lambda i: (0, 0)),
            pl.BlockSpec(gather.shape, lambda i: (0, 0)),
        ],
        out_specs=[
            pl.BlockSpec((pairs, per * SPAN, LANES), lambda i: (0, i, 0)),
            pl.BlockSpec((per, heads_j * groups, SPAN), lambda i: (i, 0, 0)),
        ],
        out_shape=[
            jax.ShapeDtypeStruct((pairs, count, LANES), BF16),
            jax.ShapeDtypeStruct((spans, heads_j * groups, SPAN), F32),
        ],
        cost_estimate=cost(4),
        name="scales",
    )(
        jnp.transpose(step_size, (1, 2, 0)).reshape(heads_j * groups, count),
        decay_log,
        gather,
    )
    rim_in, parts = lax.optimization_barrier((x[count - rim :], parts))
    halo = passed_along(rim_in, "seq", 1)
    skips = jnp.broadcast_to(skip_gain[:, :, None], (heads_j, groups, HALF)).reshape(heads_j, width)
    a_m, dt_m, e_m, df_m = (jnp.asarray(spread_matrix(q, heads_j), BF16) for q in range(4))
    heads_m = jnp.asarray(head_matrix(heads_j), BF16)

    values, slopes, s_all, r_all, froms, tos = [], [], [], [], [], []
    exchanges = []

    def boundary(token, *others):
        moved = [e for e in exchanges if not e.finished()]
        if moved:
            combine(moved, token)
        tied = lax.optimization_barrier((token, *[e.sent for e in moved], *others))
        for e, value in zip(moved, tied[1:]):
            e.sent = value
            e.swap()
        return [tied[0], *[e.sent for e in moved]], tied[len(tied) - len(others) :]

    waits = []
    for p in range(pairs):
        u, slope, s_loc, r_loc, from_start, to_end, total = states_call(
            p, waits, x, halo, taps, write_in, parts, out_grad, read_in, e_m, df_m
        )
        ready = exchanges[0].finish(from_start) if p == pairs - 1 else ()
        waits, (total, *ready) = boundary(from_start, total, *ready)
        exchanges.append(Exchange(total))
        exchanges[-1].swap()
        values.append(u)
        slopes.append(slope)
        s_all.append(s_loc)
        r_all.append(r_loc)
        froms.append(from_start)
        tos.append(to_end)

    mixed = dx = None
    cores = [(i, i ^ 1) for i in range(n_head)]
    sums, edges, arrived, summed = [], [], [], []
    for p in range(pairs):
        enter, leave, token = ready
        mixed, dx, keep, send, total, edge = main_call(
            p, [*waits, token], core, x, values[p], slopes[p], out_grad, write_in, read_in, parts, rows, s_all[p], r_all[p], enter,
            leave, froms[p], tos[p], taps, skips, heads_m, a_m, dt_m, mixed, dx,
        )
        sums.append(total)
        edges.append(edge)
        ready = exchanges[p + 1].finish(edge) if p < pairs - 1 else ()
        waits, (send, *tied) = boundary(edge, send, *ready, *arrived)
        ready = tied[: len(ready)]
        if summed:
            summed[-1] = tied[-1]
        mine = keep + lax.ppermute(send, "head", cores)
        waits.append(mine)
        arrived = []
        distance = 2
        while distance < n_head:
            got = lax.ppermute(mine, "head", [(i, i ^ distance) for i in range(n_head)])
            if p == pairs - 1 and 2 * distance >= n_head:
                break
            mine = mine + got
            distance *= 2
        arrived.append(mine)
        if p < pairs - 1:
            summed.append(mine)

    edge = jnp.transpose(jnp.concatenate(edges, axis=-1)[:, :rim, :], (1, 0, 2))
    after = passed_along(edge, "seq", -1)
    before = halo.astype(F32)
    sums = jnp.concatenate(sums, axis=-1)
    extra = []
    for tap in range(5):
        piece = jnp.zeros_like(sums[0])
        for row in range(rim - tap):
            piece = piece + edge[row] * before[row + tap]
        extra.append(piece)
    sums = swap_sum(sums + jnp.stack(extra), "seq")
    others = [lax.ppermute(value, "head", cores) for value in summed]
    write_grad, read_grad, token = place_call(core, summed, others, edges[-1], None, None, 0, count, groups)
    got, token, sums, after = lax.optimization_barrier((got, token, sums, after))
    mine = mine + got
    other = lax.ppermute(mine, "head", cores)
    write_grad, read_grad, _ = place_call(core, [mine], [other], token, write_grad, read_grad, pairs - 1, count, groups)
    tail_spec = pl.BlockSpec((EDGE, heads_j, width), lambda i: (count // EDGE - 1, 0, 0))
    dx = pl.pallas_call(
        edge_kernel,
        grid=(1,),
        in_specs=[fixed(after), fixed(taps), tail_spec],
        out_specs=tail_spec,
        out_shape=jax.ShapeDtypeStruct(x.shape, BF16),
        input_output_aliases={2: 0},
        cost_estimate=cost(1),
        name="edge",
    )(after, taps, dx)
    conv_grad = sums[:4]
    decay_grad = LN2 * sums[4].reshape(heads_j, groups, HALF).sum(-1)
    return (mixed, dx, conv_grad, decay_grad, write_grad, read_grad)


def solution(mesh):
    return jax.shard_map(
        on_device,
        mesh=mesh,
        in_specs=(
            P("seq", "head", None),
            P(None, "head", None),
            P("seq", "head", None),
            P("head", None),
            P("seq", None),
            P("seq", None),
            P("head", None),
            P("seq", "head", None),
        ),
        out_specs=(
            P("seq", "head", None),
            P("seq", "head", None),
            P(None, "head", None),
            P("head", None),
            P("seq", None),
            P("seq", None),
        ),
        check_vma=False,
    )
```

```python
import functools

import jax
import jax.numpy as jnp
import numpy as np
from jax import lax
from jax.experimental import pallas as pl
from jax.experimental.pallas import tpu as pltpu
from jax.sharding import PartitionSpec as P

SPAN = 128
LANES = 128
HALF = 64
EDGE = 8
F32 = jnp.float32
BF16 = jnp.bfloat16
NT = (((1,), (1,)), ((), ()))
TN = (((0,), (0,)), ((), ()))
LOG2E = 1.4426950408889634
LN2 = 0.6931471805599453
PARTS = (3, 2, 2, 2)


def cost(microseconds):
    return pl.CostEstimate(flops=int(microseconds * 1.15e9), transcendentals=0, bytes_accessed=0)


def dot(a, b, dims=None):
    if dims is None:
        return jnp.dot(a, b, preferred_element_type=F32)
    return lax.dot_general(a, b, dims, preferred_element_type=F32)


def low_half(rows):
    return lax.broadcasted_iota(jnp.int32, (rows, LANES), 1) < HALF


def split_parts(value, count):
    parts = []
    for _ in range(count - 1):
        part = value.astype(BF16)
        parts.append(part)
        value = value - part.astype(F32)
    parts.append(value.astype(BF16))
    return parts


def part_lane(quantity, part, head, heads):
    return (sum(PARTS[:quantity]) + part) * heads + head


def gather_matrix(heads_j, groups):
    heads, pairs, count = 2 * heads_j, groups // 2, sum(PARTS)
    matrix = np.zeros((count * heads_j * groups, pairs * LANES), np.float32)
    for part in range(count):
        for j in range(heads_j):
            for g in range(groups):
                matrix[part * heads_j * groups + j * groups + g, (g // 2) * LANES + part * heads + 2 * j + g % 2] = 1.0
    return matrix


def spread_matrix(quantity, heads_j):
    heads = 2 * heads_j
    matrix = np.zeros((LANES, heads_j * LANES), np.float32)
    for part in range(PARTS[quantity]):
        for h in range(heads):
            matrix[part_lane(quantity, part, h, heads), h * HALF : (h + 1) * HALF] = 1.0
    return matrix


def head_matrix(heads_j):
    heads = 2 * heads_j
    matrix = np.zeros((LANES, heads * LANES), np.float32)
    for part in range(PARTS[0]):
        for h in range(heads):
            matrix[part_lane(0, part, h, heads), h * LANES : (h + 1) * LANES] = 1.0
    return matrix


def scales_kernel(dt_ref, log_ref, gather_ref, parts_ref, rows_ref):
    every, count = dt_ref.shape
    heads_j, groups = log_ref.shape
    logs = log_ref[...]
    own = lax.broadcasted_iota(jnp.int32, (groups, groups), 0) == lax.broadcasted_iota(jnp.int32, (groups, groups), 1)
    logs = [jnp.sum(jnp.where(own, logs[j : j + 1], 0.0), axis=1, keepdims=True) for j in range(heads_j)]
    rates = -LOG2E * jnp.exp(jnp.concatenate(logs, axis=0))
    upper = (
        lax.broadcasted_iota(jnp.int32, (SPAN, SPAN), 0) <= lax.broadcasted_iota(jnp.int32, (SPAN, SPAN), 1)
    ).astype(BF16)
    for at in range(0, count, SPAN):
        dt = dt_ref[:, at : at + SPAN]
        summed = dot(jnp.concatenate(split_parts(dt * rates, 3), axis=0), upper)
        cumul = summed[:every] + summed[every : 2 * every] + summed[2 * every :]
        tail = jnp.exp2(cumul[:, SPAN - 1 : SPAN] - cumul)
        parts = []
        for value, number in zip((cumul, dt, jnp.exp2(cumul), dt * tail), PARTS, strict=True):
            parts += split_parts(value, number)
        placed = dot(jnp.concatenate(parts, axis=0), gather_ref[...], TN).astype(BF16)
        for p in range(parts_ref.shape[0]):
            parts_ref[p, at : at + SPAN, :] = placed[:, p * LANES : (p + 1) * LANES]
        rows_ref[at // SPAN] = cumul


def states_kernel(
    x_ref, halo_ref, w_ref, b_ref, partf_ref, y_ref, c_ref, partr_ref, lead_ref, tail_ref,
    u_ref, slope_ref, s_ref, r_ref, from_ref, to_ref, total_ref, x_buf, s_acc, r_acc, f_acc, t_acc,
):
    step = pl.program_id(0)
    rows, heads_j, _ = x_ref.shape
    low = low_half(SPAN)

    @pl.when(step == 0)
    def _():
        s_acc[...] = jnp.zeros_like(s_acc)
        r_acc[...] = jnp.zeros_like(r_acc)
        f_acc[...] = jnp.ones_like(f_acc)
        t_acc[...] = jnp.ones_like(t_acc)
        halo = halo_ref[...].astype(F32)
        for j in range(heads_j):
            for row in range(3):
                x_buf[j, EDGE - 3 + row : EDGE - 2 + row, :] = halo[row, j : j + 1, :]

    @pl.when(step > 0)
    def _():
        x_buf[:, 0:EDGE, :] = x_buf[:, rows : rows + EDGE, :]

    x_buf[:, EDGE : EDGE + rows, :] = jnp.swapaxes(x_ref[...], 0, 1).astype(F32)
    weights = w_ref[...]
    number = rows // SPAN
    def one(k):
        m = number - 1 - k
        start = k * SPAN
        here = pl.ds(start, SPAN)
        there = pl.ds(m * SPAN, SPAN)
        grads_all = jnp.swapaxes(y_ref[there], 0, 1)
        partf = partf_ref[0, here, :]
        tails = dot(partf, tail_ref[...])
        leads = dot(jnp.concatenate([partr_ref[0, there, :], partf[SPAN - EDGE :]], axis=0), lead_ref[...])
        s_ref[k] = s_acc[...].astype(BF16)
        r_ref[m] = r_acc[...].astype(BF16)
        from_ref[k] = f_acc[...]
        to_ref[m] = t_acc[...]
        wrote, read = [], []
        for j in range(heads_j):
            lanes = slice(j * LANES, (j + 1) * LANES)
            at = start + EDGE - 3
            v = 0.5 * weights[0, j : j + 1, :] * x_buf[j, at : at + SPAN, :]
            for tap in range(1, 4):
                v = v + 0.5 * weights[tap, j : j + 1, :] * x_buf[j, at + tap : at + tap + SPAN, :]
            gate = 1.0 + jnp.tanh(v)
            u = v * gate
            u_ref[j, k] = u.astype(BF16)
            slope_ref[j, k] = (gate + u * (2.0 - gate)).astype(BF16)
            wrote.append((u * tails[:, lanes]).astype(BF16))
            read.append((grads_all[j].astype(F32) * leads[:SPAN, lanes]).astype(BF16))
        own_s = dot(b_ref[here, :], jnp.concatenate(wrote, axis=1), TN)
        own_r = dot(c_ref[there, :], jnp.concatenate(read, axis=1), TN)
        for j in range(heads_j):
            lanes = slice(j * LANES, (j + 1) * LANES)
            keep = leads[SPAN + EDGE - 1 : SPAN + EDGE, lanes]
            s_acc[j] = keep * s_acc[j] + jnp.where(low, own_s[:LANES, lanes], own_s[LANES:, lanes])
            f_acc[j] = f_acc[j] * keep
            keep = leads[SPAN - 1 : SPAN, lanes]
            r_acc[j] = keep * r_acc[j] + jnp.where(low, own_r[:LANES, lanes], own_r[LANES:, lanes])
            t_acc[j] = t_acc[j] * keep

    for turn in range(number):
        one(turn)

    @pl.when(step == pl.num_programs(0) - 1)
    def _():
        total_ref[0, :, :LANES, :] = s_acc[...].astype(BF16)
        total_ref[1, :, :LANES, :] = r_acc[...].astype(BF16)
        for j in range(heads_j):
            decay = f_acc[j][0:1]
            high = decay.astype(BF16).astype(F32)
            pair = jnp.concatenate([high, decay - high, jnp.zeros((6, LANES), F32)], axis=0)
            total_ref[0, j, LANES:, :] = pair.astype(BF16)
            total_ref[1, j, LANES:, :] = pair.astype(BF16)


def fold(value):
    return jnp.sum(value.reshape(value.shape[0] // 8, 8, value.shape[1]), axis=0)


def main_kernel(
    head0, core_ref, x_ref, u_ref, slope_ref, y_ref, b_ref, c_ref, part_ref, row_ref, s_ref, r_ref,
    enter_ref, leave_ref, from_ref, to_ref, w_ref, skip_ref, heads_ref, a_ref, dt_ref, *rest,
):
    mixed_ref, dx_ref, keep_ref, send_ref, sums_ref, edge_ref, dv_buf, acc = rest[-8:]
    step = pl.program_id(0)
    size, heads_j, _ = x_ref.shape
    span = SPAN
    number = size // span
    groups = row_ref.shape[1] // heads_j
    low = low_half(span)
    causal = lax.broadcasted_iota(jnp.int32, (span, span), 0) >= lax.broadcasted_iota(
        jnp.int32, (span, span), 1
    )

    @pl.when(step == 0)
    def _():
        acc[...] = jnp.zeros_like(acc)
        dv_buf[:, 0:EDGE, :] = jnp.zeros((heads_j, EDGE, LANES), F32)

    def one(turn, nothing):
        k = number - 1 - turn
        base = pl.multiple_of(k * span, span)
        dv_buf[:, span : span + EDGE, :] = dv_buf[:, 0:EDGE, :]
        here = pl.ds(base, span)
        xs = jnp.swapaxes(x_ref[here], 0, 1)
        grads = jnp.swapaxes(y_ref[here], 0, 1)
        b_all = b_ref[here, :]
        c_all = c_ref[here, :]
        weights = w_ref[...]
        skips = skip_ref[...]
        part = part_ref[0, here, :]
        zero = jnp.zeros((span, LANES), BF16)
        def diagonal(array):
            return jnp.concatenate(
                [jnp.concatenate([array[:, :LANES], zero], axis=1), jnp.concatenate([zero, array[:, LANES:]], axis=1)],
                axis=0,
            )

        b_diag = diagonal(b_all)
        scores16 = dot(c_all, b_diag, NT).astype(BF16)
        a_all = dot(part, a_ref[...])
        dt_all = dot(part, dt_ref[...])
        score_grads = [None, None]
        logs = row_ref[k]
        states, rstates, state_cat, rstate_cat = [], [], [], []
        for j in range(heads_j):
            state = s_ref[k, j].astype(F32) + from_ref[k, j][0:1] * enter_ref[j]
            rstate = r_ref[k, j].astype(F32) + to_ref[k, j][0:1] * leave_ref[j]
            states.append(fold(state * rstate))
            state = state.astype(BF16)
            rstate = rstate.astype(BF16)
            state_cat.append(jnp.concatenate([jnp.where(low, state, zero), jnp.where(low, zero, state)], axis=0))
            rstate_cat.append(jnp.concatenate([jnp.where(low, rstate, zero), jnp.where(low, zero, rstate)], axis=0))
        state_cat = jnp.concatenate(state_cat, axis=1)
        rstate_cat = jnp.concatenate(rstate_cat, axis=1)
        out_rows, leads, tails = [], [], []
        for j in range(heads_j):
            lanes = slice(j * LANES, (j + 1) * LANES)
            a_b = a_all[:, lanes]
            dt_b = dt_all[:, lanes]
            a_last = a_b[span - 1 : span]
            e_b = jnp.exp2(a_b)
            f_b = jnp.exp2(a_last - a_b)
            e_last = e_b[span - 1 : span]
            heads_b = dot(part, heads_ref[:, 2 * j * LANES : 2 * (j + 1) * LANES])
            u = u_ref[j, k].astype(F32)
            dy = grads[j].astype(F32)
            dy16 = dy.astype(BF16)
            val16 = (u * dt_b).astype(BF16)
            val = val16.astype(F32)
            tails.append((val * f_b).astype(BF16))
            leads.append((dy * e_b).astype(BF16))
            dy_two = jnp.concatenate([jnp.where(low, dy16, zero), jnp.where(low, zero, dy16)], axis=0)
            val_two = jnp.concatenate([jnp.where(low, val16, zero), jnp.where(low, zero, val16)], axis=0)
            products = dot(dy16, val_two, NT)
            mixes = []
            for g in range(2):
                at = j * groups + head0 + g
                inside = slice(g * LANES, (g + 1) * LANES)
                spread = heads_b[:, inside] - logs[at : at + 1]
                decay = jnp.exp2(jnp.where(causal, spread, -jnp.inf))
                mixes.append(scores16[:, inside] * decay.astype(BF16))
                weighted = decay * products[:, inside]
                score_grads[g] = weighted if score_grads[g] is None else score_grads[g] + weighted
            inner = dot(jnp.concatenate(mixes, axis=1), val_two)
            dval = dot(jnp.concatenate(mixes, axis=0), dy_two, TN)
            carried = dot(c_all, state_cat[:, lanes]) * e_b
            back = dot(b_all, rstate_cat[:, lanes]) * f_b
            out = inner + carried
            dval_full = dval + back
            log_part = a_b * (dy * out - val * dval_full)
            acc[4, j] = acc[4, j] + fold(log_part) + fold(val * back) * a_last + states[j] * (a_last * e_last)
            skip = skips[j : j + 1, :]
            out_rows.append((out + skip * u).astype(BF16))
            dv_buf[j, 0:span, :] = (dt_b * dval_full + skip * dy) * (0.5 * slope_ref[j, k].astype(F32))
        mixed_ref[here] = jnp.swapaxes(jnp.stack(out_rows, axis=0), 0, 1)
        dc_inter = dot(jnp.concatenate(leads, axis=1), state_cat, NT)
        db_inter = dot(jnp.concatenate(tails, axis=1), rstate_cat, NT)
        dx_rows = []
        for j in range(heads_j):
            x = xs[j].astype(F32)
            total = None
            for tap in range(4):
                shifted = dv_buf[j, 3 - tap : 3 - tap + span, :]
                piece = weights[tap, j : j + 1, :] * shifted
                total = piece if total is None else total + piece
                acc[tap, j] = acc[tap, j] + fold(shifted * x)
            dx_rows.append(total.astype(BF16))
        dx_ref[here] = jnp.swapaxes(jnp.stack(dx_rows, axis=0), 0, 1)
        flows = [flow.astype(BF16) for flow in score_grads]
        dc = (dot(jnp.concatenate(flows, axis=1), b_diag) + dc_inter).astype(BF16)
        db = (dot(jnp.concatenate(flows, axis=0), diagonal(c_all), TN) + db_inter).astype(BF16)

        @pl.when(core_ref[0] == 0)
        def _():
            keep_ref[here, :] = db
            send_ref[here, :] = dc

        @pl.when(core_ref[0] != 0)
        def _():
            keep_ref[here, :] = dc
            send_ref[here, :] = db

        return nothing

    lax.fori_loop(0, number, one, 0)

    @pl.when(step == pl.num_programs(0) - 1)
    def _():
        edge_ref[...] = dv_buf[:, 0:EDGE, :]
        for tap in range(5):
            for j in range(heads_j):
                sums_ref[tap, j : j + 1, :] = jnp.sum(acc[tap, j], axis=0, keepdims=True)


def place_kernel(number, core_ref, *refs):
    mine, got = refs[:number], refs[number : 2 * number]
    write_ref, read_ref, token_ref = refs[-3:]
    token_ref[...] = jnp.zeros_like(token_ref)

    @pl.when(core_ref[0] == 0)
    def _():
        for n in range(number):
            lanes = slice(2 * n * LANES, 2 * (n + 1) * LANES)
            write_ref[:, lanes] = mine[n][...]
            read_ref[:, lanes] = got[n][...]

    @pl.when(core_ref[0] != 0)
    def _():
        for n in range(number):
            lanes = slice(2 * n * LANES, 2 * (n + 1) * LANES)
            write_ref[:, lanes] = got[n][...]
            read_ref[:, lanes] = mine[n][...]


def place_call(core, mine, got, token, write_grad, read_grad, at, count, groups):
    number = len(mine)
    rows = at_most(4, count // SPAN) * SPAN
    anywhere = pl.BlockSpec(memory_space=pl.ANY)
    block = pl.BlockSpec((rows, 2 * LANES), lambda i: (i, 0))
    operands = [core, *mine, *got, token]
    in_specs = [pl.BlockSpec(memory_space=pltpu.SMEM)] + [block] * (2 * number) + [anywhere]
    aliases = {}
    if write_grad is not None:
        aliases = {len(operands): 0, len(operands) + 1: 1}
        operands += [write_grad, read_grad]
        in_specs += [anywhere] * 2
    return pl.pallas_call(
        functools.partial(place_kernel, number),
        grid=(count // rows,),
        in_specs=in_specs,
        out_specs=[pl.BlockSpec((rows, 2 * number * LANES), lambda i: (i, at))] * 2
        + [pl.BlockSpec((EDGE, LANES), lambda i: (0, 0))],
        out_shape=[jax.ShapeDtypeStruct((count, groups * LANES), BF16)] * 2 + [jax.ShapeDtypeStruct((EDGE, LANES), F32)],
        input_output_aliases=aliases,
        cost_estimate=cost(2 * number),
        name="place",
    )(*operands)


def edge_kernel(after_ref, w_ref, dx_ref, out_ref):
    rows = dx_ref.shape[0]
    weights = w_ref[...]
    after = after_ref[...]
    out_ref[: rows - 3] = dx_ref[: rows - 3]
    for row in range(3):
        fix = weights[0] * after[row]
        for tap in range(1, row + 1):
            fix = fix + weights[tap] * after[row - tap]
        at = rows - 3 + row
        out_ref[at] = (dx_ref[at].astype(F32) + fix).astype(BF16)


def halves_of(ref):
    decay = ref[0, :, LANES, :].astype(F32) + ref[0, :, LANES + 1, :].astype(F32)
    return ref[0, :, :LANES, :].astype(F32), ref[1, :, :LANES, :].astype(F32), decay


def combine_kernel(first, last, bits_ref, mine_ref, got_ref, *refs):
    if not first:
        enter_ref, leave_ref, reach_ref = refs[:3]
    send_ref, enter_out, leave_out, reach_out = refs[-4:]

    def write(forward, backward, decay):
        if last:

            @pl.when(bits_ref[1] == 1)
            def _():
                send_ref[...] = backward.astype(BF16)

            @pl.when(bits_ref[1] == 0)
            def _():
                send_ref[...] = forward.astype(BF16)
        else:
            high = decay.astype(BF16).astype(F32)
            send_ref[0, :, :LANES, :] = forward.astype(BF16)
            send_ref[1, :, :LANES, :] = backward.astype(BF16)
            zeros = jnp.zeros((6, LANES), F32)
            for j in range(decay.shape[0]):
                rows = jnp.concatenate([high[j : j + 1], decay[j : j + 1] - high[j : j + 1], zeros], axis=0)
                send_ref[0, j, LANES:, :] = rows.astype(BF16)
                send_ref[1, j, LANES:, :] = rows.astype(BF16)

    own_f, own_b, own_d = halves_of(mine_ref)
    got_f, got_b, got_d = halves_of(got_ref)
    wide, got_wide = own_d[:, None, :], got_d[:, None, :]

    @pl.when(bits_ref[0] == 1)
    def _():
        if first:
            enter_out[...] = got_f.astype(BF16)
            leave_out[...] = jnp.zeros_like(leave_out)
            reach_out[0] = got_d
            reach_out[1] = jnp.ones_like(got_d)
        else:
            enter_out[...] = (enter_ref[...].astype(F32) + reach_ref[0][:, None, :] * got_f).astype(BF16)
            leave_out[...] = leave_ref[...]
            reach_out[0] = reach_ref[0] * got_d
            reach_out[1] = reach_ref[1]
        write(own_f + wide * got_f, got_b + got_wide * own_b, own_d * got_d)

    @pl.when(bits_ref[0] == 0)
    def _():
        if first:
            enter_out[...] = jnp.zeros_like(enter_out)
            leave_out[...] = got_b.astype(BF16)
            reach_out[0] = jnp.ones_like(got_d)
            reach_out[1] = got_d
        else:
            enter_out[...] = enter_ref[...]
            leave_out[...] = (leave_ref[...].astype(F32) + reach_ref[1][:, None, :] * got_b).astype(BF16)
            reach_out[0] = reach_ref[0]
            reach_out[1] = reach_ref[1] * got_d
        write(got_f + got_wide * own_f, own_b + wide * got_b, own_d * got_d)


class Exchange:
    def __init__(self, total):
        self.count = lax.axis_size("seq")
        self.sent = total
        self.shape = (total.shape[1], LANES, LANES)
        self.distance = 1
        self.known = ()
        self.got = None

    def bit(self, distance):
        return (lax.axis_index("seq") // distance % 2).astype(jnp.int32)

    def swap(self):
        self.got = lax.ppermute(self.sent, "seq", [(i, i ^ self.distance) for i in range(self.count)])

    def finish(self, after):
        while not self.finished():
            combine([self], after)
            self.swap()
        near_in, near_out, after = lax.optimization_barrier((self.known[0], self.known[1], after))
        reach = self.known[2][:, :, None, :]
        upper = self.bit(self.distance) == 1
        far = self.got.astype(F32)
        enter = near_in.astype(F32) + jnp.where(upper, reach[0] * far, 0.0)
        leave = near_out.astype(F32) + jnp.where(upper, 0.0, reach[1] * far)
        return enter, leave, after

    def finished(self):
        return 2 * self.distance >= self.count

    def step(self):
        bits = jnp.stack([self.bit(self.distance), self.bit(2 * self.distance)])
        last = 4 * self.distance >= self.count
        shapes = [
            jax.ShapeDtypeStruct(self.shape if last else self.sent.shape, BF16),
            jax.ShapeDtypeStruct(self.shape, BF16),
            jax.ShapeDtypeStruct(self.shape, BF16),
            jax.ShapeDtypeStruct((2, self.shape[0], LANES), F32),
        ]
        return [bits, self.sent, self.got, *self.known], shapes, (not self.known, last)


def combine(exchanges, *after):
    steps = [e.step() for e in exchanges]
    operands = [value for step in steps for value in step[0]]
    shapes = [shape for step in steps for shape in step[1]]
    vmem, smem = pl.BlockSpec(memory_space=pltpu.VMEM), pl.BlockSpec(memory_space=pltpu.SMEM)

    def kernel(*refs):
        ins, outs = refs[: len(operands)], refs[len(operands) + len(after) :]
        for n, (values, _, form) in enumerate(steps):
            combine_kernel(*form, *ins[: len(values)], *outs[4 * n : 4 * n + 4])
            ins = ins[len(values) :]

    results = pl.pallas_call(
        kernel,
        in_specs=[spec for step in steps for spec in [smem] + [vmem] * (len(step[0]) - 1)]
        + [pl.BlockSpec(memory_space=pl.ANY)] * len(after),
        out_specs=[vmem] * len(shapes),
        out_shape=shapes,
        cost_estimate=cost(2),
        name="combine",
    )(*operands, *after)
    for n, e in enumerate(exchanges):
        e.sent, *e.known = results[4 * n : 4 * n + 4]
        e.distance *= 2


def passed_along(block, axis, distance):
    devices = range(lax.axis_size(axis))
    route = [(i - distance, i) for i in devices if i - distance in devices]
    return lax.ppermute(block, axis, route)


def swap_sum(value, axis, distance=1):
    count = lax.axis_size(axis)
    while distance < count:
        value = value + lax.ppermute(value, axis, [(i, i ^ distance) for i in range(count)])
        distance *= 2
    return value


SCALES_SPANS = 6
STATES_SPANS = 3
MAIN_SPANS = 1


def at_most(limit, spans):
    return max(n for n in range(1, limit + 1) if spans % n == 0)


def fixed(array):
    return pl.BlockSpec(array.shape, lambda i: (0,) * array.ndim)


def states_call(p, waits, x, halo, taps, write_in, parts, out_grad, read_in, e_m, df_m):
    count, heads_j, _ = x.shape
    spans = count // SPAN
    per = at_most(STATES_SPANS, spans)
    size = per * SPAN
    end = spans // per - 1
    def kernel(*refs):
        states_kernel(*refs[:10], *refs[10 + len(waits) :])

    return pl.pallas_call(
        kernel,
        grid=(spans // per,),
        in_specs=[
            pl.BlockSpec((size, heads_j, LANES), lambda i: (i, 0, p)),
            pl.BlockSpec((halo.shape[0], heads_j, LANES), lambda i: (0, 0, p)),
            pl.BlockSpec((4, heads_j, LANES), lambda i: (0, 0, p)),
            pl.BlockSpec((size, 2 * LANES), lambda i: (i, p)),
            pl.BlockSpec((1, size, LANES), lambda i: (p, i, 0)),
            pl.BlockSpec((size, heads_j, LANES), lambda i: (end - i, 0, p)),
            pl.BlockSpec((size, 2 * LANES), lambda i: (end - i, p)),
            pl.BlockSpec((1, size, LANES), lambda i: (p, end - i, 0)),
            fixed(e_m), fixed(df_m),
        ] + [pl.BlockSpec(memory_space=pl.ANY)] * len(waits),
        out_specs=[
            pl.BlockSpec((heads_j, per, SPAN, LANES), lambda i: (0, i, 0, 0)),
            pl.BlockSpec((heads_j, per, SPAN, LANES), lambda i: (0, i, 0, 0)),
            pl.BlockSpec((per, heads_j, LANES, LANES), lambda i: (i, 0, 0, 0)),
            pl.BlockSpec((per, heads_j, LANES, LANES), lambda i: (end - i, 0, 0, 0)),
            pl.BlockSpec((per, heads_j, EDGE, LANES), lambda i: (i, 0, 0, 0)),
            pl.BlockSpec((per, heads_j, EDGE, LANES), lambda i: (end - i, 0, 0, 0)),
            pl.BlockSpec((2, heads_j, LANES + EDGE, LANES), lambda i: (0, 0, 0, 0)),
        ],
        out_shape=[
            jax.ShapeDtypeStruct((heads_j, spans, SPAN, LANES), BF16),
            jax.ShapeDtypeStruct((heads_j, spans, SPAN, LANES), BF16),
            jax.ShapeDtypeStruct((spans, heads_j, LANES, LANES), BF16),
            jax.ShapeDtypeStruct((spans, heads_j, LANES, LANES), BF16),
            jax.ShapeDtypeStruct((spans, heads_j, EDGE, LANES), F32),
            jax.ShapeDtypeStruct((spans, heads_j, EDGE, LANES), F32),
            jax.ShapeDtypeStruct((2, heads_j, LANES + EDGE, LANES), BF16),
        ],
        scratch_shapes=[
            pltpu.VMEM((heads_j, size + EDGE, LANES), F32),
            pltpu.VMEM((heads_j, LANES, LANES), F32),
            pltpu.VMEM((heads_j, LANES, LANES), F32),
            pltpu.VMEM((heads_j, EDGE, LANES), F32),
            pltpu.VMEM((heads_j, EDGE, LANES), F32),
        ],
        cost_estimate=cost(9),
        name=f"states{p}",
    )(x, halo, taps, write_in, parts, out_grad, read_in, parts, e_m, df_m, *waits)


def main_call(
    p, waits, core, x, value, slope, out_grad, write_in, read_in, parts, rows, s_loc, r_loc, enter,
    leave, from_start, to_end, taps, skips, heads_m, a_m, dt_m, mixed, dx,
):
    count, heads_j, _ = x.shape
    spans = count // SPAN
    per = at_most(MAIN_SPANS, spans)
    size = per * SPAN
    last = spans // per - 1
    operands = [core, x, value, slope, out_grad, write_in, read_in, parts, rows, s_loc, r_loc,
                enter, leave, from_start, to_end, taps, skips, heads_m, a_m, dt_m, *waits]
    time3 = pl.BlockSpec((size, heads_j, LANES), lambda i: (last - i, 0, p))
    time2 = pl.BlockSpec((size, 2 * LANES), lambda i: (last - i, p))
    own3 = pl.BlockSpec((heads_j, per, SPAN, LANES), lambda i: (0, last - i, 0, 0))
    own2 = pl.BlockSpec((size, 2 * LANES), lambda i: (last - i, 0))
    state = pl.BlockSpec((per, heads_j, LANES, LANES), lambda i: (last - i, 0, 0, 0))
    lane_row = pl.BlockSpec((per, heads_j, EDGE, LANES), lambda i: (last - i, 0, 0, 0))
    in_specs = [
        pl.BlockSpec(memory_space=pltpu.SMEM), time3, own3, own3, time3, time2, time2,
        pl.BlockSpec((1, size, LANES), lambda i: (p, last - i, 0)),
        pl.BlockSpec((per, rows.shape[1], SPAN), lambda i: (last - i, 0, 0)),
        state, state, fixed(enter), fixed(leave), lane_row, lane_row,
        pl.BlockSpec((4, heads_j, LANES), lambda i: (0, 0, p)),
        pl.BlockSpec((heads_j, LANES), lambda i: (0, p)),
        fixed(heads_m), fixed(a_m), fixed(dt_m),
    ] + [pl.BlockSpec(memory_space=pl.ANY)] * len(waits)
    aliases = {}
    if mixed is not None:
        aliases = {len(operands): 0, len(operands) + 1: 1}
        operands += [mixed, dx]
        in_specs += [pl.BlockSpec(memory_space=pl.ANY)] * 2
    return pl.pallas_call(
        functools.partial(main_kernel, 2 * p),
        grid=(spans // per,),
        in_specs=in_specs,
        out_specs=[
            time3, time3, own2, own2,
            pl.BlockSpec((5, heads_j, LANES), lambda i: (0, 0, 0)),
            pl.BlockSpec((heads_j, EDGE, LANES), lambda i: (0, 0, 0)),
        ],
        out_shape=[
            jax.ShapeDtypeStruct(x.shape, BF16),
            jax.ShapeDtypeStruct(x.shape, BF16),
            jax.ShapeDtypeStruct((count, 2 * LANES), BF16),
            jax.ShapeDtypeStruct((count, 2 * LANES), BF16),
            jax.ShapeDtypeStruct((5, heads_j, LANES), F32),
            jax.ShapeDtypeStruct((heads_j, EDGE, LANES), F32),
        ],
        scratch_shapes=[
            pltpu.VMEM((heads_j, SPAN + EDGE, LANES), F32),
            pltpu.VMEM((5, heads_j, EDGE, LANES), F32),
        ],
        input_output_aliases=aliases,
        cost_estimate=cost(20),
        name=f"main{p}",
    )(*operands)


def on_device(x, taps, step_size, decay_log, write_in, read_in, skip_gain, out_grad):
    count, heads_j, width = x.shape
    groups = decay_log.shape[1]
    pairs = groups // 2
    spans = count // SPAN
    heads = 2 * heads_j
    rim = taps.shape[0] - 1
    n_head = lax.axis_size("head")
    core = (lax.axis_index("head") % 2).astype(jnp.int32).reshape(1)
    per = at_most(SCALES_SPANS, spans)
    gather = jnp.asarray(gather_matrix(heads_j, groups), BF16)
    parts, rows = pl.pallas_call(
        scales_kernel,
        grid=(spans // per,),
        in_specs=[
            pl.BlockSpec((heads_j * groups, per * SPAN), lambda i: (0, i)),
            pl.BlockSpec((heads_j, groups), lambda i: (0, 0)),
            pl.BlockSpec(gather.shape, lambda i: (0, 0)),
        ],
        out_specs=[
            pl.BlockSpec((pairs, per * SPAN, LANES), lambda i: (0, i, 0)),
            pl.BlockSpec((per, heads_j * groups, SPAN), lambda i: (i, 0, 0)),
        ],
        out_shape=[
            jax.ShapeDtypeStruct((pairs, count, LANES), BF16),
            jax.ShapeDtypeStruct((spans, heads_j * groups, SPAN), F32),
        ],
        cost_estimate=cost(4),
        name="scales",
    )(
        jnp.transpose(step_size, (1, 2, 0)).reshape(heads_j * groups, count),
        decay_log,
        gather,
    )
    rim_in, parts = lax.optimization_barrier((x[count - rim :], parts))
    halo = passed_along(rim_in, "seq", 1)
    skips = jnp.broadcast_to(skip_gain[:, :, None], (heads_j, groups, HALF)).reshape(heads_j, width)
    a_m, dt_m, e_m, df_m = (jnp.asarray(spread_matrix(q, heads_j), BF16) for q in range(4))
    heads_m = jnp.asarray(head_matrix(heads_j), BF16)

    values, slopes, s_all, r_all, froms, tos = [], [], [], [], [], []
    exchanges = []

    def boundary(token, *others):
        moved = [e for e in exchanges if not e.finished()]
        if moved:
            combine(moved, token)
        tied = lax.optimization_barrier((token, *[e.sent for e in moved], *others))
        for e, value in zip(moved, tied[1:]):
            e.sent = value
            e.swap()
        return [tied[0], *[e.sent for e in moved]], tied[len(tied) - len(others) :]

    waits = []
    for p in range(pairs):
        u, slope, s_loc, r_loc, from_start, to_end, total = states_call(
            p, waits, x, halo, taps, write_in, parts, out_grad, read_in, e_m, df_m
        )
        ready = exchanges[0].finish(from_start) if p == pairs - 1 else ()
        waits, (total, *ready) = boundary(from_start, total, *ready)
        exchanges.append(Exchange(total))
        exchanges[-1].swap()
        values.append(u)
        slopes.append(slope)
        s_all.append(s_loc)
        r_all.append(r_loc)
        froms.append(from_start)
        tos.append(to_end)

    mixed = dx = None
    cores = [(i, i ^ 1) for i in range(n_head)]
    sums, edges, arrived, summed = [], [], [], []
    for p in range(pairs):
        enter, leave, token = ready
        mixed, dx, keep, send, total, edge = main_call(
            p, [*waits, token], core, x, values[p], slopes[p], out_grad, write_in, read_in, parts, rows, s_all[p], r_all[p], enter,
            leave, froms[p], tos[p], taps, skips, heads_m, a_m, dt_m, mixed, dx,
        )
        sums.append(total)
        edges.append(edge)
        ready = exchanges[p + 1].finish(edge) if p < pairs - 1 else ()
        waits, (send, *tied) = boundary(edge, send, *ready, *arrived)
        ready = tied[: len(ready)]
        if summed:
            summed[-1] = tied[-1]
        mine = keep + lax.ppermute(send, "head", cores)
        waits.append(mine)
        arrived = []
        distance = 2
        while distance < n_head:
            got = lax.ppermute(mine, "head", [(i, i ^ distance) for i in range(n_head)])
            if p == pairs - 1 and 2 * distance >= n_head:
                break
            mine = mine + got
            distance *= 2
        arrived.append(mine)
        if p < pairs - 1:
            summed.append(mine)

    edge = jnp.transpose(jnp.concatenate(edges, axis=-1)[:, :rim, :], (1, 0, 2))
    after = passed_along(edge, "seq", -1)
    before = halo.astype(F32)
    sums = jnp.concatenate(sums, axis=-1)
    extra = []
    for tap in range(5):
        piece = jnp.zeros_like(sums[0])
        for row in range(rim - tap):
            piece = piece + edge[row] * before[row + tap]
        extra.append(piece)
    sums = sums + jnp.stack(extra)
    n_seq = lax.axis_size("seq")
    if n_seq > 1:
        sums = sums + lax.ppermute(sums, "seq", [(i, i ^ 1) for i in range(n_seq)])
    others = [lax.ppermute(value, "head", cores) for value in summed]
    write_grad, read_grad, token = place_call(core, summed, others, edges[-1], None, None, 0, count, groups)
    sums, token = lax.optimization_barrier((sums, token))
    sums = swap_sum(sums, "seq", 2)
    got, token, sums, after = lax.optimization_barrier((got, token, sums, after))
    mine = mine + got
    other = lax.ppermute(mine, "head", cores)
    write_grad, read_grad, _ = place_call(core, [mine], [other], token, write_grad, read_grad, pairs - 1, count, groups)
    tail_spec = pl.BlockSpec((EDGE, heads_j, width), lambda i: (count // EDGE - 1, 0, 0))
    dx = pl.pallas_call(
        edge_kernel,
        grid=(1,),
        in_specs=[fixed(after), fixed(taps), tail_spec],
        out_specs=tail_spec,
        out_shape=jax.ShapeDtypeStruct(x.shape, BF16),
        input_output_aliases={2: 0},
        cost_estimate=cost(1),
        name="edge",
    )(after, taps, dx)
    conv_grad = sums[:4]
    decay_grad = LN2 * sums[4].reshape(heads_j, groups, HALF).sum(-1)
    return (mixed, dx, conv_grad, decay_grad, write_grad, read_grad)


def solution(mesh):
    return jax.shard_map(
        on_device,
        mesh=mesh,
        in_specs=(
            P("seq", "head", None),
            P(None, "head", None),
            P("seq", "head", None),
            P("head", None),
            P("seq", None),
            P("seq", None),
            P("head", None),
            P("seq", "head", None),
        ),
        out_specs=(
            P("seq", "head", None),
            P("seq", "head", None),
            P(None, "head", None),
            P("head", None),
            P("seq", None),
            P("seq", None),
        ),
        check_vma=False,
    )
```
